32 devices in a mesh: fsdp: 8 (over y, x, core), dp: 4 (over z).
Axes of the slice: x: 2, y: 2, z: 4, core: 2. Of those that a mesh axis runs over, the one named last changes fastest.
Arguments:
- tokens: bfloat16 [32768, 768], P(('fsdp', 'dp')), may hold values from -6 to 6
- crop_ids: int32 [32768], P(('fsdp', 'dp')), may hold values from 0 to 23, as said below
- gain_first: bfloat16 [768], P('fsdp'), may hold values from 0.25 to 1.75
- shift_first: bfloat16 [768], P('fsdp'), may hold values from -1 to 1
- joint_weight: bfloat16 [768, 2304], P('fsdp'), may hold values from -0.3125 to 0.3125
- joint_bias: bfloat16 [2, 768], P(None, 'fsdp'), may hold values from -1 to 1
- output_weight: bfloat16 [768, 768], P('fsdp'), may hold values from -0.4375 to 0.4375
- output_bias: bfloat16 [768], P('fsdp'), may hold values from -1 to 1
- gain_second: bfloat16 [768], P('fsdp'), may hold values from 0.25 to 1.75
- shift_second: bfloat16 [768], P('fsdp'), may hold values from -1 to 1
- up_weight: bfloat16 [768, 3072], P('fsdp'), may hold values from -0.21875 to 0.21875
- up_bias: bfloat16 [3072], P('fsdp'), may hold values from -1 to 1
- down_weight: bfloat16 [3072, 768], P('fsdp'), may hold values from -0.15625 to 0.15625
- down_bias: bfloat16 [768], P('fsdp'), may hold values from -1 to 1
- cotangent: bfloat16 [32768, 768], P(('fsdp', 'dp')), may hold values from -6 to 6
Outputs:
- activations: float32 [32768, 768], P(('fsdp', 'dp'))
- input_grad: float32 [32768, 768], P(('fsdp', 'dp'))
- grad_gain_first: float32 [768], P('fsdp')
- grad_shift_first: float32 [768], P('fsdp')
- grad_joint_weight: float32 [768, 2304], P('fsdp')
- grad_joint_bias: float32 [2, 768], P(None, 'fsdp')
- grad_output_weight: float32 [768, 768], P('fsdp')
- grad_output_bias: float32 [768], P('fsdp')
- grad_gain_second: float32 [768], P('fsdp')
- grad_shift_second: float32 [768], P('fsdp')
- grad_up_weight: float32 [768, 3072], P('fsdp')
- grad_up_bias: float32 [3072], P('fsdp')
- grad_down_weight: float32 [3072, 768], P('fsdp')
- grad_down_bias: float32 [768], P('fsdp')
The draws below stay inside these ranges and needn't reach their ends.
Inputs may be any that keep to these rules, and one draw needn't show every extreme that they name: `crop_ids`: each device's 1024 tokens hold whole crops in random order: at least one global crop of 197 tokens, local crops of 37 tokens, and at most one shorter remainder crop; the first device's block holds exactly one global crop. Ids number the crops of a block from 0 in order of position; a crop has at most 197 tokens and every block has a crop of exactly 197.
All inputs are finite; a program needn't handle non-finite values.
Results may differ from the reference program's by a relative error of at most 0.015.
Values may be sent and summed in bfloat16 or wider, within the bound.
No kernel may reach another device: no remote copies, remote signals or barrier semaphores. Data moves between devices by JAX's collectives and lax.ppermute only.
A program may use at most 256 MiB of HBM per device.

```python
import jax
import jax.numpy as jnp
from jax import lax

D = 768
HEADS = 12
HD = 64
FF = 3072
GLOBAL = 197
LOCAL = 37
TOK_DEV = 1024
TOKENS = 32768


def draw_crop_ids(key, part):
    block_count = TOKENS // TOK_DEV
    most_global = 2 * (TOK_DEV // (2 * GLOBAL))
    slot_count = most_global + TOK_DEV // LOCAL + 1

    def one_block(block_key, block_index):
        count_key, order_key = jax.random.split(block_key)
        drawn_count = jax.random.randint(count_key, (), 1, most_global + 1)
        global_count = jnp.where(block_index == 0, 1, drawn_count).astype(jnp.int32)
        slot_index = jnp.arange(slot_count, dtype=jnp.int32)
        local_count = (TOK_DEV - GLOBAL * global_count) // LOCAL
        remainder = TOK_DEV - GLOBAL * global_count - LOCAL * local_count
        lengths = jnp.where(slot_index < global_count, GLOBAL, jnp.where(slot_index < global_count + local_count, LOCAL, jnp.where(slot_index == global_count + local_count, remainder, 0)))
        ranking = jax.random.randint(order_key, (slot_count,), 0, 4096) * slot_count + slot_index
        ranking = jnp.where(lengths > 0, ranking, 8192 * slot_count + slot_index)
        arrangement = jnp.argsort(ranking)
        lengths = lengths[arrangement]
        boundary = jnp.cumsum(lengths)
        position = jnp.arange(TOK_DEV, dtype=jnp.int32)
        return jnp.sum((boundary[None, :] <= position[:, None]).astype(jnp.int32), axis=1).astype(jnp.int32)
    block_keys = jax.random.split(key, block_count)
    block_indices = jnp.arange(block_count, dtype=jnp.int32)
    return jax.vmap(one_block)(block_keys, block_indices).reshape(TOKENS).astype(jnp.int32)


def strengthened(array, rng, source, target, blocks, factor):
    def block_of(axis_at):
        return (jnp.arange(array.shape[axis_at]) // (array.shape[axis_at] // blocks)).reshape((-1,) + (1,) * (array.ndim - 1 - axis_at))

    one_side = jax.random.permutation(rng, blocks)[block_of(target)]
    second = (block_of(target) + blocks // 2) % blocks
    return jnp.where((block_of(source) == one_side) | (block_of(source) == second), factor * array, array)


def level_of(rng, dims, shards, low, high):
    def one(dim, blocks):
        heights = jax.random.uniform(jax.random.fold_in(jax.random.fold_in(rng, 6), dim), (blocks,), jnp.float32, low / len(shards), high / len(shards))
        return jnp.repeat(jnp.exp(heights), dims[dim] // blocks).reshape((-1,) + (1,) * (len(dims) - dim - 1))

    loudness = one(*shards[0])
    for cut in shards[1:]:
        loudness = loudness * one(*cut)
    return loudness


def bell_draw(stream_key, shape, scale, most, cuts=(), held_as=jnp.bfloat16):
    level = level_of(stream_key, shape, cuts, -0.22, 0.18) if cuts else 1.0
    drawn = jax.random.normal(stream_key, shape, jnp.float32) * scale * level
    return jnp.minimum(jnp.maximum(drawn, -most), most).astype(held_as)


def heavy_noise(own_key, extent, deviation, bound, cuts, heavy, kind=jnp.bfloat16):
    values = deviation * jax.random.normal(own_key, extent, jnp.float32)
    if cuts:
        values = values * level_of(own_key, extent, cuts, -0.22, 0.18)
    return jnp.clip(strengthened(values, jax.random.fold_in(own_key, 3), *heavy), -bound, bound).astype(kind)


def setup_inputs(seed: int = 0) -> dict:
    splits = jax.random.split(jax.random.key(seed), 16)
    tokens = bell_draw(splits[0], (TOKENS, D), 1.0, 6.0, ((0, 32),))
    crop_ids = draw_crop_ids(jax.random.fold_in(splits[15], 71), 0)
    gain_first = jnp.clip(1.0 + 0.15 * jax.random.normal(splits[2], (D,), jnp.float32), 0.25, 1.75).astype(jnp.bfloat16)
    shift_first = bell_draw(splits[3], (D,), 0.2, 1.0, ((0, 8),))
    joint_weight = bell_draw(splits[4], (D, 3 * D), (D // 2) ** -0.5, 0.3125, ((0, 8),))
    joint_bias = bell_draw(splits[5], (2, D), 0.2, 1.0, ((1, 8),))
    output_weight = bell_draw(splits[6], (D, D), (D // 4) ** -0.5, 0.4375, ((0, 8),))
    output_bias = bell_draw(splits[7], (D,), 0.2, 1.0, ((0, 8),))
    gain_second = jnp.clip(1.0 + 0.15 * jax.random.normal(splits[8], (D,), jnp.float32), 0.25, 1.75).astype(jnp.bfloat16)
    shift_second = bell_draw(splits[9], (D,), 0.2, 1.0, ((0, 8),))
    up_weight = bell_draw(splits[10], (D, FF), D ** -0.5, 0.21875, ((0, 8),))
    up_bias = bell_draw(splits[11], (FF,), 0.2, 1.0, ((0, 8),))
    down_weight = bell_draw(splits[12], (FF, D), (FF // 2) ** -0.5, 0.15625, ((0, 8),))
    down_bias = bell_draw(splits[13], (D,), 0.2, 1.0, ((0, 8),))
    cotangent = heavy_noise(splits[14], (TOKENS, D), 1.0, 6.0, ((0, 32),), (0, 1, 32, 2.75))
    return dict(tokens=tokens, crop_ids=crop_ids, gain_first=gain_first, shift_first=shift_first, joint_weight=joint_weight, joint_bias=joint_bias, output_weight=output_weight, output_bias=output_bias, gain_second=gain_second, shift_second=shift_second, up_weight=up_weight, up_bias=up_bias, down_weight=down_weight, down_bias=down_bias, cotangent=cotangent)


@jax.custom_vjp
def low(v):
    return lax.optimization_barrier(v.astype(jnp.bfloat16)).astype(jnp.float32)

@jax.custom_vjp
def low_back(v):
    return v

def low_keep(v):
    return (low(v), None)

def low_pass(kept, grad):
    return (grad,)

def back_keep(v):
    return (v, None)

def back_low(kept, grad):
    return (low(grad),)
low.defvjp(low_keep, low_pass)
low_back.defvjp(back_keep, back_low)
HIGHEST = lax.Precision.HIGHEST

def layer_norm(values, gain, shift):
    center = values - lax.optimization_barrier(jnp.mean(values, axis=-1, keepdims=True))
    spread = lax.optimization_barrier(jnp.mean(center * center, axis=-1, keepdims=True))
    return center * lax.rsqrt(spread + 1e-06) * gain + shift

def matmul(left, right):
    return jnp.dot(left, right, precision=HIGHEST, preferred_element_type=jnp.float32)

def forward(inputs, crop_block, params):
    gain_first, shift_first, joint_weight, joint_bias, output_weight, output_bias, gain_second, shift_second, up_weight, up_bias, down_weight, down_bias = params
    row_count = inputs.shape[0]
    hidden_first = low(layer_norm(inputs, gain_first, shift_first))
    bias_full = jnp.concatenate([joint_bias[0], jnp.zeros((D,), jnp.float32), joint_bias[1]])
    joint_proj = low(low_back(matmul(hidden_first, joint_weight) + bias_full))
    queries = joint_proj[:, :D].reshape(row_count, HEADS, HD)
    key_rows = joint_proj[:, D:2 * D].reshape(row_count, HEADS, HD)
    value_rows = joint_proj[:, 2 * D:].reshape(row_count, HEADS, HD)
    scores = jnp.einsum('qhd,khd->hqk', queries, key_rows, precision=HIGHEST) * HD ** (-0.5)
    same_crop = crop_block[:, None] == crop_block[None, :]
    scores = low_back(jnp.where(same_crop[None], scores, -1e+30))
    weights = jax.nn.softmax(scores, axis=-1)
    mixed_heads = jnp.einsum('hqk,khd->qhd', low(weights), value_rows, precision=HIGHEST)
    mixed_heads = low(low_back(mixed_heads.reshape(row_count, D)))
    branch_first = low_back(matmul(mixed_heads, output_weight) + output_bias)
    middle = inputs + branch_first
    hidden_second = low(layer_norm(middle, gain_second, shift_second))
    up_value = low_back(matmul(hidden_second, up_weight) + up_bias)
    active = low(jax.nn.gelu(up_value, approximate=False))
    branch_second = low_back(matmul(active, down_weight) + down_bias)
    return middle + branch_second

def reference(tokens, crop_ids, gain_first, shift_first, joint_weight, joint_bias, output_weight, output_bias, gain_second, shift_second, up_weight, up_bias, down_weight, down_bias, cotangent):
    params = (gain_first, shift_first, joint_weight, joint_bias, output_weight, output_bias, gain_second, shift_second, up_weight, up_bias, down_weight, down_bias)
    params = tuple((item.astype(jnp.float32) for item in params))
    block_count = TOKENS // TOK_DEV
    token_blocks = tokens.astype(jnp.float32).reshape(block_count, TOK_DEV, D)
    crop_blocks = crop_ids.reshape(block_count, TOK_DEV)
    slope_blocks = cotangent.astype(jnp.float32).reshape(block_count, TOK_DEV, D)

    def one_block(carry, inputs):
        token_block, crop_block, slope_block = inputs

        def apply_layer(values, weights):
            return forward(values, crop_block, weights)
        output, pullback = jax.vjp(apply_layer, token_block, params)
        grad_tokens, grad_params = pullback(slope_block)
        carry = jax.tree.map(lambda total, term: total + term, carry, grad_params)
        return (carry, (output, grad_tokens))
    zeros = jax.tree.map(jnp.zeros_like, params)
    sums, (outputs, grad_inputs) = lax.scan(one_block, zeros, (token_blocks, crop_blocks, slope_blocks))
    return (outputs.reshape(TOKENS, D), grad_inputs.reshape(TOKENS, D), sums[0], sums[1], sums[2], sums[3], sums[4], sums[5], sums[6], sums[7], sums[8], sums[9], sums[10], sums[11])
```

```python
import functools

import jax
import jax.numpy as jnp
from jax import lax
from jax.experimental import pallas as pl
from jax.experimental.pallas import tpu as pltpu
from jax.sharding import PartitionSpec as P

HD = 64
PAIR = 2 * HD
EPS = 1e-06
WIN = 256
SNAP = 16
TILE = 256
CHUNK = 512
LIMIT = 58 << 20
F32 = jnp.float32
BF16 = jnp.bfloat16
NT = (((1,), (1,)), ((), ()))
NN = (((1,), (0,)), ((), ()))


def mm(left, right, dims=NN):
    return lax.dot_general(left, right, dims, preferred_element_type=F32)


def fold(values):
    return jnp.sum(values.reshape(values.shape[0] // 8, 8, values.shape[1]), axis=0)


def swap(value, axis, size, bit):
    return lax.ppermute(value, axis, [(i, i ^ bit) for i in range(size)])


def gather_eight(shard, x_first):
    go = lambda v, bit: swap(v, "fsdp", 8, bit)
    via_x, via_y = go(shard, 2), go(shard, 4)
    far = go(via_x, 4) if x_first else go(via_y, 2)
    own = [shard, via_x, via_y, far]
    pieces = []
    for value in own:
        pieces += [value, go(value, 1)]
    return pieces


def gather_weight(shards, size):
    if size == 8:
        return [(gather_eight(shard, at % 2 == 0), True) for at, shard in enumerate(shards)]
    return [([lax.all_gather(shard, "fsdp", axis=0, tiled=True)], False) for shard in shards]


def pick(value, at, axis):
    return lax.dynamic_index_in_dim(value, at, axis, keepdims=False)


def add_low(left, right):
    return (left.astype(F32) + right.astype(F32)).astype(left.dtype)


def scatter_sum(value, size, x_first):
    if size != 8:
        return lax.psum_scatter(value, "fsdp", scatter_dimension=0, tiled=True)[0]
    me = lax.axis_index("fsdp")
    core, at_x, at_y = me & 1, (me >> 1) & 1, me >> 2
    rows, columns = value.shape[1:]
    pairs = value.reshape(4, 2, rows, columns)
    total = add_low(pick(pairs, core, 1), swap(pick(pairs, 1 - core, 1), "fsdp", 8, 1))
    total = total.reshape(2, 2, rows, columns)
    if x_first:
        total = add_low(pick(total, at_x, 1), swap(pick(total, 1 - at_x, 1), "fsdp", 8, 2))
        return add_low(pick(total, at_y, 0), swap(pick(total, 1 - at_y, 0), "fsdp", 8, 4))
    total = add_low(pick(total, at_y, 0), swap(pick(total, 1 - at_y, 0), "fsdp", 8, 4))
    return add_low(pick(total, at_x, 0), swap(pick(total, 1 - at_x, 0), "fsdp", 8, 2))


def join(mine, other, bit):
    first = jnp.where(bit == 0, mine, other)
    second = jnp.where(bit == 0, other, mine)
    return jnp.concatenate([first, second], axis=0)


def reduce_groups(value, size):
    if size != 4:
        return lax.psum(value, "dp")
    me = lax.axis_index("dp")
    low, high = me & 1, me >> 1
    rows, columns = value.shape
    if rows % 4:
        value = add_low(value, swap(value, "dp", 4, 1))
        return add_low(value, swap(value, "dp", 4, 2))
    half = value.reshape(2, rows // 2, columns)
    half = add_low(pick(half, low, 0), swap(pick(half, 1 - low, 0), "dp", 4, 1))
    part = half.reshape(2, rows // 4, columns)
    part = add_low(pick(part, high, 0), swap(pick(part, 1 - high, 0), "dp", 4, 2))
    half = join(part, swap(part, "dp", 4, 2), high)
    return join(half, swap(half, "dp", 4, 1), low)


class Weight:
    def __init__(self, shape, split, gathered, size):
        self.shape = shape
        self.arrays = []
        self.places = []
        at_row = at_column = 0
        for pieces, is_shard in gathered:
            rows, columns = pieces[0].shape
            for offset, piece in enumerate(pieces):
                if is_shard:
                    step = shape[0] // size
                    self.places.append((len(self.arrays), offset, step, at_row, rows, at_column, columns))
                else:
                    self.places.append((len(self.arrays), None, 0, at_row, rows, at_column, columns))
                self.arrays.append(piece)
            if split == "columns":
                at_column += columns
            else:
                at_row += rows

    def copies(self, me, refs, scratch, sems):
        made = []
        for at, (ref, offset, step, row, rows, column, columns) in enumerate(self.places):
            start = row if offset is None else pl.multiple_of((me ^ offset) * step + row, 16)
            target = scratch.at[pl.ds(start, rows), pl.ds(column, columns)]
            made.append(pltpu.make_async_copy(refs[ref], target, sems.at[at]))
        return made

    def scratch(self):
        return [pltpu.VMEM(self.shape, BF16), pltpu.SemaphoreType.DMA((len(self.places),))]


def any_specs(count):
    return [pl.BlockSpec(memory_space=pl.ANY)] * count


def params():
    return pltpu.CompilerParams(dimension_semantics=("arbitrary",), vmem_limit_bytes=LIMIT)


def cost(flops, reads, exps=0):
    return pl.CostEstimate(flops=int(flops), transcendentals=int(exps), bytes_accessed=int(reads))


def row_spec(columns):
    return pl.BlockSpec((TILE, columns), lambda i, *_: (i, 0))


def whole_spec(shape):
    return pl.BlockSpec(shape, lambda i, *_: (0,) * len(shape))


def normed(values):
    center = values - jnp.mean(values, axis=-1, keepdims=True)
    scale = lax.rsqrt(jnp.mean(center * center, axis=-1, keepdims=True) + EPS)
    return center * scale, scale


def norm_back(grad, unit, scale, gain):
    scaled = grad * gain
    first = jnp.mean(scaled, axis=-1, keepdims=True)
    second = jnp.mean(scaled * unit, axis=-1, keepdims=True)
    return (scaled - first - unit * second) * scale


def load_first(weights, me, refs, scratches):
    @pl.when(pl.program_id(0) == 0)
    def _():
        started = []
        at = 0
        for weight, (scratch, sems) in zip(weights, scratches):
            mine = refs[at : at + len(weight.arrays)]
            at += len(weight.arrays)
            started += weight.copies(me, mine, scratch, sems)
        for copy in started:
            copy.start()
        for copy in started:
            copy.wait()


def joint_kernel(weight, me_ref, x_ref, gain_ref, shift_ref, bias_ref, *refs):
    count = len(weight.arrays)
    out_ref, hidden_ref, scratch, sems = refs[count:]
    load_first([weight], me_ref[0], refs[:count], [(scratch, sems)])
    unit, _ = normed(x_ref[...].astype(F32))
    hidden = (unit * gain_ref[...] + shift_ref[...]).astype(BF16)
    hidden_ref[...] = hidden
    out_ref[...] = (mm(hidden, scratch[...]) + bias_ref[...]).astype(BF16)


def joint_forward(me, tokens, gain, shift, bias, weight):
    rows, width = tokens.shape
    columns = weight.shape[1]
    return pl.pallas_call(
        functools.partial(joint_kernel, weight),
        grid_spec=pltpu.PrefetchScalarGridSpec(
            num_scalar_prefetch=1,
            grid=(rows // TILE,),
            in_specs=[row_spec(width), whole_spec((1, width)), whole_spec((1, width)), whole_spec((1, columns))]
            + any_specs(len(weight.arrays)),
            out_specs=[row_spec(columns), row_spec(width)],
            scratch_shapes=weight.scratch(),
        ),
        out_shape=[jax.ShapeDtypeStruct((rows, columns), BF16), jax.ShapeDtypeStruct((rows, width), BF16)],
        compiler_params=params(),
        cost_estimate=cost(2 * rows * width * columns, 2 * (rows * (2 * width + columns) + width * columns)),
        name="joint_forward",
    )(me, tokens, gain, shift, bias, *weight.arrays)


def plan_groups(starts_ref, crops_ref, table_ref, bias_ref, rows):
    def one(state):
        at, start = state
        base = jnp.minimum((start // SNAP) * SNAP, rows - WIN)
        base = pl.multiple_of(base, SNAP)
        edge = base + WIN
        stop = jnp.where(edge >= rows, rows, starts_ref[jnp.minimum(edge, rows - 1)])
        table_ref[0, at] = base
        table_ref[1, at] = start
        down = crops_ref[pl.ds(base, WIN), :]
        across = down.T
        down = jnp.concatenate([down] * (WIN // 128), axis=1)
        across = jnp.concatenate([across] * (WIN // 128), axis=0)
        bias_ref[at] = jnp.where(down == across, 0.0, -1e30)
        return at + 1, stop

    more = lambda state: jnp.logical_and(state[1] < rows, state[0] < group_bound(rows))
    table_ref[2, 0] = lax.while_loop(more, one, (jnp.int32(0), jnp.int32(0)))[0]


def group_bound(rows):
    return 2 * (rows // (WIN - SNAP + 2)) + 2


def keep_from(ref, base, start, columns, value):
    window = (pl.ds(base, WIN), pl.ds(columns, PAIR))
    row = base + lax.broadcasted_iota(jnp.int32, (WIN, PAIR), 0)
    ref[window] = jnp.where(row >= start, value, ref[window].astype(F32)).astype(ref.dtype)


def attend_kernel(rows, starts_ref, crops_ref, joint_ref, mixed_ref, log_ref, table_ref, bias_ref):
    @pl.when(pl.program_id(0) == 0)
    def _():
        plan_groups(starts_ref, crops_ref, table_ref, bias_ref, rows)

    lane = lax.broadcasted_iota(jnp.int32, (WIN, PAIR), 1)

    def one(at, carry):
        base = pl.multiple_of(table_ref[0, at], SNAP)
        start = table_ref[1, at]
        window = pl.ds(base, WIN)
        query = joint_ref[window, 0:PAIR] * jnp.asarray(HD**-0.5, BF16)
        key = joint_ref[window, PAIR : 2 * PAIR]
        value_t = joint_ref[window, 2 * PAIR : 3 * PAIR].T
        outs = []
        for head in range(2):
            mine = (lane >= HD) if head else (lane < HD)
            scores = mm(jnp.where(mine, key, jnp.zeros_like(key)), query, NT) + bias_ref[at]
            top = jnp.max(scores, axis=0, keepdims=True)
            expo = jnp.exp(scores - top)
            total = jnp.sum(expo, axis=0, keepdims=True)
            mixed = mm(value_t[head * HD : (head + 1) * HD, :], expo.astype(BF16))
            outs.append(mixed * (1.0 / total))
            log_ref[0, at, pl.ds(head, 1), :] = top + jnp.log(total)
        keep_from(mixed_ref, base, start, 0, jnp.concatenate(outs, axis=0).T)
        return carry

    lax.fori_loop(0, table_ref[2, 0], one, 0)


def attend(starts, crops, joint):
    rows, columns = joint.shape
    pairs = columns // (3 * PAIR)
    groups = group_bound(rows)
    return pl.pallas_call(
        functools.partial(attend_kernel, rows),
        grid_spec=pltpu.PrefetchScalarGridSpec(
            num_scalar_prefetch=1,
            grid=(pairs,),
            in_specs=[whole_spec((rows, 128)), pl.BlockSpec((rows, 3 * PAIR), lambda i, *_: (0, i))],
            out_specs=[
                pl.BlockSpec((rows, PAIR), lambda i, *_: (0, i)),
                pl.BlockSpec((1, groups, 8, WIN), lambda i, *_: (i, 0, 0, 0)),
            ],
            scratch_shapes=[pltpu.SMEM((3, 16), jnp.int32), pltpu.VMEM((groups, WIN, WIN), F32)],
        ),
        out_shape=[
            jax.ShapeDtypeStruct((rows, pairs * PAIR), BF16),
            jax.ShapeDtypeStruct((pairs, groups, 8, WIN), F32),
        ],
        compiler_params=params(),
        cost_estimate=cost(pairs * 6 * 8 * WIN**3, 2 * rows * columns * 4 // 3, pairs * 12 * WIN * WIN),
        name="attend",
    )(starts, crops, joint)


def attend_back_kernel(rows, starts_ref, crops_ref, joint_ref, mixed_ref, grad_ref, log_ref, out_ref, table_ref, bias_ref):
    @pl.when(pl.program_id(0) == 0)
    def _():
        plan_groups(starts_ref, crops_ref, table_ref, bias_ref, rows)

    lane = lax.broadcasted_iota(jnp.int32, (WIN, PAIR), 1)

    def one(at, carry):
        base = pl.multiple_of(table_ref[0, at], SNAP)
        start = table_ref[1, at]
        window = pl.ds(base, WIN)
        query = joint_ref[window, 0:PAIR] * jnp.asarray(HD**-0.5, BF16)
        key = joint_ref[window, PAIR : 2 * PAIR]
        value = joint_ref[window, 2 * PAIR : 3 * PAIR]
        key_t = key.T
        grad = grad_ref[window, :]
        inner_t = (grad.astype(F32) * mixed_ref[window, :].astype(F32)).T
        d_query, d_key, d_value = [], [], []
        for head in range(2):
            mine = (lane >= HD) if head else (lane < HD)
            zero = jnp.zeros_like(key)
            scores = mm(jnp.where(mine, key, zero), query, NT) + bias_ref[at]
            weights = jnp.exp(scores - log_ref[0, at, pl.ds(head, 1), :])
            inner = jnp.sum(inner_t[head * HD : (head + 1) * HD, :], axis=0, keepdims=True)
            d_weights = mm(jnp.where(mine, value, zero), grad, NT)
            d_scores = (weights * (d_weights - inner)).astype(BF16)
            d_value.append(mm(weights.astype(BF16), grad))
            d_key.append(mm(d_scores, query))
            d_query.append(mm(key_t[head * HD : (head + 1) * HD, :], d_scores) * HD**-0.5)
        low = lane < HD
        keep_from(out_ref, base, start, 0, jnp.concatenate(d_query, axis=0).T)
        keep_from(out_ref, base, start, PAIR, jnp.where(low, d_key[0], d_key[1]))
        keep_from(out_ref, base, start, 2 * PAIR, jnp.where(low, d_value[0], d_value[1]))
        return carry

    lax.fori_loop(0, table_ref[2, 0], one, 0)


def attend_back(starts, crops, joint, mixed, grad, logs, first, count):
    rows = joint.shape[0]
    groups = group_bound(rows)
    wide = lambda columns: pl.BlockSpec((rows, columns), lambda i, *_: (0, first + i))
    return pl.pallas_call(
        functools.partial(attend_back_kernel, rows),
        grid_spec=pltpu.PrefetchScalarGridSpec(
            num_scalar_prefetch=1,
            grid=(count,),
            in_specs=[
                whole_spec((rows, 128)),
                wide(3 * PAIR),
                wide(PAIR),
                wide(PAIR),
                pl.BlockSpec((1, groups, 8, WIN), lambda i, *_: (first + i, 0, 0, 0)),
            ],
            out_specs=pl.BlockSpec((rows, 3 * PAIR), lambda i, *_: (0, i)),
            scratch_shapes=[pltpu.SMEM((3, 16), jnp.int32), pltpu.VMEM((groups, WIN, WIN), F32)],
        ),
        out_shape=jax.ShapeDtypeStruct((rows, count * 3 * PAIR), BF16),
        compiler_params=params(),
        cost_estimate=cost(count * 6 * 20 * WIN**3, 2 * rows * count * 8 * PAIR, count * 12 * WIN * WIN),
        name="attend_back",
    )(starts, crops, joint, mixed, grad, logs)


def up_kernel(out_weight, up_weight, me_ref, x_ref, mixed_ref, vec_ref, bias_ref, *refs):
    count = len(out_weight.arrays) + len(up_weight.arrays)
    middle_ref, hidden_ref, active_ref, slope_ref, out_s, out_sem, up_s, up_sem = refs[count:]
    load_first([out_weight, up_weight], me_ref[0], refs[:count], [(out_s, out_sem), (up_s, up_sem)])
    middle = x_ref[...].astype(F32) + mm(mixed_ref[...], out_s[...]) + vec_ref[0:1, :]
    middle_ref[...] = middle
    unit, _ = normed(middle)
    hidden = (unit * vec_ref[1:2, :] + vec_ref[2:3, :]).astype(BF16)
    hidden_ref[...] = hidden
    for at in range(0, up_weight.shape[1], CHUNK):
        part = pl.ds(at, CHUNK)
        value = mm(hidden, up_s[:, part]) + bias_ref[:, part]
        below = 0.5 + 0.5 * lax.erf(value * (0.5**0.5))
        active_ref[:, part] = (value * below).astype(BF16)
        bell = jnp.exp(value * value * -0.5) * 0.3989422804014327
        slope_ref[:, part] = (below + value * bell).astype(BF16)


def up_forward(me, tokens, mixed, vectors, bias, out_weight, up_weight):
    rows, width = tokens.shape
    inner = up_weight.shape[1]
    arrays = out_weight.arrays + up_weight.arrays
    return pl.pallas_call(
        functools.partial(up_kernel, out_weight, up_weight),
        grid_spec=pltpu.PrefetchScalarGridSpec(
            num_scalar_prefetch=1,
            grid=(rows // TILE,),
            in_specs=[row_spec(width), row_spec(width), whole_spec(vectors.shape), whole_spec((1, inner))]
            + any_specs(len(arrays)),
            out_specs=[row_spec(width), row_spec(width), row_spec(inner), row_spec(inner)],
            scratch_shapes=out_weight.scratch() + up_weight.scratch(),
        ),
        out_shape=[
            jax.ShapeDtypeStruct((rows, width), F32),
            jax.ShapeDtypeStruct((rows, width), BF16),
            jax.ShapeDtypeStruct((rows, inner), BF16),
            jax.ShapeDtypeStruct((rows, inner), BF16),
        ],
        compiler_params=params(),
        cost_estimate=cost(2 * rows * width * (width + inner), rows * (10 * width + 4 * inner) + 2 * width * inner, rows * inner * 2),
        name="up_forward",
    )(me, tokens, mixed, vectors, bias, *arrays)


def middle_kernel(
    out_weight, up_weight, down_weight, me_ref, middle_ref, grad_ref, active_ref, slope_ref, vec_ref, *refs
):
    weights = [out_weight, up_weight, down_weight]
    count = sum(len(weight.arrays) for weight in weights)
    refs, rest = refs[:count], refs[count:]
    acts_ref, ga_ref, gmid_ref, glow_ref, gmix_ref, sums_ref, upsum_ref = rest[:7]
    out_s, out_sem, up_s, up_sem, down_s, down_sem = rest[7:]
    load_first(weights, me_ref[0], refs, [(out_s, out_sem), (up_s, up_sem), (down_s, down_sem)])

    @pl.when(pl.program_id(0) == 0)
    def _():
        sums_ref[...] = jnp.zeros_like(sums_ref)
        upsum_ref[...] = jnp.zeros_like(upsum_ref)

    middle = middle_ref[...]
    grad = grad_ref[...]
    acts_ref[...] = middle + mm(active_ref[...], down_s[...]) + vec_ref[3:4, :]
    total = None
    for at in range(0, up_weight.shape[1], CHUNK):
        part = pl.ds(at, CHUNK)
        inner = (mm(grad, down_s[part, :], NT) * slope_ref[:, part].astype(F32)).astype(BF16)
        ga_ref[:, part] = inner
        upsum_ref[:, part] += fold(inner.astype(F32))
        term = mm(inner, up_s[:, part], NT)
        total = term if total is None else total + term
    unit, scale = normed(middle)
    wide = grad.astype(F32)
    sums_ref[0] += fold(total * unit)
    sums_ref[1] += fold(total)
    sums_ref[2] += fold(wide)
    gmid = wide + norm_back(total, unit, scale, vec_ref[1:2, :])
    gmid_ref[...] = gmid
    low = gmid.astype(BF16)
    glow_ref[...] = low
    sums_ref[3] += fold(low.astype(F32))
    gmix_ref[...] = mm(low, out_s[...], NT).astype(BF16)


def middle_back(me, middle, grad, active, slope, vectors, out_weight, up_weight, down_weight):
    rows, width = middle.shape
    inner = active.shape[1]
    arrays = out_weight.arrays + up_weight.arrays + down_weight.arrays
    return pl.pallas_call(
        functools.partial(middle_kernel, out_weight, up_weight, down_weight),
        grid_spec=pltpu.PrefetchScalarGridSpec(
            num_scalar_prefetch=1,
            grid=(rows // TILE,),
            in_specs=[row_spec(width), row_spec(width), row_spec(inner), row_spec(inner), whole_spec(vectors.shape)]
            + any_specs(len(arrays)),
            out_specs=[
                row_spec(width),
                row_spec(inner),
                row_spec(width),
                row_spec(width),
                row_spec(width),
                whole_spec((4, 8, width)),
                whole_spec((8, inner)),
            ],
            scratch_shapes=out_weight.scratch() + up_weight.scratch() + down_weight.scratch(),
        ),
        out_shape=[
            jax.ShapeDtypeStruct((rows, width), F32),
            jax.ShapeDtypeStruct((rows, inner), BF16),
            jax.ShapeDtypeStruct((rows, width), F32),
            jax.ShapeDtypeStruct((rows, width), BF16),
            jax.ShapeDtypeStruct((rows, width), BF16),
            jax.ShapeDtypeStruct((4, 8, width), F32),
            jax.ShapeDtypeStruct((8, inner), F32),
        ],
        compiler_params=params(),
        cost_estimate=cost(2 * rows * width * (width + 3 * inner), rows * (18 * width + 6 * inner) + 4 * width * inner),
        name="middle_back",
    )(me, middle, grad, active, slope, vectors, *arrays)


def first_kernel(weight, me_ref, x_ref, gmid_ref, part_a_ref, part_b_ref, gain_ref, *refs):
    count = len(weight.arrays)
    out_ref, sums_ref, joint_sum_ref, scratch, sems = refs[count:]
    load_first([weight], me_ref[0], refs[:count], [(scratch, sems)])

    @pl.when(pl.program_id(0) == 0)
    def _():
        sums_ref[...] = jnp.zeros_like(sums_ref)
        joint_sum_ref[...] = jnp.zeros_like(joint_sum_ref)

    grad = jnp.concatenate([part_a_ref[...], part_b_ref[...]], axis=1)
    joint_sum_ref[...] += fold(grad.astype(F32))
    total = mm(grad, scratch[...], NT)
    unit, scale = normed(x_ref[...].astype(F32))
    sums_ref[0] += fold(total * unit)
    sums_ref[1] += fold(total)
    out_ref[...] = gmid_ref[...] + norm_back(total, unit, scale, gain_ref[...])


def first_back(me, tokens, gmid, part_a, part_b, gain, weight):
    rows, width = tokens.shape
    columns = weight.shape[1]
    return pl.pallas_call(
        functools.partial(first_kernel, weight),
        grid_spec=pltpu.PrefetchScalarGridSpec(
            num_scalar_prefetch=1,
            grid=(rows // TILE,),
            in_specs=[row_spec(width), row_spec(width), row_spec(columns // 2), row_spec(columns // 2), whole_spec((1, width))]
            + any_specs(len(weight.arrays)),
            out_specs=[row_spec(width), whole_spec((2, 8, width)), whole_spec((8, columns))],
            scratch_shapes=weight.scratch(),
        ),
        out_shape=[
            jax.ShapeDtypeStruct((rows, width), F32),
            jax.ShapeDtypeStruct((2, 8, width), F32),
            jax.ShapeDtypeStruct((8, columns), F32),
        ],
        compiler_params=params(),
        cost_estimate=cost(2 * rows * width * columns, rows * (10 * width + 2 * columns) + 2 * width * columns),
        name="first_back",
    )(me, tokens, gmid, part_a, part_b, gain, *weight.arrays)


def by_pair(matrix, parts):
    rows, columns = matrix.shape
    pairs = columns // (parts * PAIR)
    return matrix.reshape(rows, parts, pairs, PAIR).transpose(0, 2, 1, 3).reshape(rows, columns)


def by_part(matrix, parts):
    rows, columns = matrix.shape
    pairs = columns // (parts * PAIR)
    return matrix.reshape(rows, pairs, parts, PAIR).transpose(0, 2, 1, 3).reshape(rows, columns)


def weight_grad(left, right):
    return lax.dot_general(left, right, (((0,), (0,)), ((), ())), preferred_element_type=F32).astype(BF16)


def on_device(
    fsdp,
    dp,
    tokens,
    crop_ids,
    gain_first,
    shift_first,
    joint_weight,
    joint_bias,
    output_weight,
    output_bias,
    gain_second,
    shift_second,
    up_weight,
    up_bias,
    down_weight,
    down_bias,
    cotangent,
):
    rows, width = tokens.shape
    inner = up_bias.shape[0] * fsdp
    joint_width = joint_weight.shape[1]
    rank = lax.axis_index("fsdp")
    me = rank.astype(jnp.int32).reshape(1)
    own = width // fsdp
    own_up = inner // fsdp

    pack = jnp.concatenate(
        [
            gain_first,
            shift_first,
            joint_bias.reshape(-1),
            output_bias,
            gain_second,
            shift_second,
            down_bias,
            up_bias,
        ]
    ).reshape(1, -1)
    if fsdp == 8:
        pieces = jnp.concatenate([pack] + [swap(pack, "fsdp", 8, k) for k in range(1, 8)], axis=0)
        order = (jnp.arange(8)[:, None] ^ rank) == jnp.arange(8)[None, :]
        vectors = mm(order.astype(BF16), pieces)
    else:
        vectors = lax.all_gather(pack, "fsdp", axis=0, tiled=True).astype(F32)
    small = vectors[:, : 8 * own].reshape(fsdp, 8, own).transpose(1, 0, 2).reshape(8, width)
    up_row = vectors[:, 8 * own :].reshape(1, inner)
    gain_one, shift_one = small[0:1], small[1:2]
    bias_joint = jnp.concatenate([small[2:3], jnp.zeros((1, width), F32), small[3:4]], axis=1)
    bias_joint = by_pair(bias_joint, 3)
    second = jnp.stack([small[4], small[5], small[6], small[7]] + [jnp.zeros((width,), F32)] * 4)

    paired = by_pair(joint_weight, 3)
    half = joint_width // 2
    joint_parts = gather_weight([paired[:, :half], paired[:, half:]], fsdp)
    joint_full = Weight((width, joint_width), "columns", joint_parts, fsdp)
    gate = joint_full.arrays[-1]
    output_in, up_in, gate = lax.optimization_barrier((output_weight, up_weight, gate))
    out_full = Weight((width, width), "columns", gather_weight([output_in], fsdp), fsdp)
    cut = inner // 2
    up_full = Weight((width, inner), "columns", gather_weight([up_in[:, :cut], up_in[:, cut:]], fsdp), fsdp)
    down_in, gate = lax.optimization_barrier((down_weight, up_full.arrays[-1]))
    if fsdp == 8:
        cut = own_up // 2
        down_parts = gather_weight([down_in[:cut], down_in[cut:]], fsdp)
    else:
        down_parts = gather_weight([down_in], fsdp)
    down_full = Weight((inner, width), "rows", down_parts, fsdp)

    starts = jnp.sum((crop_ids[None, :] < crop_ids[:, None]).astype(jnp.int32), axis=1)
    crops = jnp.broadcast_to(crop_ids.astype(F32)[:, None], (rows, 128))

    joint, hidden_first = joint_forward(me, tokens, gain_one, shift_one, bias_joint, joint_full)
    mixed, logs = attend(starts, crops, joint)
    middle, hidden_second, active, slope = up_forward(me, tokens, mixed, second, up_row, out_full, up_full)
    acts, grad_up, grad_middle, grad_low, grad_mixed, sums, up_sums = middle_back(
        me, middle, cotangent, active, slope, second, out_full, up_full, down_full
    )

    def finish(slabs, x_first):
        return reduce_groups(scatter_sum(slabs, fsdp, x_first), dp)

    down_sum = finish(weight_grad(active, cotangent).reshape(fsdp, own_up, width), False)
    up_sum = finish(weight_grad(hidden_second, grad_up).reshape(fsdp, own, inner), True)
    out_sum = finish(weight_grad(mixed, grad_low).reshape(fsdp, own, width), False)

    pairs = joint_width // (3 * PAIR)
    near = pairs // 2
    grad_a = attend_back(starts, crops, joint, mixed, grad_mixed, logs, 0, near)
    sum_a = finish(weight_grad(hidden_first, grad_a).reshape(fsdp, own, -1), True)
    grad_b = attend_back(starts, crops, joint, mixed, grad_mixed, logs, near, pairs - near)
    sum_b = finish(weight_grad(hidden_first, grad_b).reshape(fsdp, own, -1), False)
    input_grad, first_sums, joint_sums = first_back(me, tokens, grad_middle, grad_a, grad_b, gain_one, joint_full)

    joint_row = by_part(jnp.sum(joint_sums, axis=0, keepdims=True), 3)
    rows_out = jnp.stack(
        [
            jnp.sum(first_sums[0], axis=0),
            jnp.sum(first_sums[1], axis=0),
            joint_row[0, :width],
            joint_row[0, 2 * width :],
            jnp.sum(sums[3], axis=0),
            jnp.sum(sums[0], axis=0),
            jnp.sum(sums[1], axis=0),
            jnp.sum(sums[2], axis=0),
        ]
    )
    packed = jnp.concatenate(
        [
            rows_out.reshape(8, fsdp, own).transpose(1, 0, 2).reshape(fsdp, 8 * own),
            jnp.sum(up_sums, axis=0).reshape(fsdp, own_up),
        ],
        axis=1,
    )
    total = finish(packed.reshape(fsdp, 1, -1), True)[0]
    vec = lambda at: total[at * own : (at + 1) * own]
    grad_joint = by_part(jnp.concatenate([sum_a, sum_b], axis=1), 3)
    return (
        acts,
        input_grad,
        vec(0),
        vec(1),
        grad_joint.astype(F32),
        jnp.stack([vec(2), vec(3)]),
        out_sum.astype(F32),
        vec(4),
        vec(5),
        vec(6),
        up_sum.astype(F32),
        total[8 * own :],
        down_sum.astype(F32),
        vec(7),
    )


def solution(mesh):
    rows, line, flat = P(("fsdp", "dp"), None), P("fsdp"), P("fsdp", None)
    both = P(None, "fsdp")
    return jax.shard_map(
        functools.partial(on_device, mesh.shape["fsdp"], mesh.shape["dp"]),
        mesh=mesh,
        in_specs=(rows, P(("fsdp", "dp")), line, line, flat, both, flat, line, line, line, flat, line, flat, line, rows),
        out_specs=(rows, rows, line, line, flat, both, flat, line, line, line, flat, line, flat, line),
        check_vma=False,
    )
```

```python
import functools

import jax
import jax.numpy as jnp
from jax import lax
from jax.experimental import pallas as pl
from jax.experimental.pallas import tpu as pltpu
from jax.sharding import PartitionSpec as P

HD = 64
PAIR = 2 * HD
EPS = 1e-06
WIN = 256
SNAP = 16
TILE = 256
CHUNK = 512
LIMIT = 58 << 20
F32 = jnp.float32
BF16 = jnp.bfloat16
NT = (((1,), (1,)), ((), ()))
NN = (((1,), (0,)), ((), ()))


def mm(left, right, dims=NN):
    return lax.dot_general(left, right, dims, preferred_element_type=F32)


def fold(values):
    return jnp.sum(values.reshape(values.shape[0] // 8, 8, values.shape[1]), axis=0)


CORE = [(i, i ^ 1) for i in range(8)]
FIRST = [(i, i ^ (4 if i & 1 else 2)) for i in range(8)]
SECOND = [(i, i ^ (2 if i & 1 else 4)) for i in range(8)]


def send(value, pairs):
    return lax.ppermute(value, "fsdp", pairs)


def send_dp(value, bit):
    return lax.ppermute(value, "dp", [(i, i ^ bit) for i in range(4)])


def after(value, *others):
    return lax.optimization_barrier((value,) + others)[0]


def pick(value, at, axis=0):
    return lax.dynamic_index_in_dim(value, at, axis, keepdims=False)


def wide(value):
    return value.astype(F32)


class Scatter:
    def __init__(self, slabs):
        me = lax.axis_index("fsdp")
        self.core = me & 1
        at_x, at_y = (me >> 1) & 1, me >> 2
        rows, columns = slabs.shape[1:]
        self.slabs = slabs.reshape(4, 2, rows, columns)
        even = self.core == 0
        keep, leave = 1 - at_y, 1 - at_x
        self.away = (jnp.where(even, 2 * keep, leave), jnp.where(even, 2 * keep + 1, 2 + leave))
        self.near = jnp.where(even, at_x, at_y)
        self.chip = 2 * at_y + at_x
        self.next_chip = jnp.where(even, 2 * at_y + 1 - at_x, 2 * (1 - at_y) + at_x)
        self.mine = pick(self.slabs, self.core, 1)
        self.got = []

    def give(self):
        if not self.got:
            return pick(self.slabs, 1 - self.core, 1)
        if len(self.got) == 1:
            return jnp.stack([wide(pick(self.mine, at)) + wide(pick(self.got[0], at)) for at in self.away]).astype(BF16)
        total = wide(pick(self.mine, self.next_chip)) + wide(pick(self.got[0], self.next_chip))
        return (total + wide(pick(self.got[1], 1 - self.near))).astype(BF16)

    def take(self, value):
        self.got.append(value)

    def pairs(self):
        return (CORE, SECOND, FIRST)[len(self.got)]

    def result(self):
        total = wide(pick(self.mine, self.chip)) + wide(pick(self.got[0], self.chip))
        return (total + wide(pick(self.got[1], self.near)) + wide(self.got[2])).astype(BF16)


class Sum:
    def __init__(self, value, short=False):
        me = lax.axis_index("dp")
        self.low, self.high = me & 1, me >> 1
        self.value = value
        self.short = short
        self.got = []
        self.split()

    def split(self):
        rows, columns = self.value.shape
        self.halves = self.value.reshape(2, rows // 2, columns)

    def half(self):
        return wide(pick(self.halves, self.low)) + wide(self.got[0])

    def quarters(self):
        half = self.half()
        return half.reshape(2, half.shape[0] // 2, half.shape[1])

    def own(self):
        return (pick(self.quarters(), self.high) + wide(self.got[1])).astype(BF16)

    def join(self, mine, other, bit):
        return jnp.concatenate([jnp.where(bit == 0, mine, other), jnp.where(bit == 0, other, mine)], axis=0)

    def give(self):
        step = len(self.got)
        if self.short:
            return self.value.astype(BF16) if step == 0 else (wide(self.value) + wide(self.got[0])).astype(BF16)
        if step == 0:
            return pick(self.halves, 1 - self.low).astype(BF16)
        if step == 1:
            return pick(self.quarters(), 1 - self.high).astype(BF16)
        if step == 2:
            return self.own()
        return self.join(self.own(), self.got[2], self.high)

    def bit(self):
        return ((1, 2) if self.short else (1, 2, 2, 1))[len(self.got)]

    def take(self, value):
        self.got.append(value)

    def result(self):
        if self.short:
            return wide(self.value) + wide(self.got[0]) + wide(self.got[1])
        half = self.join(self.own(), self.got[2], self.high)
        return wide(self.join(half, self.got[3], self.low))


class Grad:
    def __init__(self, slabs, fsdp, dp, short=False):
        self.dp, self.short = dp, short
        self.sum = self.scatter = None
        if fsdp == 8:
            self.scatter = Scatter(slabs)
        else:
            self.enter(lax.psum_scatter(slabs, "fsdp", scatter_dimension=0, tiled=True)[0])

    def enter(self, value):
        if self.dp == 4:
            self.sum = Sum(value, self.short)
        else:
            self.out = lax.psum(value, "dp").astype(F32)

    def step(self, *behind):
        stage = self.scatter if self.scatter is not None else self.sum
        if stage is None or (stage is self.sum and len(stage.got) == (2 if self.short else 4)):
            return None
        if behind and stage.got:
            stage.got[-1] = after(stage.got[-1], *behind)
        elif behind and stage is self.sum:
            stage.value = after(stage.value, *behind)
            stage.split()
        given = stage.give()
        if stage is self.sum:
            stage.take(send_dp(given, stage.bit()))
            return given
        stage.take(send(given, stage.pairs()))
        if len(stage.got) == 3:
            self.scatter = None
            self.enter(stage.result())
        return given

    def result(self):
        while self.step() is not None:
            pass
        return self.sum.result() if self.sum is not None else self.out


class Gather:
    def __init__(self, shard, fsdp):
        self.fsdp = fsdp
        self.shard = shard

    def whole(self):
        self.arrays = [lax.all_gather(self.shard, "fsdp", axis=0, tiled=True)]
        return self

    def first(self):
        self.two = jnp.stack([self.shard, send(self.shard, FIRST)])
        return self.two

    def second(self):
        self.more = send(self.two, SECOND)
        self.swapped = send(self.two, CORE)
        return self.more

    def third(self):
        self.arrays = [self.two, self.more, self.swapped, send(self.more, CORE)]
        return self.arrays[-1]

    def blocks(self):
        def owner(theirs, far, at):
            def of(me):
                base = me ^ 1 if theirs else me
                one, two = 2 + 2 * (base & 1), 4 - 2 * (base & 1)
                return base ^ ((two if far else 0) + (one if at else 0))

            return of

        return [(a, at, owner(a >= 2, a % 2 == 1, at)) for a in range(4) for at in range(2)]


class Weight:
    def __init__(self, gathered, first, columns, deep=1, spare=0):
        self.gathered, self.first, self.columns, self.deep = gathered, first, columns, deep
        self.arrays = gathered.arrays
        self.rows = gathered.shard.shape[0] - spare
        self.shape = (self.rows * deep * gathered.fsdp, columns)
        self.count = deep * gathered.fsdp if gathered.fsdp == 8 else 1

    def copies(self, me, refs, scratch, sems):
        if self.gathered.fsdp != 8:
            source = refs[0].at[:, pl.ds(self.first, self.columns)]
            return [pltpu.make_async_copy(source, scratch, sems.at[0])]
        made = []
        for array, at, owner in self.gathered.blocks():
            for part in range(self.deep):
                start = pl.multiple_of((owner(me) * self.deep + part) * self.rows, 16)
                source = refs[array].at[at, pl.ds(0, self.rows), pl.ds(self.first + part * self.columns, self.columns)]
                made.append(pltpu.make_async_copy(source, scratch.at[pl.ds(start, self.rows), :], sems.at[len(made)]))
        return made

    def vectors(self, me, refs, held, sems):
        made = []
        for array, at, owner in self.gathered.blocks():
            source = refs[array].at[at, pl.ds(self.rows, 8), pl.ds(0, 512)]
            made.append(pltpu.make_async_copy(source, held.at[owner(me)], sems.at[len(made)]))
        return made

    def scratch(self):
        return [pltpu.VMEM(self.shape, BF16), pltpu.SemaphoreType.DMA((self.count,))]


def any_specs(count):
    return [pl.BlockSpec(memory_space=pl.ANY)] * count


def params():
    return pltpu.CompilerParams(dimension_semantics=("arbitrary",), vmem_limit_bytes=LIMIT)


def cost(flops, reads, exps=0):
    return pl.CostEstimate(flops=int(flops), transcendentals=int(exps), bytes_accessed=int(reads))


def row_spec(columns):
    return pl.BlockSpec((TILE, columns), lambda i, *_: (i, 0))


def whole_spec(shape):
    return pl.BlockSpec(shape, lambda i, *_: (0,) * len(shape))


def normed(values):
    center = values - jnp.mean(values, axis=-1, keepdims=True)
    scale = lax.rsqrt(jnp.mean(center * center, axis=-1, keepdims=True) + EPS)
    return center * scale, scale


def norm_back(grad, unit, scale, gain):
    scaled = grad * gain
    first = jnp.mean(scaled, axis=-1, keepdims=True)
    second = jnp.mean(scaled * unit, axis=-1, keepdims=True)
    return (scaled - first - unit * second) * scale


def load_first(weights, me, refs, scratches):
    @pl.when(pl.program_id(0) == 0)
    def _():
        started = []
        for weight, (scratch, sems) in zip(weights, scratches):
            started += weight.copies(me, refs, scratch, sems)
        for copy in started:
            copy.start()
        for copy in started:
            copy.wait()


def unpack(held_ref):
    total = None
    for at in range(8):
        row = held_ref[at][:, 0:128].astype(F32)
        row = jnp.concatenate([row, jnp.zeros((8, 640), F32)], axis=1)
        row = pltpu.roll(row, 96 * at, axis=1) if at else row
        total = row if total is None else total + row
    flat = [held_ref[at][0:1, 128:512].astype(F32) for at in range(8)]
    rows = [jnp.concatenate([flat[2 * at], flat[2 * at + 1]], axis=1) for at in range(4)]
    return jnp.concatenate([total] + rows + [jnp.zeros((4, 768), F32)], axis=0)


def joint_kernel(weight, packed, me_ref, x_ref, *refs):
    count = len(weight.arrays)
    if packed:
        arrays, (out_ref, hidden_ref, vec_ref, scratch, sems, held_ref, held_sems) = refs[:count], refs[count:]

        @pl.when(pl.program_id(0) == 0)
        def _():
            started = weight.vectors(me_ref[0], arrays, held_ref, held_sems)
            for copy in started:
                copy.start()
            load = weight.copies(me_ref[0], arrays, scratch, sems)
            for copy in load:
                copy.start()
            for copy in started:
                copy.wait()
            vec_ref[...] = unpack(held_ref)
            for copy in load:
                copy.wait()
    else:
        vec_ref, arrays, (out_ref, hidden_ref, scratch, sems) = refs[0], refs[1 : 1 + count], refs[1 + count :]
        load_first([weight], me_ref[0], arrays, [(scratch, sems)])
    unit, _ = normed(x_ref[...].astype(F32))
    hidden = (unit * vec_ref[0:1, :] + vec_ref[1:2, :]).astype(BF16)
    hidden_ref[...] = hidden
    bias = jnp.concatenate([vec_ref[2:3, :], jnp.zeros_like(vec_ref[2:3, :]), vec_ref[3:4, :]], axis=1)
    out_ref[...] = (mm(hidden, scratch[...]) + bias).astype(BF16)


def joint_forward(me, tokens, vectors, weight):
    rows, width = tokens.shape
    columns = weight.shape[1]
    packed = vectors is None
    out_specs = [row_spec(columns), row_spec(width)]
    out_shape = [jax.ShapeDtypeStruct((rows, columns), BF16), jax.ShapeDtypeStruct((rows, width), BF16)]
    scratch = weight.scratch()
    if packed:
        out_specs.append(whole_spec((16, width)))
        out_shape.append(jax.ShapeDtypeStruct((16, width), F32))
        scratch += [pltpu.VMEM((8, 8, 512), BF16), pltpu.SemaphoreType.DMA((8,))]
    outs = pl.pallas_call(
        functools.partial(joint_kernel, weight, packed),
        grid_spec=pltpu.PrefetchScalarGridSpec(
            num_scalar_prefetch=1,
            grid=(rows // TILE,),
            in_specs=[row_spec(width)] + ([] if packed else [whole_spec((16, width))]) + any_specs(len(weight.arrays)),
            out_specs=out_specs,
            scratch_shapes=scratch,
        ),
        out_shape=out_shape,
        compiler_params=params(),
        cost_estimate=cost(2 * rows * width * columns, 2 * (rows * (2 * width + columns) + width * columns)),
        name="joint_forward",
    )(me, tokens, *([] if packed else [vectors]), *weight.arrays)
    return outs if packed else (*outs, vectors)


def plan_groups(starts_ref, crops_ref, table_ref, bias_ref, rows):
    def one(state):
        at, start = state
        base = jnp.minimum((start // SNAP) * SNAP, rows - WIN)
        base = pl.multiple_of(base, SNAP)
        edge = base + WIN
        stop = jnp.where(edge >= rows, rows, starts_ref[jnp.minimum(edge, rows - 1)])
        table_ref[0, at] = base
        table_ref[1, at] = start
        down = crops_ref[pl.ds(base, WIN), :]
        across = down.T
        down = jnp.concatenate([down] * (WIN // 128), axis=1)
        across = jnp.concatenate([across] * (WIN // 128), axis=0)
        bias_ref[at] = jnp.where(down == across, 0.0, -1e30)
        return at + 1, stop

    more = lambda state: jnp.logical_and(state[1] < rows, state[0] < group_bound(rows))
    table_ref[2, 0] = lax.while_loop(more, one, (jnp.int32(0), jnp.int32(0)))[0]


def group_bound(rows):
    return 2 * (rows // (WIN - SNAP + 2)) + 2


def keep_from(ref, base, start, columns, value):
    window = (pl.ds(base, WIN), pl.ds(columns, PAIR))
    row = base + lax.broadcasted_iota(jnp.int32, (WIN, PAIR), 0)
    ref[window] = jnp.where(row >= start, value, ref[window].astype(F32)).astype(ref.dtype)


def attend_kernel(rows, starts_ref, crops_ref, query_ref, key_ref, value_ref, mixed_ref, log_ref, table_ref, bias_ref):
    @pl.when(pl.program_id(0) == 0)
    def _():
        plan_groups(starts_ref, crops_ref, table_ref, bias_ref, rows)

    lane = lax.broadcasted_iota(jnp.int32, (WIN, PAIR), 1)

    def one(at, carry):
        base = pl.multiple_of(table_ref[0, at], SNAP)
        start = table_ref[1, at]
        window = pl.ds(base, WIN)
        query = query_ref[window, :] * jnp.asarray(HD**-0.5, BF16)
        key = key_ref[window, :]
        value_t = value_ref[window, :].T
        outs = []
        for head in range(2):
            mine = (lane >= HD) if head else (lane < HD)
            scores = mm(jnp.where(mine, key, jnp.zeros_like(key)), query, NT) + bias_ref[at]
            top = jnp.max(scores, axis=0, keepdims=True)
            expo = jnp.exp(scores - top)
            total = jnp.sum(expo, axis=0, keepdims=True)
            mixed = mm(value_t[head * HD : (head + 1) * HD, :], expo.astype(BF16))
            outs.append(mixed * (1.0 / total))
            log_ref[0, at, pl.ds(head, 1), :] = top + jnp.log(total)
        keep_from(mixed_ref, base, start, 0, jnp.concatenate(outs, axis=0).T)
        return carry

    lax.fori_loop(0, table_ref[2, 0], one, 0)


def attend(starts, crops, joint, first, pairs):
    rows = joint.shape[0]
    columns = pairs * 3 * PAIR
    all_pairs = joint.shape[1] // (3 * PAIR)
    part = lambda at: pl.BlockSpec((rows, PAIR), lambda i, *_: (0, at * all_pairs + first + i))
    groups = group_bound(rows)
    return pl.pallas_call(
        functools.partial(attend_kernel, rows),
        grid_spec=pltpu.PrefetchScalarGridSpec(
            num_scalar_prefetch=1,
            grid=(pairs,),
            in_specs=[whole_spec((rows, 128)), part(0), part(1), part(2)],
            out_specs=[
                pl.BlockSpec((rows, PAIR), lambda i, *_: (0, i)),
                pl.BlockSpec((1, groups, 8, WIN), lambda i, *_: (i, 0, 0, 0)),
            ],
            scratch_shapes=[pltpu.SMEM((3, 16), jnp.int32), pltpu.VMEM((groups, WIN, WIN), F32)],
        ),
        out_shape=[
            jax.ShapeDtypeStruct((rows, pairs * PAIR), BF16),
            jax.ShapeDtypeStruct((pairs, groups, 8, WIN), F32),
        ],
        compiler_params=params(),
        cost_estimate=cost(pairs * 6 * 8 * WIN**3, 2 * rows * columns * 4 // 3, pairs * 12 * WIN * WIN),
        name="attend",
    )(starts, crops, joint, joint, joint)


def attend_back_kernel(
    rows,
    starts_ref,
    crops_ref,
    query_ref,
    key_ref,
    value_ref,
    mixed_ref,
    grad_ref,
    log_ref,
    out_ref,
    table_ref,
    bias_ref,
):
    @pl.when(pl.program_id(0) == 0)
    def _():
        plan_groups(starts_ref, crops_ref, table_ref, bias_ref, rows)

    lane = lax.broadcasted_iota(jnp.int32, (WIN, PAIR), 1)

    def one(at, carry):
        base = pl.multiple_of(table_ref[0, at], SNAP)
        start = table_ref[1, at]
        window = pl.ds(base, WIN)
        query = query_ref[window, :] * jnp.asarray(HD**-0.5, BF16)
        key = key_ref[window, :]
        value = value_ref[window, :]
        key_t = key.T
        grad = grad_ref[window, :]
        inner_t = (grad.astype(F32) * mixed_ref[window, :].astype(F32)).T
        d_query, d_key, d_value = [], [], []
        for head in range(2):
            mine = (lane >= HD) if head else (lane < HD)
            zero = jnp.zeros_like(key)
            scores = mm(jnp.where(mine, key, zero), query, NT) + bias_ref[at]
            weights = jnp.exp(scores - log_ref[0, at, pl.ds(head, 1), :])
            inner = jnp.sum(inner_t[head * HD : (head + 1) * HD, :], axis=0, keepdims=True)
            d_weights = mm(jnp.where(mine, value, zero), grad, NT)
            d_scores = (weights * (d_weights - inner)).astype(BF16)
            d_value.append(mm(weights.astype(BF16), grad))
            d_key.append(mm(d_scores, query))
            d_query.append(mm(key_t[head * HD : (head + 1) * HD, :], d_scores) * HD**-0.5)
        low = lane < HD
        keep_from(out_ref, base, start, 0, jnp.concatenate(d_query, axis=0).T)
        keep_from(out_ref, base, start, PAIR, jnp.where(low, d_key[0], d_key[1]))
        keep_from(out_ref, base, start, 2 * PAIR, jnp.where(low, d_value[0], d_value[1]))
        return carry

    lax.fori_loop(0, table_ref[2, 0], one, 0)


def attend_back(starts, crops, joint, mixed, grad, logs, first, count):
    rows = joint.shape[0]
    groups = group_bound(rows)
    far = lambda columns: pl.BlockSpec((rows, columns), lambda i, *_: (0, first + i))
    all_pairs = joint.shape[1] // (3 * PAIR)
    part = lambda at: pl.BlockSpec((rows, PAIR), lambda i, *_: (0, at * all_pairs + first + i))
    return pl.pallas_call(
        functools.partial(attend_back_kernel, rows),
        grid_spec=pltpu.PrefetchScalarGridSpec(
            num_scalar_prefetch=1,
            grid=(count,),
            in_specs=[
                whole_spec((rows, 128)),
                part(0),
                part(1),
                part(2),
                pl.BlockSpec((rows, PAIR), lambda i, *_: (0, i)),
                far(PAIR),
                pl.BlockSpec((1, groups, 8, WIN), lambda i, *_: (i, 0, 0, 0)),
            ],
            out_specs=pl.BlockSpec((rows, 3 * PAIR), lambda i, *_: (0, i)),
            scratch_shapes=[pltpu.SMEM((3, 16), jnp.int32), pltpu.VMEM((groups, WIN, WIN), F32)],
        ),
        out_shape=jax.ShapeDtypeStruct((rows, count * 3 * PAIR), BF16),
        compiler_params=params(),
        cost_estimate=cost(count * 6 * 20 * WIN**3, 2 * rows * count * 8 * PAIR, count * 12 * WIN * WIN),
        name="attend_back",
    )(starts, crops, joint, joint, joint, mixed, grad, logs)


def up_kernel(out_weight, up_weight, me_ref, x_ref, mixed_a_ref, mixed_b_ref, vec_ref, *refs):
    count = len(out_weight.arrays)
    middle_ref, hidden_ref, active_ref, slope_ref, out_s, out_sem, up_s, up_sem = refs[count:]
    load_first([out_weight, up_weight], me_ref[0], refs[:count], [(out_s, out_sem), (up_s, up_sem)])
    mixed = jnp.concatenate([mixed_a_ref[...], mixed_b_ref[...]], axis=1)
    middle = x_ref[...].astype(F32) + mm(mixed, out_s[...]) + vec_ref[4:5, :]
    middle_ref[...] = middle
    unit, _ = normed(middle)
    hidden = (unit * vec_ref[5:6, :] + vec_ref[6:7, :]).astype(BF16)
    hidden_ref[...] = hidden
    chunk = vec_ref.shape[1]
    for at in range(up_weight.shape[1] // chunk):
        part = pl.ds(at * chunk, chunk)
        value = mm(hidden, up_s[:, part]) + vec_ref[8 + at : 9 + at, :]
        below = 0.5 + 0.5 * lax.erf(value * (0.5**0.5))
        active_ref[:, part] = (value * below).astype(BF16)
        bell = jnp.exp(value * value * -0.5) * 0.3989422804014327
        slope_ref[:, part] = (below + value * bell).astype(BF16)


def up_forward(me, tokens, mixed_a, mixed_b, vectors, out_weight, up_weight):
    rows, width = tokens.shape
    inner = up_weight.shape[1]
    arrays = out_weight.arrays
    return pl.pallas_call(
        functools.partial(up_kernel, out_weight, up_weight),
        grid_spec=pltpu.PrefetchScalarGridSpec(
            num_scalar_prefetch=1,
            grid=(rows // TILE,),
            in_specs=[row_spec(width), row_spec(width // 2), row_spec(width // 2), whole_spec(vectors.shape)]
            + any_specs(len(arrays)),
            out_specs=[row_spec(width), row_spec(width), row_spec(inner), row_spec(inner)],
            scratch_shapes=out_weight.scratch() + up_weight.scratch(),
        ),
        out_shape=[
            jax.ShapeDtypeStruct((rows, width), F32),
            jax.ShapeDtypeStruct((rows, width), BF16),
            jax.ShapeDtypeStruct((rows, inner), BF16),
            jax.ShapeDtypeStruct((rows, inner), BF16),
        ],
        compiler_params=params(),
        cost_estimate=cost(2 * rows * width * (width + inner), rows * (10 * width + 4 * inner) + 2 * width * inner, rows * inner * 2),
        name="up_forward",
    )(me, tokens, mixed_a, mixed_b, vectors, *arrays)


def slope_kernel(down_weight, me_ref, grad_ref, slope_ref, *refs):
    count = len(down_weight.arrays)
    ga_ref, sums_ref, upsum_ref, down_s, down_sem = refs[count:]
    load_first([down_weight], me_ref[0], refs[:count], [(down_s, down_sem)])

    @pl.when(pl.program_id(0) == 0)
    def _():
        sums_ref[...] = jnp.zeros_like(sums_ref)
        upsum_ref[...] = jnp.zeros_like(upsum_ref)

    grad = grad_ref[...]
    sums_ref[...] += fold(grad.astype(F32))
    for at in range(0, down_weight.shape[0], CHUNK):
        part = pl.ds(at, CHUNK)
        inner = (mm(grad, down_s[part, :], NT) * slope_ref[:, part].astype(F32)).astype(BF16)
        ga_ref[:, part] = inner
        upsum_ref[:, part] += fold(inner.astype(F32))


def slope_back(me, grad, slope, down_weight):
    rows, width = grad.shape
    inner = slope.shape[1]
    return pl.pallas_call(
        functools.partial(slope_kernel, down_weight),
        grid_spec=pltpu.PrefetchScalarGridSpec(
            num_scalar_prefetch=1,
            grid=(rows // TILE,),
            in_specs=[row_spec(width), row_spec(inner)] + any_specs(len(down_weight.arrays)),
            out_specs=[row_spec(inner), whole_spec((8, width)), whole_spec((8, inner))],
            scratch_shapes=down_weight.scratch(),
        ),
        out_shape=[
            jax.ShapeDtypeStruct((rows, inner), BF16),
            jax.ShapeDtypeStruct((8, width), F32),
            jax.ShapeDtypeStruct((8, inner), F32),
        ],
        compiler_params=params(),
        cost_estimate=cost(2 * rows * width * inner, rows * (2 * width + 4 * inner) + 2 * width * inner),
        name="slope_back",
    )(me, grad, slope, *down_weight.arrays)


def middle_kernel(out_weight, up_weight, me_ref, middle_ref, grad_ref, ga_ref, vec_ref, *refs):
    count = len(up_weight.arrays)
    gmid_ref, glow_ref, gmix_ref, sums_ref, out_s, out_sem, up_s, up_sem = refs[count:]
    load_first([out_weight, up_weight], me_ref[0], refs[:count], [(out_s, out_sem), (up_s, up_sem)])

    @pl.when(pl.program_id(0) == 0)
    def _():
        sums_ref[...] = jnp.zeros_like(sums_ref)

    total = mm(ga_ref[...], up_s[...], NT)
    unit, scale = normed(middle_ref[...])
    sums_ref[0] += fold(total * unit)
    sums_ref[1] += fold(total)
    gmid = grad_ref[...].astype(F32) + norm_back(total, unit, scale, vec_ref[5:6, :])
    gmid_ref[...] = gmid
    low = gmid.astype(BF16)
    glow_ref[...] = low
    sums_ref[2] += fold(low.astype(F32))
    gmix_ref[...] = mm(low, out_s[...], NT).astype(BF16)


def middle_back(me, middle, grad, ga, vectors, out_weight, up_weight):
    rows, width = middle.shape
    inner = ga.shape[1]
    return pl.pallas_call(
        functools.partial(middle_kernel, out_weight, up_weight),
        grid_spec=pltpu.PrefetchScalarGridSpec(
            num_scalar_prefetch=1,
            grid=(rows // TILE,),
            in_specs=[row_spec(width), row_spec(width), row_spec(inner), whole_spec(vectors.shape)]
            + any_specs(len(up_weight.arrays)),
            out_specs=[row_spec(width), row_spec(width), row_spec(width), whole_spec((3, 8, width))],
            scratch_shapes=out_weight.scratch() + up_weight.scratch(),
        ),
        out_shape=[
            jax.ShapeDtypeStruct((rows, width), F32),
            jax.ShapeDtypeStruct((rows, width), BF16),
            jax.ShapeDtypeStruct((rows, width), BF16),
            jax.ShapeDtypeStruct((3, 8, width), F32),
        ],
        compiler_params=params(),
        cost_estimate=cost(2 * rows * width * (width + inner), rows * (14 * width + 2 * inner) + 2 * width * inner),
        name="middle_back",
    )(me, middle, grad, ga, vectors, *up_weight.arrays)


def down_kernel(down_weight, me_ref, middle_ref, active_ref, vec_ref, *refs):
    count = len(down_weight.arrays)
    acts_ref, down_s, down_sem = refs[count:]
    load_first([down_weight], me_ref[0], refs[:count], [(down_s, down_sem)])
    acts_ref[...] = middle_ref[...] + mm(active_ref[...], down_s[...]) + vec_ref[7:8, :]


def down_forward(me, middle, active, vectors, down_weight):
    rows, width = middle.shape
    inner = active.shape[1]
    return pl.pallas_call(
        functools.partial(down_kernel, down_weight),
        grid_spec=pltpu.PrefetchScalarGridSpec(
            num_scalar_prefetch=1,
            grid=(rows // TILE,),
            in_specs=[row_spec(width), row_spec(inner), whole_spec(vectors.shape)] + any_specs(len(down_weight.arrays)),
            out_specs=row_spec(width),
            scratch_shapes=down_weight.scratch(),
        ),
        out_shape=jax.ShapeDtypeStruct((rows, width), F32),
        compiler_params=params(),
        cost_estimate=cost(2 * rows * width * inner, rows * (8 * width + 2 * inner) + 2 * width * inner),
        name="down_forward",
    )(me, middle, active, vectors, *down_weight.arrays)


def first_kernel(
    weight, me_ref, x_ref, gmid_ref, part_a_ref, part_b_ref, vec_ref, cot_ref, mid_ref, up_ref, *refs
):
    count = len(weight.arrays)
    out_ref, rows_ref, sums_ref, joint_sum_ref, scratch, sems = refs[count:]
    load_first([weight], me_ref[0], refs[:count], [(scratch, sems)])

    @pl.when(pl.program_id(0) == 0)
    def _():
        sums_ref[...] = jnp.zeros_like(sums_ref)
        joint_sum_ref[...] = jnp.zeros_like(joint_sum_ref)

    halves = [part_a_ref, part_b_ref]
    pairs = part_a_ref.shape[1] // (3 * PAIR)
    blocks = [
        half[:, (3 * pair + part) * PAIR : (3 * pair + part + 1) * PAIR]
        for part in range(3)
        for half in halves
        for pair in range(pairs)
    ]
    grad = jnp.concatenate(blocks, axis=1)
    joint_sum_ref[...] += fold(grad.astype(F32))
    total = mm(grad, scratch[...], NT)
    unit, scale = normed(x_ref[...].astype(F32))
    sums_ref[0] += fold(total * unit)
    sums_ref[1] += fold(total)
    out_ref[...] = gmid_ref[...] + norm_back(total, unit, scale, vec_ref[0:1, :])

    @pl.when(pl.program_id(0) == pl.num_programs(0) - 1)
    def _():
        width = x_ref.shape[1]
        line = lambda value: jnp.sum(value, axis=0, keepdims=True)
        wide = [line(up_ref[:, at : at + width]) for at in range(0, up_ref.shape[1], width)]
        rows_ref[...] = jnp.concatenate(
            [
                line(sums_ref[0]),
                line(sums_ref[1]),
                line(joint_sum_ref[:, :width]),
                line(joint_sum_ref[:, 2 * width :]),
                line(mid_ref[2]),
                line(mid_ref[0]),
                line(mid_ref[1]),
                line(cot_ref[...]),
            ]
            + wide
            + [jnp.zeros((8 - len(wide), width), F32)],
            axis=0,
        )


def first_back(me, tokens, gmid, part_a, part_b, vectors, cot_sums, mid_sums, up_sums, weight):
    rows, width = tokens.shape
    columns = weight.shape[1]
    return pl.pallas_call(
        functools.partial(first_kernel, weight),
        grid_spec=pltpu.PrefetchScalarGridSpec(
            num_scalar_prefetch=1,
            grid=(rows // TILE,),
            in_specs=[row_spec(width), row_spec(width), row_spec(columns // 2), row_spec(columns // 2)]
            + [whole_spec(array.shape) for array in (vectors, cot_sums, mid_sums, up_sums)]
            + any_specs(len(weight.arrays)),
            out_specs=[row_spec(width), whole_spec((16, width))],
            scratch_shapes=[pltpu.VMEM((2, 8, width), F32), pltpu.VMEM((8, columns), F32)] + weight.scratch(),
        ),
        out_shape=[jax.ShapeDtypeStruct((rows, width), F32), jax.ShapeDtypeStruct((16, width), F32)],
        compiler_params=params(),
        cost_estimate=cost(2 * rows * width * columns, rows * (10 * width + 2 * columns) + 2 * width * columns),
        name="first_back",
    )(me, tokens, gmid, part_a, part_b, vectors, cot_sums, mid_sums, up_sums, *weight.arrays)


def own_rows_kernel(me_ref, left_ref, right_ref, gain_a, shift_a, joint_b, out_b, gain_b, shift_b, down_b, up_b):
    me = me_ref[0]
    own = gain_a.shape[0]
    total = left_ref[0:8, :] + right_ref[0:8, :]
    mine = pltpu.roll(total, lax.rem(8 - me, 8) * own, axis=1)[:, :own]
    for at, ref in enumerate((gain_a, shift_a, None, None, out_b, gain_b, shift_b, down_b)):
        if ref is not None:
            ref[...] = mine[at]
    joint_b[...] = mine[2:4]
    line = 8 + (me >> 1)
    row = left_ref[pl.ds(line, 1), :] + right_ref[pl.ds(line, 1), :]
    half = up_b.shape[0]
    up_b[...] = jnp.where((me & 1) == 1, row[:, half:], row[:, :half])[0]


def own_rows(me, left, right):
    own = left.shape[1] // 8
    vector = jax.ShapeDtypeStruct((own,), F32)
    out_shape = [vector, vector, jax.ShapeDtypeStruct((2, own), F32), vector, vector, vector, vector]
    out_shape.append(jax.ShapeDtypeStruct((4 * own,), F32))
    return pl.pallas_call(
        own_rows_kernel,
        grid_spec=pltpu.PrefetchScalarGridSpec(
            num_scalar_prefetch=1,
            grid=(1,),
            in_specs=[whole_spec(left.shape), whole_spec(right.shape)],
            out_specs=[whole_spec(shape.shape) for shape in out_shape],
        ),
        out_shape=out_shape,
        compiler_params=params(),
        name="own_rows",
    )(me, left, right)


def weight_grad(left, right):
    return lax.dot_general(left, right, (((0,), (0,)), ((), ())), preferred_element_type=F32).astype(BF16)


def on_device(
    fsdp,
    dp,
    tokens,
    crop_ids,
    gain_first,
    shift_first,
    joint_weight,
    joint_bias,
    output_weight,
    output_bias,
    gain_second,
    shift_second,
    up_weight,
    up_bias,
    down_weight,
    down_bias,
    cotangent,
):
    rows, width = tokens.shape
    inner = up_bias.shape[0] * fsdp
    joint_width = joint_weight.shape[1]
    rank = lax.axis_index("fsdp")
    me = rank.astype(jnp.int32).reshape(1)
    own = width // fsdp
    own_up = inner // fsdp

    eight = fsdp == 8
    if eight:
        lines = [gain_first, shift_first, joint_bias[0], joint_bias[1], output_bias, gain_second, shift_second, down_bias]
        first_in = jnp.pad(joint_weight, ((0, 8), (0, 0)))
        for at, line in enumerate(lines):
            first_in += jnp.pad(line[None], ((own + at, 7 - at), (0, joint_width - own)))
        first_in += jnp.pad(up_bias[None], ((own, 7), (128, joint_width - 128 - own_up)))
        vectors = None
    else:
        first_in = joint_weight
        pack = [gain_first, shift_first, joint_bias[0], joint_bias[1], output_bias, gain_second, shift_second, down_bias]
        pack = [lax.all_gather(line.astype(BF16), "fsdp", axis=0, tiled=True) for line in pack + [up_bias]]
        vectors = jnp.concatenate([jnp.stack(pack[:8]), pack[8].reshape(-1, width)], axis=0).astype(F32)
        vectors = jnp.pad(vectors, ((0, 16 - vectors.shape[0]), (0, 0)))
    outer = jnp.concatenate([output_weight, up_weight], axis=1)
    deep = own_up // own if eight else 1
    lower = jnp.concatenate([down_weight[at * own : (at + 1) * own] for at in range(deep)], axis=1) if eight else down_weight

    starts = jnp.sum((crop_ids[None, :] < crop_ids[:, None]).astype(jnp.int32), axis=1)
    crops = jnp.broadcast_to(crop_ids.astype(F32)[:, None], (rows, 128))

    pairs = joint_width // (3 * PAIR)
    near = pairs // 2
    group = Gather(first_in, fsdp)
    source = tokens
    if eight:
        group.first()
        group.second()
        group.third()
        outer_group = Gather(after(outer, group.more), fsdp)
        outer_group.first()
        source = after(source, outer_group.shard, starts, crops)
    else:
        group.whole()
        outer_group = Gather(outer, fsdp).whole()
        lower_group = Gather(lower, fsdp).whole()
    joint_full = Weight(group, 0, joint_width, spare=8 if eight else 0)
    joint, hidden_first, vectors = joint_forward(me, source, vectors, joint_full)
    read = joint
    if eight:
        outer_group.two = after(outer_group.two, joint)
        outer_group.second()
        read = after(joint, outer_group.two)
    mixed_a, logs_a = attend(starts, crops, read, 0, near)
    if eight:
        lower_group = Gather(after(lower, mixed_a), fsdp)
        lower_group.first()
        read = after(joint, lower_group.shard)
    mixed_b, logs_b = attend(starts, crops, read, near, pairs - near)
    source = tokens
    if eight:
        outer_group.more = after(outer_group.more, mixed_b)
        outer_group.third()
        lower_group.two = after(lower_group.two, mixed_b)
        lower_group.second()
        source = after(source, lower_group.two)
    out_full = Weight(outer_group, 0, width)
    up_full = Weight(outer_group, width, inner)
    middle, hidden_second, active, slope = up_forward(me, source, mixed_a, mixed_b, vectors, out_full, up_full)
    grad = cotangent
    if eight:
        lower_group.more = after(lower_group.more, middle)
        lower_group.third()
        grad = after(grad, lower_group.more)
    down_full = Weight(lower_group, 0, width, deep)

    start = lambda slabs, short=False: Grad(slabs, fsdp, dp, short)
    behind = lambda value, *grads: after(value, *[g for g in grads if g is not None])

    down_grad = start(weight_grad(active, grad).reshape(fsdp, own_up, width), True)
    grad_up, cotangent_sums, up_sums = slope_back(me, behind(cotangent, down_grad.step()), slope, down_full)
    sent = down_grad.step(grad_up)
    up_grad = start(weight_grad(behind(hidden_second, sent), grad_up).reshape(fsdp, own, inner))
    grad_middle, grad_low, grad_mixed, sums = middle_back(
        me, middle, cotangent, behind(grad_up, up_grad.step()), vectors, out_full, up_full
    )
    sent = [down_grad.step(grad_low), up_grad.step(grad_low)]
    grad_a = attend_back(starts, crops, joint, mixed_a, behind(grad_mixed, *sent), logs_a, 0, near)
    sent = [down_grad.step(grad_a), up_grad.step(grad_a)]
    low = behind(grad_low, *sent)
    out_slabs = jnp.concatenate([weight_grad(mixed_a, low), weight_grad(mixed_b, low)], axis=0).reshape(fsdp, own, width)
    slabs_a = weight_grad(behind(hidden_first, *sent), grad_a).reshape(fsdp, own, -1)
    mixed_grad = start(jnp.concatenate([out_slabs, slabs_a], axis=2))
    sent = mixed_grad.step()
    grad_b = attend_back(starts, crops, joint, mixed_b, behind(grad_mixed, sent), logs_b, near, pairs - near)
    sent = [down_grad.step(grad_b), up_grad.step(grad_b), mixed_grad.step(grad_b)]
    last_grad = start(weight_grad(behind(hidden_first, *sent), grad_b).reshape(fsdp, own, -1), True)
    input_grad, total = first_back(
        me,
        behind(tokens, last_grad.step()),
        grad_middle,
        grad_a,
        grad_b,
        vectors,
        cotangent_sums,
        sums,
        up_sums,
        joint_full,
    )
    sent = [last_grad.step(total), mixed_grad.step(total), up_grad.step(total)]
    if eight and dp == 4:
        other = send(total, CORE)
        acts = down_forward(me, behind(middle, *sent), active, vectors, down_full)
        total = total + other
        for bit in (2, 4):
            total = total + send(total, [(i, i ^ bit) for i in range(8)])
        total = total + send_dp(total, 1)
        vecs = own_rows(me, total, send_dp(total, 2))
    else:
        acts = down_forward(me, behind(middle, *sent), active, vectors, down_full)
        total = lax.psum(total, ("fsdp", "dp"))
        vecs = [lax.dynamic_slice_in_dim(total[at], rank * own, own) for at in range(8)]
        vecs.append(lax.dynamic_slice_in_dim(total[8:].reshape(-1), rank * own_up, own_up))
        vecs = vecs[:2] + [jnp.stack(vecs[2:4])] + vecs[4:]
    last = last_grad.result()
    mixed_out = mixed_grad.result()
    wide_grads = [mixed_out[:, width:], last]
    grad_joint = jnp.concatenate(
        [
            half[:, (3 * pair + part) * PAIR : (3 * pair + part + 1) * PAIR]
            for part in range(3)
            for half in wide_grads
            for pair in range(half.shape[1] // (3 * PAIR))
        ],
        axis=1,
    )
    gain_a, shift_a, joint_b, out_b, gain_b, shift_b, down_b, up_b = vecs
    return (
        acts,
        input_grad,
        gain_a,
        shift_a,
        grad_joint,
        joint_b,
        mixed_out[:, :width],
        out_b,
        gain_b,
        shift_b,
        up_grad.result(),
        up_b,
        down_grad.result(),
        down_b,
    )


def solution(mesh):
    rows, line, flat = P(("fsdp", "dp"), None), P("fsdp"), P("fsdp", None)
    both = P(None, "fsdp")
    return jax.shard_map(
        functools.partial(on_device, mesh.shape["fsdp"], mesh.shape["dp"]),
        mesh=mesh,
        in_specs=(rows, P(("fsdp", "dp")), line, line, flat, both, flat, line, line, line, flat, line, flat, line, rows),
        out_specs=(rows, rows, line, line, flat, both, flat, line, line, line, flat, line, flat, line),
        check_vma=False,
    )
```

```python
import functools

import jax
import jax.numpy as jnp
from jax import lax
from jax.experimental import pallas as pl
from jax.experimental.pallas import tpu as pltpu
from jax.sharding import PartitionSpec as P

HD = 64
PAIR = 2 * HD
EPS = 1e-06
WIN = 256
SNAP = 16
TILE = 256
CHUNK = 512
LIMIT = 58 << 20
F32 = jnp.float32
BF16 = jnp.bfloat16
NT = (((1,), (1,)), ((), ()))
NN = (((1,), (0,)), ((), ()))


def mm(left, right, dims=NN):
    return lax.dot_general(left, right, dims, preferred_element_type=F32)


def fold(values):
    return jnp.sum(values.reshape(values.shape[0] // 8, 8, values.shape[1]), axis=0)


CORE = [(i, i ^ 1) for i in range(8)]
FIRST = [(i, i ^ (4 if i & 1 else 2)) for i in range(8)]
SECOND = [(i, i ^ (2 if i & 1 else 4)) for i in range(8)]


def send(value, pairs):
    return lax.ppermute(value, "fsdp", pairs)


def send_dp(value, bit):
    return lax.ppermute(value, "dp", [(i, i ^ bit) for i in range(4)])


def after(value, *others):
    return lax.optimization_barrier((value,) + others)[0]


def pick(value, at, axis=0):
    return lax.dynamic_index_in_dim(value, at, axis, keepdims=False)


def wide(value):
    return value.astype(F32)


class Scatter:
    def __init__(self, slabs):
        me = lax.axis_index("fsdp")
        self.core = me & 1
        at_x, at_y = (me >> 1) & 1, me >> 2
        rows, columns = slabs.shape[1:]
        self.slabs = slabs.reshape(4, 2, rows, columns)
        even = self.core == 0
        keep, leave = 1 - at_y, 1 - at_x
        self.away = (jnp.where(even, 2 * keep, leave), jnp.where(even, 2 * keep + 1, 2 + leave))
        self.near = jnp.where(even, at_x, at_y)
        self.chip = 2 * at_y + at_x
        self.next_chip = jnp.where(even, 2 * at_y + 1 - at_x, 2 * (1 - at_y) + at_x)
        self.mine = pick(self.slabs, self.core, 1)
        self.got = []

    def give(self):
        if not self.got:
            return pick(self.slabs, 1 - self.core, 1)
        if len(self.got) == 1:
            return jnp.stack([wide(pick(self.mine, at)) + wide(pick(self.got[0], at)) for at in self.away]).astype(BF16)
        total = wide(pick(self.mine, self.next_chip)) + wide(pick(self.got[0], self.next_chip))
        return (total + wide(pick(self.got[1], 1 - self.near))).astype(BF16)

    def take(self, value):
        self.got.append(value)

    def pairs(self):
        return (CORE, SECOND, FIRST)[len(self.got)]

    def result(self):
        total = wide(pick(self.mine, self.chip)) + wide(pick(self.got[0], self.chip))
        return (total + wide(pick(self.got[1], self.near)) + wide(self.got[2])).astype(BF16)


class Sum:
    def __init__(self, value, short=False):
        me = lax.axis_index("dp")
        self.low, self.high = me & 1, me >> 1
        self.value = value
        self.short = short
        self.got = []
        self.split()

    def split(self):
        rows, columns = self.value.shape
        self.halves = self.value.reshape(2, rows // 2, columns)

    def half(self):
        return wide(pick(self.halves, self.low)) + wide(self.got[0])

    def quarters(self):
        half = self.half()
        return half.reshape(2, half.shape[0] // 2, half.shape[1])

    def own(self):
        return (pick(self.quarters(), self.high) + wide(self.got[1])).astype(BF16)

    def join(self, mine, other, bit):
        return jnp.concatenate([jnp.where(bit == 0, mine, other), jnp.where(bit == 0, other, mine)], axis=0)

    def give(self):
        step = len(self.got)
        if self.short:
            return self.value.astype(BF16) if step == 0 else (wide(self.value) + wide(self.got[0])).astype(BF16)
        if step == 0:
            return pick(self.halves, 1 - self.low).astype(BF16)
        if step == 1:
            return pick(self.quarters(), 1 - self.high).astype(BF16)
        if step == 2:
            return self.own()
        return self.join(self.own(), self.got[2], self.high)

    def bit(self):
        return ((1, 2) if self.short else (1, 2, 2, 1))[len(self.got)]

    def take(self, value):
        self.got.append(value)

    def result(self):
        if self.short:
            return wide(self.value) + wide(self.got[0]) + wide(self.got[1])
        half = self.join(self.own(), self.got[2], self.high)
        return wide(self.join(half, self.got[3], self.low))


class Grad:
    def __init__(self, slabs, fsdp, dp, short=False, scattered=False):
        self.dp, self.short = dp, short
        self.sum = self.scatter = self.more = None
        if scattered:
            self.enter(slabs)
        elif fsdp == 8:
            self.scatter = Scatter(slabs)
        else:
            self.enter(lax.psum_scatter(slabs, "fsdp", scatter_dimension=0, tiled=True)[0])

    def enter(self, value):
        if self.dp == 4:
            self.sum = Sum(value, self.short)
        else:
            self.out = lax.psum(value, "dp").astype(F32)

    def step(self, *behind):
        stage = self.scatter if self.scatter is not None else self.sum
        if stage is None or (stage is self.sum and len(stage.got) == (2 if self.short else 4)):
            return None
        if behind and stage.got:
            stage.got[-1] = after(stage.got[-1], *behind)
        elif behind and stage is self.sum:
            stage.value = after(stage.value, *behind)
            stage.split()
        given = stage.give()
        if stage is self.sum:
            stage.take(send_dp(given, stage.bit()))
            return given
        stage.take(send(given, stage.pairs()))
        if len(stage.got) == 3:
            self.scatter = None
            value = stage.result()
            self.enter(value if self.more is None else jnp.concatenate([value, self.more], axis=1))
        return given

    def hold(self, *behind):
        stage = self.scatter if self.scatter is not None else self.sum
        if stage.got:
            stage.got[-1] = after(stage.got[-1], *behind)
        else:
            stage.value = after(stage.value, *behind)
            stage.split()

    def result(self):
        while self.step() is not None:
            pass
        return self.sum.result() if self.sum is not None else self.out


class Gather:
    def __init__(self, shard, fsdp):
        self.fsdp = fsdp
        self.shard = shard

    def whole(self):
        self.fsdp = 1
        self.arrays = [lax.all_gather(self.shard, "fsdp", axis=0, tiled=True)]
        return self

    def first(self):
        self.two = jnp.stack([self.shard, send(self.shard, FIRST)])
        return self.two

    def second(self):
        self.more = send(self.two, SECOND)
        self.swapped = send(self.two, CORE)
        return self.more

    def third(self):
        self.arrays = [self.two, self.more, self.swapped, send(self.more, CORE)]
        return self.arrays[-1]

    def blocks(self):
        def owner(theirs, far, at):
            def of(me):
                base = me ^ 1 if theirs else me
                one, two = 2 + 2 * (base & 1), 4 - 2 * (base & 1)
                return base ^ ((two if far else 0) + (one if at else 0))

            return of

        return [(a, at, owner(a >= 2, a % 2 == 1, at)) for a in range(4) for at in range(2)]


class Weight:
    def __init__(self, gathered, first, columns, deep=1, spare=0):
        self.gathered, self.first, self.columns, self.deep = gathered, first, columns, deep
        self.arrays = gathered.arrays
        self.rows = gathered.shard.shape[0] - spare
        self.shape = (self.rows * deep * 8 if gathered.fsdp == 8 else self.arrays[0].shape[0], columns)
        self.count = deep * 8 if gathered.fsdp == 8 else 1

    def copies(self, me, refs, scratch, sems):
        if self.gathered.fsdp != 8:
            source = refs[0].at[:, pl.ds(self.first, self.columns)]
            return [pltpu.make_async_copy(source, scratch, sems.at[0])]
        made = []
        for array, at, owner in self.gathered.blocks():
            for part in range(self.deep):
                start = pl.multiple_of((owner(me) * self.deep + part) * self.rows, 16)
                source = refs[array].at[at, pl.ds(0, self.rows), pl.ds(self.first + part * self.columns, self.columns)]
                made.append(pltpu.make_async_copy(source, scratch.at[pl.ds(start, self.rows), :], sems.at[len(made)]))
        return made

    def vectors(self, me, refs, held, sems):
        made = []
        for array, at, owner in self.gathered.blocks():
            source = refs[array].at[at, pl.ds(self.rows, 8), pl.ds(0, 512)]
            made.append(pltpu.make_async_copy(source, held.at[owner(me)], sems.at[len(made)]))
        return made

    def scratch(self):
        return [pltpu.VMEM(self.shape, BF16), pltpu.SemaphoreType.DMA((self.count,))]


def any_specs(count):
    return [pl.BlockSpec(memory_space=pl.ANY)] * count


def params():
    return pltpu.CompilerParams(dimension_semantics=("arbitrary",), vmem_limit_bytes=LIMIT)


def cost(flops, reads, exps=0):
    return pl.CostEstimate(flops=int(flops), transcendentals=int(exps), bytes_accessed=int(reads))


def row_spec(columns):
    return pl.BlockSpec((TILE, columns), lambda i, *_: (i, 0))


def whole_spec(shape):
    return pl.BlockSpec(shape, lambda i, *_: (0,) * len(shape))


def normed(values):
    center = values - jnp.mean(values, axis=-1, keepdims=True)
    scale = lax.rsqrt(jnp.mean(center * center, axis=-1, keepdims=True) + EPS)
    return center * scale, scale


def norm_back(grad, unit, scale, gain):
    scaled = grad * gain
    first = jnp.mean(scaled, axis=-1, keepdims=True)
    second = jnp.mean(scaled * unit, axis=-1, keepdims=True)
    return (scaled - first - unit * second) * scale


def load_first(weights, me, refs, scratches):
    @pl.when(pl.program_id(0) == 0)
    def _():
        started = []
        for weight, (scratch, sems) in zip(weights, scratches):
            started += weight.copies(me, refs, scratch, sems)
        for copy in started:
            copy.start()
        for copy in started:
            copy.wait()


def unpack(held_ref):
    total = None
    for at in range(8):
        row = held_ref[at][:, 0:128].astype(F32)
        row = jnp.concatenate([row, jnp.zeros((8, 640), F32)], axis=1)
        row = pltpu.roll(row, 96 * at, axis=1) if at else row
        total = row if total is None else total + row
    flat = [held_ref[at][0:1, 128:512].astype(F32) for at in range(8)]
    rows = [jnp.concatenate([flat[2 * at], flat[2 * at + 1]], axis=1) for at in range(4)]
    return jnp.concatenate([total] + rows + [jnp.zeros((4, 768), F32)], axis=0)


def joint_kernel(weight, packed, me_ref, x_ref, *refs):
    count = len(weight.arrays)
    if packed:
        arrays, (out_ref, hidden_ref, vec_ref, scratch, sems, held_ref, held_sems) = refs[:count], refs[count:]

        @pl.when(pl.program_id(0) == 0)
        def _():
            started = weight.vectors(me_ref[0], arrays, held_ref, held_sems)
            for copy in started:
                copy.start()
            load = weight.copies(me_ref[0], arrays, scratch, sems)
            for copy in load:
                copy.start()
            for copy in started:
                copy.wait()
            vec_ref[...] = unpack(held_ref)
            for copy in load:
                copy.wait()
    else:
        vec_ref, arrays, (out_ref, hidden_ref, scratch, sems) = refs[0], refs[1 : 1 + count], refs[1 + count :]
        load_first([weight], me_ref[0], arrays, [(scratch, sems)])
    unit, _ = normed(x_ref[...].astype(F32))
    hidden = (unit * vec_ref[0:1, :] + vec_ref[1:2, :]).astype(BF16)
    hidden_ref[...] = hidden
    bias = jnp.concatenate([vec_ref[2:3, :], jnp.zeros_like(vec_ref[2:3, :]), vec_ref[3:4, :]], axis=1)
    out_ref[...] = (mm(hidden, scratch[...]) + bias).astype(BF16)


def joint_forward(me, tokens, vectors, weight):
    rows, width = tokens.shape
    columns = weight.shape[1]
    packed = vectors is None
    out_specs = [row_spec(columns), row_spec(width)]
    out_shape = [jax.ShapeDtypeStruct((rows, columns), BF16), jax.ShapeDtypeStruct((rows, width), BF16)]
    scratch = weight.scratch()
    if packed:
        out_specs.append(whole_spec((16, width)))
        out_shape.append(jax.ShapeDtypeStruct((16, width), F32))
        scratch += [pltpu.VMEM((8, 8, 512), BF16), pltpu.SemaphoreType.DMA((8,))]
    outs = pl.pallas_call(
        functools.partial(joint_kernel, weight, packed),
        grid_spec=pltpu.PrefetchScalarGridSpec(
            num_scalar_prefetch=1,
            grid=(rows // TILE,),
            in_specs=[row_spec(width)] + ([] if packed else [whole_spec((16, width))]) + any_specs(len(weight.arrays)),
            out_specs=out_specs,
            scratch_shapes=scratch,
        ),
        out_shape=out_shape,
        compiler_params=params(),
        cost_estimate=cost(2 * rows * width * columns, 2 * (rows * (2 * width + columns) + width * columns)),
        name="joint_forward",
    )(me, tokens, *([] if packed else [vectors]), *weight.arrays)
    return outs if packed else (*outs, vectors)


def plan_groups(starts_ref, crops_ref, table_ref, bias_ref, rows):
    def one(state):
        at, start = state
        base = jnp.minimum((start // SNAP) * SNAP, rows - WIN)
        base = pl.multiple_of(base, SNAP)
        edge = base + WIN
        stop = jnp.where(edge >= rows, rows, starts_ref[jnp.minimum(edge, rows - 1)])
        table_ref[0, at] = base
        table_ref[1, at] = start
        down = crops_ref[pl.ds(base, WIN), :]
        across = down.T
        down = jnp.concatenate([down] * (WIN // 128), axis=1)
        across = jnp.concatenate([across] * (WIN // 128), axis=0)
        bias_ref[at] = jnp.where(down == across, 0.0, -1e30)
        return at + 1, stop

    more = lambda state: jnp.logical_and(state[1] < rows, state[0] < group_bound(rows))
    table_ref[2, 0] = lax.while_loop(more, one, (jnp.int32(0), jnp.int32(0)))[0]


def group_bound(rows):
    return 2 * (rows // (WIN - SNAP + 2)) + 2


def keep_from(ref, base, start, columns, value):
    window = (pl.ds(base, WIN), pl.ds(columns, PAIR))
    row = base + lax.broadcasted_iota(jnp.int32, (WIN, PAIR), 0)
    ref[window] = jnp.where(row >= start, value, ref[window].astype(F32)).astype(ref.dtype)


def attend_kernel(rows, starts_ref, crops_ref, query_ref, key_ref, value_ref, mixed_ref, log_ref, table_ref, bias_ref):
    @pl.when(pl.program_id(0) == 0)
    def _():
        plan_groups(starts_ref, crops_ref, table_ref, bias_ref, rows)

    lane = lax.broadcasted_iota(jnp.int32, (WIN, PAIR), 1)

    def one(at, carry):
        base = pl.multiple_of(table_ref[0, at], SNAP)
        start = table_ref[1, at]
        window = pl.ds(base, WIN)
        query = query_ref[window, :] * jnp.asarray(HD**-0.5, BF16)
        key = key_ref[window, :]
        value_t = value_ref[window, :].T
        outs = []
        for head in range(2):
            mine = (lane >= HD) if head else (lane < HD)
            scores = mm(jnp.where(mine, key, jnp.zeros_like(key)), query, NT) + bias_ref[at]
            top = jnp.max(scores, axis=0, keepdims=True)
            expo = jnp.exp(scores - top)
            total = jnp.sum(expo, axis=0, keepdims=True)
            mixed = mm(value_t[head * HD : (head + 1) * HD, :], expo.astype(BF16))
            outs.append(mixed * (1.0 / total))
            log_ref[0, at, pl.ds(head, 1), :] = top + jnp.log(total)
        keep_from(mixed_ref, base, start, 0, jnp.concatenate(outs, axis=0).T)
        return carry

    lax.fori_loop(0, table_ref[2, 0], one, 0)


def attend(starts, crops, joint, first, pairs):
    rows = joint.shape[0]
    columns = pairs * 3 * PAIR
    all_pairs = joint.shape[1] // (3 * PAIR)
    part = lambda at: pl.BlockSpec((rows, PAIR), lambda i, *_: (0, at * all_pairs + first + i))
    groups = group_bound(rows)
    return pl.pallas_call(
        functools.partial(attend_kernel, rows),
        grid_spec=pltpu.PrefetchScalarGridSpec(
            num_scalar_prefetch=1,
            grid=(pairs,),
            in_specs=[whole_spec((rows, 128)), part(0), part(1), part(2)],
            out_specs=[
                pl.BlockSpec((rows, PAIR), lambda i, *_: (0, i)),
                pl.BlockSpec((1, groups, 8, WIN), lambda i, *_: (i, 0, 0, 0)),
            ],
            scratch_shapes=[pltpu.SMEM((3, 16), jnp.int32), pltpu.VMEM((groups, WIN, WIN), F32)],
        ),
        out_shape=[
            jax.ShapeDtypeStruct((rows, pairs * PAIR), BF16),
            jax.ShapeDtypeStruct((pairs, groups, 8, WIN), F32),
        ],
        compiler_params=params(),
        cost_estimate=cost(pairs * 6 * 8 * WIN**3, 2 * rows * columns * 4 // 3, pairs * 12 * WIN * WIN),
        name="attend",
    )(starts, crops, joint, joint, joint)


def attend_back_kernel(
    rows,
    starts_ref,
    crops_ref,
    query_ref,
    key_ref,
    value_ref,
    mixed_ref,
    grad_ref,
    log_ref,
    out_ref,
    table_ref,
    bias_ref,
):
    @pl.when(pl.program_id(0) == 0)
    def _():
        plan_groups(starts_ref, crops_ref, table_ref, bias_ref, rows)

    lane = lax.broadcasted_iota(jnp.int32, (WIN, PAIR), 1)

    def one(at, carry):
        base = pl.multiple_of(table_ref[0, at], SNAP)
        start = table_ref[1, at]
        window = pl.ds(base, WIN)
        query = query_ref[window, :] * jnp.asarray(HD**-0.5, BF16)
        key = key_ref[window, :]
        value = value_ref[window, :]
        key_t = key.T
        grad = grad_ref[window, :]
        inner_t = (grad.astype(F32) * mixed_ref[window, :].astype(F32)).T
        d_query, d_key, d_value = [], [], []
        for head in range(2):
            mine = (lane >= HD) if head else (lane < HD)
            zero = jnp.zeros_like(key)
            scores = mm(jnp.where(mine, key, zero), query, NT) + bias_ref[at]
            weights = jnp.exp(scores - log_ref[0, at, pl.ds(head, 1), :])
            inner = jnp.sum(inner_t[head * HD : (head + 1) * HD, :], axis=0, keepdims=True)
            d_weights = mm(jnp.where(mine, value, zero), grad, NT)
            d_scores = (weights * (d_weights - inner)).astype(BF16)
            d_value.append(mm(weights.astype(BF16), grad))
            d_key.append(mm(d_scores, query))
            d_query.append(mm(key_t[head * HD : (head + 1) * HD, :], d_scores) * HD**-0.5)
        low = lane < HD
        keep_from(out_ref, base, start, 0, jnp.concatenate(d_query, axis=0).T)
        keep_from(out_ref, base, start, PAIR, jnp.where(low, d_key[0], d_key[1]))
        keep_from(out_ref, base, start, 2 * PAIR, jnp.where(low, d_value[0], d_value[1]))
        return carry

    lax.fori_loop(0, table_ref[2, 0], one, 0)


def attend_back(starts, crops, joint, mixed, grad, logs, first, count):
    rows = joint.shape[0]
    groups = group_bound(rows)
    far = lambda columns: pl.BlockSpec((rows, columns), lambda i, *_: (0, first + i))
    all_pairs = joint.shape[1] // (3 * PAIR)
    part = lambda at: pl.BlockSpec((rows, PAIR), lambda i, *_: (0, at * all_pairs + first + i))
    return pl.pallas_call(
        functools.partial(attend_back_kernel, rows),
        grid_spec=pltpu.PrefetchScalarGridSpec(
            num_scalar_prefetch=1,
            grid=(count,),
            in_specs=[
                whole_spec((rows, 128)),
                part(0),
                part(1),
                part(2),
                pl.BlockSpec((rows, PAIR), lambda i, *_: (0, i)),
                far(PAIR),
                pl.BlockSpec((1, groups, 8, WIN), lambda i, *_: (i, 0, 0, 0)),
            ],
            out_specs=pl.BlockSpec((rows, 3 * PAIR), lambda i, *_: (0, i)),
            scratch_shapes=[pltpu.SMEM((3, 16), jnp.int32), pltpu.VMEM((groups, WIN, WIN), F32)],
        ),
        out_shape=jax.ShapeDtypeStruct((rows, count * 3 * PAIR), BF16),
        compiler_params=params(),
        cost_estimate=cost(count * 6 * 20 * WIN**3, 2 * rows * count * 8 * PAIR, count * 12 * WIN * WIN),
        name="attend_back",
    )(starts, crops, joint, joint, joint, mixed, grad, logs)


def up_kernel(out_weight, up_weight, me_ref, x_ref, mixed_a_ref, mixed_b_ref, vec_ref, *refs):
    count = len(out_weight.arrays)
    middle_ref, hidden_ref, active_ref, slope_ref, out_s, out_sem, up_s, up_sem = refs[count:]
    load_first([out_weight, up_weight], me_ref[0], refs[:count], [(out_s, out_sem), (up_s, up_sem)])
    mixed = jnp.concatenate([mixed_a_ref[...], mixed_b_ref[...]], axis=1)
    middle = x_ref[...].astype(F32) + mm(mixed, out_s[...]) + vec_ref[4:5, :]
    middle_ref[...] = middle
    unit, _ = normed(middle)
    hidden = (unit * vec_ref[5:6, :] + vec_ref[6:7, :]).astype(BF16)
    hidden_ref[...] = hidden
    chunk = vec_ref.shape[1]
    for at in range(up_weight.shape[1] // chunk):
        part = pl.ds(at * chunk, chunk)
        value = mm(hidden, up_s[:, part]) + vec_ref[8 + at : 9 + at, :]
        below = 0.5 + 0.5 * lax.erf(value * (0.5**0.5))
        active_ref[:, part] = (value * below).astype(BF16)
        bell = jnp.exp(value * value * -0.5) * 0.3989422804014327
        slope_ref[:, part] = (below + value * bell).astype(BF16)


def up_forward(me, tokens, mixed_a, mixed_b, vectors, out_weight, up_weight):
    rows, width = tokens.shape
    inner = up_weight.shape[1]
    arrays = out_weight.arrays
    return pl.pallas_call(
        functools.partial(up_kernel, out_weight, up_weight),
        grid_spec=pltpu.PrefetchScalarGridSpec(
            num_scalar_prefetch=1,
            grid=(rows // TILE,),
            in_specs=[row_spec(width), row_spec(width // 2), row_spec(width // 2), whole_spec(vectors.shape)]
            + any_specs(len(arrays)),
            out_specs=[row_spec(width), row_spec(width), row_spec(inner), row_spec(inner)],
            scratch_shapes=out_weight.scratch() + up_weight.scratch(),
        ),
        out_shape=[
            jax.ShapeDtypeStruct((rows, width), F32),
            jax.ShapeDtypeStruct((rows, width), BF16),
            jax.ShapeDtypeStruct((rows, inner), BF16),
            jax.ShapeDtypeStruct((rows, inner), BF16),
        ],
        compiler_params=params(),
        cost_estimate=cost(2 * rows * width * (width + inner), rows * (10 * width + 4 * inner) + 2 * width * inner, rows * inner * 2),
        name="up_forward",
    )(me, tokens, mixed_a, mixed_b, vectors, *arrays)


def slope_kernel(down_weight, me_ref, grad_ref, slope_ref, *refs):
    count = len(down_weight.arrays)
    ga_ref, sums_ref, upsum_ref, down_s, down_sem = refs[count:]
    load_first([down_weight], me_ref[0], refs[:count], [(down_s, down_sem)])

    @pl.when(pl.program_id(0) == 0)
    def _():
        sums_ref[...] = jnp.zeros_like(sums_ref)
        upsum_ref[...] = jnp.zeros_like(upsum_ref)

    grad = grad_ref[...]
    sums_ref[...] += fold(grad.astype(F32))
    for at in range(0, down_weight.shape[0], CHUNK):
        part = pl.ds(at, CHUNK)
        inner = (mm(grad, down_s[part, :], NT) * slope_ref[:, part].astype(F32)).astype(BF16)
        ga_ref[:, part] = inner
        upsum_ref[:, part] += fold(inner.astype(F32))


def slope_back(me, grad, slope, down_weight):
    rows, width = grad.shape
    inner = slope.shape[1]
    return pl.pallas_call(
        functools.partial(slope_kernel, down_weight),
        grid_spec=pltpu.PrefetchScalarGridSpec(
            num_scalar_prefetch=1,
            grid=(rows // TILE,),
            in_specs=[row_spec(width), row_spec(inner)] + any_specs(len(down_weight.arrays)),
            out_specs=[row_spec(inner), whole_spec((8, width)), whole_spec((8, inner))],
            scratch_shapes=down_weight.scratch(),
        ),
        out_shape=[
            jax.ShapeDtypeStruct((rows, inner), BF16),
            jax.ShapeDtypeStruct((8, width), F32),
            jax.ShapeDtypeStruct((8, inner), F32),
        ],
        compiler_params=params(),
        cost_estimate=cost(2 * rows * width * inner, rows * (2 * width + 4 * inner) + 2 * width * inner),
        name="slope_back",
    )(me, grad, slope, *down_weight.arrays)


def middle_kernel(out_weight, up_weight, me_ref, middle_ref, grad_ref, ga_ref, vec_ref, *refs):
    count = len(up_weight.arrays)
    gmid_ref, glow_ref, gmix_ref, sums_ref, out_s, out_sem, up_s, up_sem = refs[count:]
    load_first([out_weight, up_weight], me_ref[0], refs[:count], [(out_s, out_sem), (up_s, up_sem)])

    @pl.when(pl.program_id(0) == 0)
    def _():
        sums_ref[...] = jnp.zeros_like(sums_ref)

    total = mm(ga_ref[...], up_s[...], NT)
    unit, scale = normed(middle_ref[...])
    sums_ref[0] += fold(total * unit)
    sums_ref[1] += fold(total)
    gmid = grad_ref[...].astype(F32) + norm_back(total, unit, scale, vec_ref[5:6, :])
    gmid_ref[...] = gmid
    low = gmid.astype(BF16)
    glow_ref[...] = low
    sums_ref[2] += fold(low.astype(F32))
    gmix_ref[...] = mm(low, out_s[...], NT).astype(BF16)


def middle_back(me, middle, grad, ga, vectors, out_weight, up_weight):
    rows, width = middle.shape
    inner = ga.shape[1]
    return pl.pallas_call(
        functools.partial(middle_kernel, out_weight, up_weight),
        grid_spec=pltpu.PrefetchScalarGridSpec(
            num_scalar_prefetch=1,
            grid=(rows // TILE,),
            in_specs=[row_spec(width), row_spec(width), row_spec(inner), whole_spec(vectors.shape)]
            + any_specs(len(up_weight.arrays)),
            out_specs=[row_spec(width), row_spec(width), row_spec(width), whole_spec((3, 8, width))],
            scratch_shapes=out_weight.scratch() + up_weight.scratch(),
        ),
        out_shape=[
            jax.ShapeDtypeStruct((rows, width), F32),
            jax.ShapeDtypeStruct((rows, width), BF16),
            jax.ShapeDtypeStruct((rows, width), BF16),
            jax.ShapeDtypeStruct((3, 8, width), F32),
        ],
        compiler_params=params(),
        cost_estimate=cost(2 * rows * width * (width + inner), rows * (14 * width + 2 * inner) + 2 * width * inner),
        name="middle_back",
    )(me, middle, grad, ga, vectors, *up_weight.arrays)


def down_kernel(down_weight, me_ref, middle_ref, active_ref, vec_ref, *refs):
    count = len(down_weight.arrays)
    acts_ref, down_s, down_sem = refs[count:]
    load_first([down_weight], me_ref[0], refs[:count], [(down_s, down_sem)])
    acts_ref[...] = middle_ref[...] + mm(active_ref[...], down_s[...]) + vec_ref[7:8, :]


def down_forward(me, middle, active, vectors, down_weight):
    rows, width = middle.shape
    inner = active.shape[1]
    return pl.pallas_call(
        functools.partial(down_kernel, down_weight),
        grid_spec=pltpu.PrefetchScalarGridSpec(
            num_scalar_prefetch=1,
            grid=(rows // TILE,),
            in_specs=[row_spec(width), row_spec(inner), whole_spec(vectors.shape)] + any_specs(len(down_weight.arrays)),
            out_specs=row_spec(width),
            scratch_shapes=down_weight.scratch(),
        ),
        out_shape=jax.ShapeDtypeStruct((rows, width), F32),
        compiler_params=params(),
        cost_estimate=cost(2 * rows * width * inner, rows * (8 * width + 2 * inner) + 2 * width * inner),
        name="down_forward",
    )(me, middle, active, vectors, *down_weight.arrays)


def first_kernel(
    weight, me_ref, x_ref, gmid_ref, part_a_ref, part_b_ref, vec_ref, cot_ref, mid_ref, up_ref, *refs
):
    count = len(weight.arrays)
    out_ref, rows_ref, sums_ref, joint_sum_ref, scratch, sems = refs[count:]
    load_first([weight], me_ref[0], refs[:count], [(scratch, sems)])

    @pl.when(pl.program_id(0) == 0)
    def _():
        sums_ref[...] = jnp.zeros_like(sums_ref)
        joint_sum_ref[...] = jnp.zeros_like(joint_sum_ref)

    halves = [part_a_ref, part_b_ref]
    pairs = part_a_ref.shape[1] // (3 * PAIR)
    blocks = [
        half[:, (3 * pair + part) * PAIR : (3 * pair + part + 1) * PAIR]
        for part in range(3)
        for half in halves
        for pair in range(pairs)
    ]
    grad = jnp.concatenate(blocks, axis=1)
    joint_sum_ref[...] += fold(grad.astype(F32))
    total = mm(grad, scratch[...], NT)
    unit, scale = normed(x_ref[...].astype(F32))
    sums_ref[0] += fold(total * unit)
    sums_ref[1] += fold(total)
    out_ref[...] = gmid_ref[...] + norm_back(total, unit, scale, vec_ref[0:1, :])

    @pl.when(pl.program_id(0) == pl.num_programs(0) - 1)
    def _():
        width = x_ref.shape[1]
        line = lambda value: jnp.sum(value, axis=0, keepdims=True)
        wide = [line(up_ref[:, at : at + width]) for at in range(0, up_ref.shape[1], width)]
        rows_ref[...] = jnp.concatenate(
            [
                line(sums_ref[0]),
                line(sums_ref[1]),
                line(joint_sum_ref[:, :width]),
                line(joint_sum_ref[:, 2 * width :]),
                line(mid_ref[2]),
                line(mid_ref[0]),
                line(mid_ref[1]),
                line(cot_ref[...]),
            ]
            + wide
            + [jnp.zeros((8 - len(wide), width), F32)],
            axis=0,
        )


def first_back(me, tokens, gmid, part_a, part_b, vectors, cot_sums, mid_sums, up_sums, weight):
    rows, width = tokens.shape
    columns = weight.shape[1]
    return pl.pallas_call(
        functools.partial(first_kernel, weight),
        grid_spec=pltpu.PrefetchScalarGridSpec(
            num_scalar_prefetch=1,
            grid=(rows // TILE,),
            in_specs=[row_spec(width), row_spec(width), row_spec(columns // 2), row_spec(columns // 2)]
            + [whole_spec(array.shape) for array in (vectors, cot_sums, mid_sums, up_sums)]
            + any_specs(len(weight.arrays)),
            out_specs=[row_spec(width), whole_spec((16, width))],
            scratch_shapes=[pltpu.VMEM((2, 8, width), F32), pltpu.VMEM((8, columns), F32)] + weight.scratch(),
        ),
        out_shape=[jax.ShapeDtypeStruct((rows, width), F32), jax.ShapeDtypeStruct((16, width), F32)],
        compiler_params=params(),
        cost_estimate=cost(2 * rows * width * columns, rows * (10 * width + 2 * columns) + 2 * width * columns),
        name="first_back",
    )(me, tokens, gmid, part_a, part_b, vectors, cot_sums, mid_sums, up_sums, *weight.arrays)


def own_rows_kernel(me_ref, left_ref, right_ref, gain_a, shift_a, joint_b, out_b, gain_b, shift_b, down_b, up_b):
    me = me_ref[0]
    own = gain_a.shape[0]
    total = left_ref[0:8, :] + right_ref[0:8, :]
    mine = pltpu.roll(total, lax.rem(8 - me, 8) * own, axis=1)[:, :own]
    for at, ref in enumerate((gain_a, shift_a, None, None, out_b, gain_b, shift_b, down_b)):
        if ref is not None:
            ref[...] = mine[at]
    joint_b[...] = mine[2:4]
    line = 8 + (me >> 1)
    row = left_ref[pl.ds(line, 1), :] + right_ref[pl.ds(line, 1), :]
    half = up_b.shape[0]
    up_b[...] = jnp.where((me & 1) == 1, row[:, half:], row[:, :half])[0]


def own_rows(me, left, right):
    own = left.shape[1] // 8
    vector = jax.ShapeDtypeStruct((own,), F32)
    out_shape = [vector, vector, jax.ShapeDtypeStruct((2, own), F32), vector, vector, vector, vector]
    out_shape.append(jax.ShapeDtypeStruct((4 * own,), F32))
    return pl.pallas_call(
        own_rows_kernel,
        grid_spec=pltpu.PrefetchScalarGridSpec(
            num_scalar_prefetch=1,
            grid=(1,),
            in_specs=[whole_spec(left.shape), whole_spec(right.shape)],
            out_specs=[whole_spec(shape.shape) for shape in out_shape],
        ),
        out_shape=out_shape,
        compiler_params=params(),
        name="own_rows",
    )(me, left, right)


def weight_grad(left, right):
    return lax.dot_general(left, right, (((0,), (0,)), ((), ())), preferred_element_type=F32).astype(BF16)


def on_device(
    fsdp,
    dp,
    tokens,
    crop_ids,
    gain_first,
    shift_first,
    joint_weight,
    joint_bias,
    output_weight,
    output_bias,
    gain_second,
    shift_second,
    up_weight,
    up_bias,
    down_weight,
    down_bias,
    cotangent,
):
    rows, width = tokens.shape
    inner = up_bias.shape[0] * fsdp
    joint_width = joint_weight.shape[1]
    rank = lax.axis_index("fsdp")
    me = rank.astype(jnp.int32).reshape(1)
    own = width // fsdp
    own_up = inner // fsdp

    eight = fsdp == 8
    if eight:
        lines = [gain_first, shift_first, joint_bias[0], joint_bias[1], output_bias, gain_second, shift_second, down_bias]
        first_in = jnp.pad(joint_weight, ((0, 8), (0, 0)))
        for at, line in enumerate(lines):
            first_in += jnp.pad(line[None], ((own + at, 7 - at), (0, joint_width - own)))
        first_in += jnp.pad(up_bias[None], ((own, 7), (128, joint_width - 128 - own_up)))
        vectors = None
    else:
        first_in = joint_weight
        pack = [gain_first, shift_first, joint_bias[0], joint_bias[1], output_bias, gain_second, shift_second, down_bias]
        pack = [lax.all_gather(line.astype(BF16), "fsdp", axis=0, tiled=True) for line in pack + [up_bias]]
        vectors = jnp.concatenate([jnp.stack(pack[:8]), pack[8].reshape(-1, width)], axis=0).astype(F32)
        vectors = jnp.pad(vectors, ((0, 16 - vectors.shape[0]), (0, 0)))
    outer = jnp.concatenate([output_weight, up_weight], axis=1)

    starts = jnp.sum((crop_ids[None, :] < crop_ids[:, None]).astype(jnp.int32), axis=1)
    crops = jnp.broadcast_to(crop_ids.astype(F32)[:, None], (rows, 128))

    pairs = joint_width // (3 * PAIR)
    near = pairs // 2
    group = Gather(first_in, fsdp)
    source = tokens
    if eight:
        group.first()
        group.second()
        group.third()
        source = after(source, starts, crops)
    else:
        group.whole()
    outer_group = Gather(outer, fsdp).whole()
    lower_group = Gather(after(down_weight, outer), fsdp).whole()
    joint_full = Weight(group, 0, joint_width, spare=8 if eight else 0)
    joint, hidden_first, vectors = joint_forward(me, source, vectors, joint_full)
    mixed_a, logs_a = attend(starts, crops, joint, 0, near)
    mixed_b, logs_b = attend(starts, crops, joint, near, pairs - near)
    out_full = Weight(outer_group, 0, width)
    up_full = Weight(outer_group, width, inner)
    middle, hidden_second, active, slope = up_forward(me, tokens, mixed_a, mixed_b, vectors, out_full, up_full)
    grad = cotangent
    down_full = Weight(lower_group, 0, width)

    start = lambda slabs, short=False, scattered=False: Grad(slabs, fsdp, dp, short, scattered)
    behind = lambda value, *grads: after(value, *[g for g in grads if g is not None])

    scattered = lambda value: lax.psum_scatter(value, "fsdp", scatter_dimension=0, tiled=True)
    down_grad = weight_grad(active, grad)
    grad_up, cotangent_sums, up_sums = slope_back(me, behind(cotangent, down_grad), slope, down_full)
    down_grad = scattered(down_grad)
    up_grad = weight_grad(hidden_second, grad_up)
    grad_middle, grad_low, grad_mixed, sums = middle_back(
        me, middle, cotangent, behind(grad_up, up_grad), vectors, out_full, up_full
    )
    up_grad = scattered(up_grad)
    down_grad = start(down_grad, scattered=True)
    grad_a = attend_back(starts, crops, joint, mixed_a, grad_mixed, logs_a, 0, near)
    low = behind(grad_low, grad_a)
    out_slabs = jnp.concatenate([weight_grad(mixed_a, low), weight_grad(mixed_b, low)], axis=0).reshape(fsdp, own, width)
    slabs_a = weight_grad(hidden_first, grad_a).reshape(fsdp, own, -1)
    mixed_grad = start(jnp.concatenate([out_slabs, slabs_a], axis=2))
    if eight:
        mixed_grad.more = up_grad
    sent = [mixed_grad.step(), down_grad.step(grad_a)]
    grad_b = attend_back(starts, crops, joint, mixed_b, behind(grad_mixed, *sent), logs_b, near, pairs - near)
    last_slabs = weight_grad(behind(hidden_first, mixed_grad.step(grad_b)), grad_b)
    last_grad = start(last_slabs.reshape(fsdp, own, -1), True)
    sent = [last_grad.step(), down_grad.step(last_slabs)]
    input_grad, total = first_back(
        me,
        behind(tokens, *sent),
        grad_middle,
        grad_a,
        grad_b,
        vectors,
        cotangent_sums,
        sums,
        up_sums,
        joint_full,
    )
    sent = [last_grad.step(total), mixed_grad.step(total), down_grad.step(total)]
    if eight and dp == 4:
        total = behind(total, *sent)
        total = total + send(total, CORE)
        sent = [down_grad.step(total), last_grad.step(total)]
        total = behind(total, *sent)
        total = total + send(total, FIRST)
        sent = [mixed_grad.step(total)]
        total = behind(total, *sent)
        total = total + send(total, SECOND)
        sent = [last_grad.step(total)]
        acts = down_forward(me, behind(middle, *sent), active, vectors, down_full)
        sent = [mixed_grad.step(acts)]
        total = behind(total, *sent)
        total = total + send_dp(total, 1)
        vecs = own_rows(me, total, send_dp(total, 2))
    else:
        acts = down_forward(me, behind(middle, *sent), active, vectors, down_full)
        total = lax.psum(total, ("fsdp", "dp"))
        vecs = [lax.dynamic_slice_in_dim(total[at], rank * own, own) for at in range(8)]
        vecs.append(lax.dynamic_slice_in_dim(total[8:].reshape(-1), rank * own_up, own_up))
        vecs = vecs[:2] + [jnp.stack(vecs[2:4])] + vecs[4:]
    last = last_grad.result()
    mixed_out = mixed_grad.result()
    down_grad = down_grad.result()
    if eight:
        mixed_out, up_grad = mixed_out[:, : -up_grad.shape[1]], mixed_out[:, -up_grad.shape[1] :]
    else:
        up_grad = lax.psum(up_grad, "dp").astype(F32)
    wide_grads = [mixed_out[:, width:], last]
    grad_joint = jnp.concatenate(
        [
            half[:, (3 * pair + part) * PAIR : (3 * pair + part + 1) * PAIR]
            for part in range(3)
            for half in wide_grads
            for pair in range(half.shape[1] // (3 * PAIR))
        ],
        axis=1,
    )
    gain_a, shift_a, joint_b, out_b, gain_b, shift_b, down_b, up_b = vecs
    return (
        acts,
        input_grad,
        gain_a,
        shift_a,
        grad_joint,
        joint_b,
        mixed_out[:, :width],
        out_b,
        gain_b,
        shift_b,
        up_grad,
        up_b,
        down_grad,
        down_b,
    )


def solution(mesh):
    rows, line, flat = P(("fsdp", "dp"), None), P("fsdp"), P("fsdp", None)
    both = P(None, "fsdp")
    return jax.shard_map(
        functools.partial(on_device, mesh.shape["fsdp"], mesh.shape["dp"]),
        mesh=mesh,
        in_specs=(rows, P(("fsdp", "dp")), line, line, flat, both, flat, line, line, line, flat, line, flat, line, rows),
        out_specs=(rows, rows, line, line, flat, both, flat, line, line, line, flat, line, flat, line),
        check_vma=False,
    )
```

```python
import functools

import jax
import jax.numpy as jnp
from jax import lax
from jax.experimental import pallas as pl
from jax.experimental.pallas import tpu as pltpu
from jax.sharding import PartitionSpec as P

HD = 64
PAIR = 2 * HD
EPS = 1e-06
WIN = 256
SNAP = 16
TILE = 256
CHUNK = 512
LIMIT = 58 << 20
F32 = jnp.float32
BF16 = jnp.bfloat16
NT = (((1,), (1,)), ((), ()))
NN = (((1,), (0,)), ((), ()))


def mm(left, right, dims=NN):
    return lax.dot_general(left, right, dims, preferred_element_type=F32)


def fold(values):
    return jnp.sum(values.reshape(values.shape[0] // 8, 8, values.shape[1]), axis=0)


CORE = [(i, i ^ 1) for i in range(8)]
FIRST = [(i, i ^ (4 if i & 1 else 2)) for i in range(8)]
SECOND = [(i, i ^ (2 if i & 1 else 4)) for i in range(8)]


def send(value, pairs):
    return lax.ppermute(value, "fsdp", pairs)


def send_dp(value, bit):
    return lax.ppermute(value, "dp", [(i, i ^ bit) for i in range(4)])


def after(value, *others):
    return lax.optimization_barrier((value,) + others)[0]


def pick(value, at, axis=0):
    return lax.dynamic_index_in_dim(value, at, axis, keepdims=False)


def wide(value):
    return value.astype(F32)


class Scatter:
    def __init__(self, slabs):
        me = lax.axis_index("fsdp")
        self.core = me & 1
        at_x, at_y = (me >> 1) & 1, me >> 2
        rows, columns = slabs.shape[1:]
        self.slabs = slabs.reshape(4, 2, rows, columns)
        even = self.core == 0
        keep, leave = 1 - at_y, 1 - at_x
        self.away = (jnp.where(even, 2 * keep, leave), jnp.where(even, 2 * keep + 1, 2 + leave))
        self.near = jnp.where(even, at_x, at_y)
        self.chip = 2 * at_y + at_x
        self.next_chip = jnp.where(even, 2 * at_y + 1 - at_x, 2 * (1 - at_y) + at_x)
        self.mine = pick(self.slabs, self.core, 1)
        self.got = []

    def give(self):
        if not self.got:
            return pick(self.slabs, 1 - self.core, 1)
        if len(self.got) == 1:
            return jnp.stack([wide(pick(self.mine, at)) + wide(pick(self.got[0], at)) for at in self.away]).astype(BF16)
        total = wide(pick(self.mine, self.next_chip)) + wide(pick(self.got[0], self.next_chip))
        return (total + wide(pick(self.got[1], 1 - self.near))).astype(BF16)

    def take(self, value):
        self.got.append(value)

    def pairs(self):
        return (CORE, SECOND, FIRST)[len(self.got)]

    def result(self):
        total = wide(pick(self.mine, self.chip)) + wide(pick(self.got[0], self.chip))
        return (total + wide(pick(self.got[1], self.near)) + wide(self.got[2])).astype(BF16)


class Sum:
    def __init__(self, value, short=False):
        me = lax.axis_index("dp")
        self.low, self.high = (me ^ (me >> 1)) & 1, me >> 1
        self.value = value
        self.short = short
        self.got = []
        self.split()

    def split(self):
        rows, columns = self.value.shape
        self.halves = self.value.reshape(2, rows // 2, columns)

    def half(self):
        return wide(pick(self.halves, self.low)) + wide(self.got[0])

    def quarters(self):
        half = self.half()
        return half.reshape(2, half.shape[0] // 2, half.shape[1])

    def own(self):
        return (pick(self.quarters(), self.high) + wide(self.got[1])).astype(BF16)

    def join(self, mine, other, bit):
        return jnp.concatenate([jnp.where(bit == 0, mine, other), jnp.where(bit == 0, other, mine)], axis=0)

    def give(self):
        step = len(self.got)
        if self.short:
            return self.value.astype(BF16) if step == 0 else (wide(self.value) + wide(self.got[0])).astype(BF16)
        if step == 0:
            return pick(self.halves, 1 - self.low).astype(BF16)
        if step == 1:
            return pick(self.quarters(), 1 - self.high).astype(BF16)
        if step == 2:
            return self.own()
        return self.join(self.own(), self.got[2], self.high)

    def bit(self):
        return ((1, 3) if self.short else (1, 3, 3, 1))[len(self.got)]

    def take(self, value):
        self.got.append(value)

    def result(self):
        if self.short:
            return wide(self.value) + wide(self.got[0]) + wide(self.got[1])
        half = self.join(self.own(), self.got[2], self.high)
        return wide(self.join(half, self.got[3], self.low))


class Grad:
    def __init__(self, slabs, fsdp, dp, short=False, scattered=False):
        self.dp, self.short = dp, short
        self.sum = self.scatter = self.more = None
        if scattered:
            self.enter(slabs)
        elif fsdp == 8:
            self.scatter = Scatter(slabs)
        else:
            self.enter(lax.psum_scatter(slabs, "fsdp", scatter_dimension=0, tiled=True)[0])

    def enter(self, value):
        if self.dp == 4:
            self.sum = Sum(value, self.short)
        else:
            self.out = lax.psum(value, "dp").astype(F32)

    def step(self, *behind):
        stage = self.scatter if self.scatter is not None else self.sum
        if stage is None or (stage is self.sum and len(stage.got) == (2 if self.short else 4)):
            return None
        if behind and stage.got:
            stage.got[-1] = after(stage.got[-1], *behind)
        elif behind and stage is self.sum:
            stage.value = after(stage.value, *behind)
            stage.split()
        given = stage.give()
        if stage is self.sum:
            stage.take(send_dp(given, stage.bit()))
            return given
        stage.take(send(given, stage.pairs()))
        if len(stage.got) == 3:
            self.scatter = None
            value = stage.result()
            self.enter(value if self.more is None else jnp.concatenate([value, self.more], axis=1))
        return given

    def hold(self, *behind):
        stage = self.scatter if self.scatter is not None else self.sum
        if stage.got:
            stage.got[-1] = after(stage.got[-1], *behind)
        else:
            stage.value = after(stage.value, *behind)
            stage.split()

    def result(self):
        while self.step() is not None:
            pass
        return self.sum.result() if self.sum is not None else self.out


class Gather:
    def __init__(self, shard, fsdp):
        self.fsdp = fsdp
        self.shard = shard

    def whole(self):
        self.fsdp = 1
        self.arrays = [lax.all_gather(self.shard, "fsdp", axis=0, tiled=True)]
        return self

    def first(self):
        self.two = jnp.stack([self.shard, send(self.shard, FIRST)])
        return self.two

    def second(self):
        self.more = send(self.two, SECOND)
        self.swapped = send(self.two, CORE)
        return self.more

    def third(self):
        self.arrays = [self.two, self.more, self.swapped, send(self.more, CORE)]
        return self.arrays[-1]

    def blocks(self):
        def owner(theirs, far, at):
            def of(me):
                base = me ^ 1 if theirs else me
                one, two = 2 + 2 * (base & 1), 4 - 2 * (base & 1)
                return base ^ ((two if far else 0) + (one if at else 0))

            return of

        return [(a, at, owner(a >= 2, a % 2 == 1, at)) for a in range(4) for at in range(2)]


class Weight:
    def __init__(self, gathered, first, columns, deep=1, spare=0):
        self.gathered, self.first, self.columns, self.deep = gathered, first, columns, deep
        self.arrays = gathered.arrays
        self.rows = gathered.shard.shape[0] - spare
        self.shape = (self.rows * deep * 8 if gathered.fsdp == 8 else self.arrays[0].shape[0], columns)
        self.count = deep * 8 if gathered.fsdp == 8 else 1

    def copies(self, me, refs, scratch, sems):
        if self.gathered.fsdp != 8:
            source = refs[0].at[:, pl.ds(self.first, self.columns)]
            return [pltpu.make_async_copy(source, scratch, sems.at[0])]
        made = []
        for array, at, owner in self.gathered.blocks():
            for part in range(self.deep):
                start = pl.multiple_of((owner(me) * self.deep + part) * self.rows, 16)
                source = refs[array].at[at, pl.ds(0, self.rows), pl.ds(self.first + part * self.columns, self.columns)]
                made.append(pltpu.make_async_copy(source, scratch.at[pl.ds(start, self.rows), :], sems.at[len(made)]))
        return made

    def vectors(self, me, refs, held, sems):
        made = []
        for array, at, owner in self.gathered.blocks():
            source = refs[array].at[at, pl.ds(self.rows, 8), pl.ds(0, 512)]
            made.append(pltpu.make_async_copy(source, held.at[owner(me)], sems.at[len(made)]))
        return made

    def scratch(self):
        return [pltpu.VMEM(self.shape, BF16), pltpu.SemaphoreType.DMA((self.count,))]


def any_specs(count):
    return [pl.BlockSpec(memory_space=pl.ANY)] * count


def params():
    return pltpu.CompilerParams(dimension_semantics=("arbitrary",), vmem_limit_bytes=LIMIT)


def cost(flops, reads, exps=0):
    return pl.CostEstimate(flops=int(flops), transcendentals=int(exps), bytes_accessed=int(reads))


def row_spec(columns):
    return pl.BlockSpec((TILE, columns), lambda i, *_: (i, 0))


def whole_spec(shape):
    return pl.BlockSpec(shape, lambda i, *_: (0,) * len(shape))


def normed(values):
    center = values - jnp.mean(values, axis=-1, keepdims=True)
    scale = lax.rsqrt(jnp.mean(center * center, axis=-1, keepdims=True) + EPS)
    return center * scale, scale


def norm_back(grad, unit, scale, gain):
    scaled = grad * gain
    first = jnp.mean(scaled, axis=-1, keepdims=True)
    second = jnp.mean(scaled * unit, axis=-1, keepdims=True)
    return (scaled - first - unit * second) * scale


def load_first(weights, me, refs, scratches):
    @pl.when(pl.program_id(0) == 0)
    def _():
        started = []
        for weight, (scratch, sems) in zip(weights, scratches):
            started += weight.copies(me, refs, scratch, sems)
        for copy in started:
            copy.start()
        for copy in started:
            copy.wait()


def unpack(held_ref):
    total = None
    for at in range(8):
        row = held_ref[at][:, 0:128].astype(F32)
        row = jnp.concatenate([row, jnp.zeros((8, 640), F32)], axis=1)
        row = pltpu.roll(row, 96 * at, axis=1) if at else row
        total = row if total is None else total + row
    flat = [held_ref[at][0:1, 128:512].astype(F32) for at in range(8)]
    rows = [jnp.concatenate([flat[2 * at], flat[2 * at + 1]], axis=1) for at in range(4)]
    return jnp.concatenate([total] + rows + [jnp.zeros((4, 768), F32)], axis=0)


def joint_kernel(weight, packed, me_ref, x_ref, *refs):
    count = len(weight.arrays)
    if packed:
        arrays, (out_ref, hidden_ref, vec_ref, scratch, sems, held_ref, held_sems) = refs[:count], refs[count:]

        @pl.when(pl.program_id(0) == 0)
        def _():
            started = weight.vectors(me_ref[0], arrays, held_ref, held_sems)
            for copy in started:
                copy.start()
            load = weight.copies(me_ref[0], arrays, scratch, sems)
            for copy in load:
                copy.start()
            for copy in started:
                copy.wait()
            vec_ref[...] = unpack(held_ref)
            for copy in load:
                copy.wait()
    else:
        vec_ref, arrays, (out_ref, hidden_ref, scratch, sems) = refs[0], refs[1 : 1 + count], refs[1 + count :]
        load_first([weight], me_ref[0], arrays, [(scratch, sems)])
    unit, _ = normed(x_ref[...].astype(F32))
    hidden = (unit * vec_ref[0:1, :] + vec_ref[1:2, :]).astype(BF16)
    hidden_ref[...] = hidden
    bias = jnp.concatenate([vec_ref[2:3, :], jnp.zeros_like(vec_ref[2:3, :]), vec_ref[3:4, :]], axis=1)
    out_ref[...] = (mm(hidden, scratch[...]) + bias).astype(BF16)


def joint_forward(me, tokens, vectors, weight):
    rows, width = tokens.shape
    columns = weight.shape[1]
    packed = vectors is None
    out_specs = [row_spec(columns), row_spec(width)]
    out_shape = [jax.ShapeDtypeStruct((rows, columns), BF16), jax.ShapeDtypeStruct((rows, width), BF16)]
    scratch = weight.scratch()
    if packed:
        out_specs.append(whole_spec((16, width)))
        out_shape.append(jax.ShapeDtypeStruct((16, width), F32))
        scratch += [pltpu.VMEM((8, 8, 512), BF16), pltpu.SemaphoreType.DMA((8,))]
    outs = pl.pallas_call(
        functools.partial(joint_kernel, weight, packed),
        grid_spec=pltpu.PrefetchScalarGridSpec(
            num_scalar_prefetch=1,
            grid=(rows // TILE,),
            in_specs=[row_spec(width)] + ([] if packed else [whole_spec((16, width))]) + any_specs(len(weight.arrays)),
            out_specs=out_specs,
            scratch_shapes=scratch,
        ),
        out_shape=out_shape,
        compiler_params=params(),
        cost_estimate=cost(2 * rows * width * columns, 2 * (rows * (2 * width + columns) + width * columns)),
        name="joint_forward",
    )(me, tokens, *([] if packed else [vectors]), *weight.arrays)
    return outs if packed else (*outs, vectors)


def plan_groups(starts_ref, crops_ref, table_ref, bias_ref, rows):
    def one(state):
        at, start = state
        base = jnp.minimum((start // SNAP) * SNAP, rows - WIN)
        base = pl.multiple_of(base, SNAP)
        edge = base + WIN
        stop = jnp.where(edge >= rows, rows, starts_ref[jnp.minimum(edge, rows - 1)])
        table_ref[0, at] = base
        table_ref[1, at] = start
        down = crops_ref[pl.ds(base, WIN), :]
        across = down.T
        down = jnp.concatenate([down] * (WIN // 128), axis=1)
        across = jnp.concatenate([across] * (WIN // 128), axis=0)
        bias_ref[at] = jnp.where(down == across, 0.0, -1e30)
        return at + 1, stop

    more = lambda state: jnp.logical_and(state[1] < rows, state[0] < group_bound(rows))
    table_ref[2, 0] = lax.while_loop(more, one, (jnp.int32(0), jnp.int32(0)))[0]


def group_bound(rows):
    return 2 * (rows // (WIN - SNAP + 2)) + 2


def keep_from(ref, base, start, columns, value):
    window = (pl.ds(base, WIN), pl.ds(columns, PAIR))
    row = base + lax.broadcasted_iota(jnp.int32, (WIN, PAIR), 0)
    ref[window] = jnp.where(row >= start, value, ref[window].astype(F32)).astype(ref.dtype)


def attend_kernel(rows, starts_ref, crops_ref, query_ref, key_ref, value_ref, mixed_ref, log_ref, table_ref, bias_ref):
    @pl.when(pl.program_id(0) == 0)
    def _():
        plan_groups(starts_ref, crops_ref, table_ref, bias_ref, rows)

    lane = lax.broadcasted_iota(jnp.int32, (WIN, PAIR), 1)

    def one(at, carry):
        base = pl.multiple_of(table_ref[0, at], SNAP)
        start = table_ref[1, at]
        for pair in range(query_ref.shape[1] // PAIR):
            window = (pl.ds(base, WIN), pl.ds(pair * PAIR, PAIR))
            query = query_ref[window] * jnp.asarray(HD**-0.5, BF16)
            key = key_ref[window]
            value_t = value_ref[window].T
            outs = []
            for head in range(2):
                mine = (lane >= HD) if head else (lane < HD)
                scores = mm(jnp.where(mine, key, jnp.zeros_like(key)), query, NT) + bias_ref[at]
                top = jnp.max(scores, axis=0, keepdims=True)
                expo = jnp.exp(scores - top)
                total = jnp.sum(expo, axis=0, keepdims=True)
                mixed = mm(value_t[head * HD : (head + 1) * HD, :], expo.astype(BF16))
                outs.append(mixed * (1.0 / total))
                log_ref[pair, at, pl.ds(head, 1), :] = top + jnp.log(total)
            keep_from(mixed_ref, base, start, pair * PAIR, jnp.concatenate(outs, axis=0).T)
        return carry

    lax.fori_loop(0, table_ref[2, 0], one, 0)


def attend_scratch(rows):
    return [pltpu.SMEM((3, 16), jnp.int32), pltpu.VMEM((group_bound(rows), WIN, WIN), F32)]


def attend(starts, crops, joint, count):
    rows = joint.shape[0]
    pairs = joint.shape[1] // (3 * PAIR)
    groups = group_bound(rows)
    part = lambda at: pl.BlockSpec((rows, count * PAIR), lambda i, *_: (0, at * (pairs // count) + i))
    return pl.pallas_call(
        functools.partial(attend_kernel, rows),
        grid_spec=pltpu.PrefetchScalarGridSpec(
            num_scalar_prefetch=1,
            grid=(pairs // count,),
            in_specs=[whole_spec((rows, 128)), part(0), part(1), part(2)],
            out_specs=[part(0), pl.BlockSpec((count, groups, 8, WIN), lambda i, *_: (i, 0, 0, 0))],
            scratch_shapes=attend_scratch(rows),
        ),
        out_shape=[
            jax.ShapeDtypeStruct((rows, pairs * PAIR), BF16),
            jax.ShapeDtypeStruct((pairs, groups, 8, WIN), F32),
        ],
        compiler_params=params(),
        cost_estimate=cost(pairs * 6 * 8 * WIN**3, 2 * rows * pairs * 4 * PAIR, pairs * 12 * WIN * WIN),
        name="attend",
    )(starts, crops, joint, joint, joint)


def attend_back_kernel(
    rows,
    starts_ref,
    crops_ref,
    query_ref,
    key_ref,
    value_ref,
    mixed_ref,
    grad_ref,
    log_ref,
    out_ref,
    table_ref,
    bias_ref,
):
    plan_groups(starts_ref, crops_ref, table_ref, bias_ref, rows)
    lane = lax.broadcasted_iota(jnp.int32, (WIN, PAIR), 1)
    low = lane < HD

    def one(at, carry):
        base = pl.multiple_of(table_ref[0, at], SNAP)
        start = table_ref[1, at]
        for pair in range(query_ref.shape[1] // PAIR):
            window = (pl.ds(base, WIN), pl.ds(pair * PAIR, PAIR))
            query = query_ref[window] * jnp.asarray(HD**-0.5, BF16)
            key = key_ref[window]
            value = value_ref[window]
            key_t = key.T
            grad = grad_ref[window]
            inner_t = (grad.astype(F32) * mixed_ref[window].astype(F32)).T
            d_query, d_key, d_value = [], [], []
            for head in range(2):
                mine = (lane >= HD) if head else low
                zero = jnp.zeros_like(key)
                scores = mm(jnp.where(mine, key, zero), query, NT) + bias_ref[at]
                weights = jnp.exp(scores - log_ref[pair, at, pl.ds(head, 1), :])
                inner = jnp.sum(inner_t[head * HD : (head + 1) * HD, :], axis=0, keepdims=True)
                d_weights = mm(jnp.where(mine, value, zero), grad, NT)
                d_scores = (weights * (d_weights - inner)).astype(BF16)
                d_value.append(mm(weights.astype(BF16), grad))
                d_key.append(mm(d_scores, query))
                d_query.append(mm(key_t[head * HD : (head + 1) * HD, :], d_scores) * HD**-0.5)
            column = 3 * PAIR * pair
            keep_from(out_ref, base, start, column, jnp.concatenate(d_query, axis=0).T)
            keep_from(out_ref, base, start, column + PAIR, jnp.where(low, d_key[0], d_key[1]))
            keep_from(out_ref, base, start, column + 2 * PAIR, jnp.where(low, d_value[0], d_value[1]))
        return carry

    lax.fori_loop(0, table_ref[2, 0], one, 0)


def attend_back(starts, crops, joint, mixed, grad, logs, first, count):
    rows = joint.shape[0]
    groups = group_bound(rows)
    at, halves = first // count, joint.shape[1] // (3 * PAIR * count)
    part = lambda at: pl.BlockSpec((rows, count * PAIR), lambda i, *_: (0, at))
    return pl.pallas_call(
        functools.partial(attend_back_kernel, rows),
        grid_spec=pltpu.PrefetchScalarGridSpec(
            num_scalar_prefetch=1,
            grid=(1,),
            in_specs=[whole_spec((rows, 128)), part(at), part(halves + at), part(2 * halves + at), part(at), part(at)]
            + [pl.BlockSpec((count, groups, 8, WIN), lambda i, *_: (at, 0, 0, 0))],
            out_specs=whole_spec((rows, count * 3 * PAIR)),
            scratch_shapes=attend_scratch(rows),
        ),
        out_shape=jax.ShapeDtypeStruct((rows, count * 3 * PAIR), BF16),
        compiler_params=params(),
        cost_estimate=cost(count * 6 * 20 * WIN**3, 2 * rows * count * 8 * PAIR, count * 12 * WIN * WIN),
        name="attend_back",
    )(starts, crops, joint, joint, joint, mixed, grad, logs)


def up_kernel(out_weight, up_weight, me_ref, x_ref, mixed_ref, vec_ref, *refs):
    count = len(out_weight.arrays)
    middle_ref, hidden_ref, active_ref, slope_ref, out_s, out_sem, up_s, up_sem = refs[count:]
    load_first([out_weight, up_weight], me_ref[0], refs[:count], [(out_s, out_sem), (up_s, up_sem)])
    middle = x_ref[...].astype(F32) + mm(mixed_ref[...], out_s[...]) + vec_ref[4:5, :]
    middle_ref[...] = middle
    unit, _ = normed(middle)
    hidden = (unit * vec_ref[5:6, :] + vec_ref[6:7, :]).astype(BF16)
    hidden_ref[...] = hidden
    chunk = vec_ref.shape[1]
    for at in range(up_weight.shape[1] // chunk):
        part = pl.ds(at * chunk, chunk)
        value = mm(hidden, up_s[:, part]) + vec_ref[8 + at : 9 + at, :]
        below = 0.5 + 0.5 * lax.erf(value * (0.5**0.5))
        active_ref[:, part] = (value * below).astype(BF16)
        bell = jnp.exp(value * value * -0.5) * 0.3989422804014327
        slope_ref[:, part] = (below + value * bell).astype(BF16)


def up_forward(me, tokens, mixed, vectors, out_weight, up_weight):
    rows, width = tokens.shape
    inner = up_weight.shape[1]
    arrays = out_weight.arrays
    return pl.pallas_call(
        functools.partial(up_kernel, out_weight, up_weight),
        grid_spec=pltpu.PrefetchScalarGridSpec(
            num_scalar_prefetch=1,
            grid=(rows // TILE,),
            in_specs=[row_spec(width), row_spec(width), whole_spec(vectors.shape)]
            + any_specs(len(arrays)),
            out_specs=[row_spec(width), row_spec(width), row_spec(inner), row_spec(inner)],
            scratch_shapes=out_weight.scratch() + up_weight.scratch(),
        ),
        out_shape=[
            jax.ShapeDtypeStruct((rows, width), F32),
            jax.ShapeDtypeStruct((rows, width), BF16),
            jax.ShapeDtypeStruct((rows, inner), BF16),
            jax.ShapeDtypeStruct((rows, inner), BF16),
        ],
        compiler_params=params(),
        cost_estimate=cost(2 * rows * width * (width + inner), rows * (10 * width + 4 * inner) + 2 * width * inner, rows * inner * 2),
        name="up_forward",
    )(me, tokens, mixed, vectors, *arrays)


def slope_kernel(down_weight, me_ref, grad_ref, slope_ref, *refs):
    count = len(down_weight.arrays)
    ga_ref, sums_ref, upsum_ref, down_s, down_sem = refs[count:]
    load_first([down_weight], me_ref[0], refs[:count], [(down_s, down_sem)])

    @pl.when(pl.program_id(0) == 0)
    def _():
        sums_ref[...] = jnp.zeros_like(sums_ref)
        upsum_ref[...] = jnp.zeros_like(upsum_ref)

    grad = grad_ref[...]
    sums_ref[...] += fold(grad.astype(F32))
    for at in range(0, down_weight.shape[0], CHUNK):
        part = pl.ds(at, CHUNK)
        inner = (mm(grad, down_s[part, :], NT) * slope_ref[:, part].astype(F32)).astype(BF16)
        ga_ref[:, part] = inner
        upsum_ref[:, part] += fold(inner.astype(F32))


def slope_back(me, grad, slope, down_weight):
    rows, width = grad.shape
    inner = slope.shape[1]
    return pl.pallas_call(
        functools.partial(slope_kernel, down_weight),
        grid_spec=pltpu.PrefetchScalarGridSpec(
            num_scalar_prefetch=1,
            grid=(rows // TILE,),
            in_specs=[row_spec(width), row_spec(inner)] + any_specs(len(down_weight.arrays)),
            out_specs=[row_spec(inner), whole_spec((8, width)), whole_spec((8, inner))],
            scratch_shapes=down_weight.scratch(),
        ),
        out_shape=[
            jax.ShapeDtypeStruct((rows, inner), BF16),
            jax.ShapeDtypeStruct((8, width), F32),
            jax.ShapeDtypeStruct((8, inner), F32),
        ],
        compiler_params=params(),
        cost_estimate=cost(2 * rows * width * inner, rows * (2 * width + 4 * inner) + 2 * width * inner),
        name="slope_back",
    )(me, grad, slope, *down_weight.arrays)


def middle_kernel(out_weight, up_weight, me_ref, middle_ref, grad_ref, ga_ref, vec_ref, *refs):
    count = len(up_weight.arrays)
    gmid_ref, glow_ref, gmix_ref, sums_ref, out_s, out_sem, up_s, up_sem = refs[count:]
    load_first([out_weight, up_weight], me_ref[0], refs[:count], [(out_s, out_sem), (up_s, up_sem)])

    @pl.when(pl.program_id(0) == 0)
    def _():
        sums_ref[...] = jnp.zeros_like(sums_ref)

    total = mm(ga_ref[...], up_s[...], NT)
    unit, scale = normed(middle_ref[...])
    sums_ref[0] += fold(total * unit)
    sums_ref[1] += fold(total)
    gmid = grad_ref[...].astype(F32) + norm_back(total, unit, scale, vec_ref[5:6, :])
    gmid_ref[...] = gmid
    low = gmid.astype(BF16)
    glow_ref[...] = low
    sums_ref[2] += fold(low.astype(F32))
    gmix_ref[...] = mm(low, out_s[...], NT).astype(BF16)


def middle_back(me, middle, grad, ga, vectors, out_weight, up_weight):
    rows, width = middle.shape
    inner = ga.shape[1]
    return pl.pallas_call(
        functools.partial(middle_kernel, out_weight, up_weight),
        grid_spec=pltpu.PrefetchScalarGridSpec(
            num_scalar_prefetch=1,
            grid=(rows // TILE,),
            in_specs=[row_spec(width), row_spec(width), row_spec(inner), whole_spec(vectors.shape)]
            + any_specs(len(up_weight.arrays)),
            out_specs=[row_spec(width), row_spec(width), row_spec(width), whole_spec((3, 8, width))],
            scratch_shapes=out_weight.scratch() + up_weight.scratch(),
        ),
        out_shape=[
            jax.ShapeDtypeStruct((rows, width), F32),
            jax.ShapeDtypeStruct((rows, width), BF16),
            jax.ShapeDtypeStruct((rows, width), BF16),
            jax.ShapeDtypeStruct((3, 8, width), F32),
        ],
        compiler_params=params(),
        cost_estimate=cost(2 * rows * width * (width + inner), rows * (14 * width + 2 * inner) + 2 * width * inner),
        name="middle_back",
    )(me, middle, grad, ga, vectors, *up_weight.arrays)


def down_kernel(down_weight, me_ref, middle_ref, active_ref, vec_ref, *refs):
    count = len(down_weight.arrays)
    acts_ref, down_s, down_sem = refs[count:]
    load_first([down_weight], me_ref[0], refs[:count], [(down_s, down_sem)])
    acts_ref[...] = middle_ref[...] + mm(active_ref[...], down_s[...]) + vec_ref[7:8, :]


def down_forward(me, middle, active, vectors, down_weight):
    rows, width = middle.shape
    inner = active.shape[1]
    return pl.pallas_call(
        functools.partial(down_kernel, down_weight),
        grid_spec=pltpu.PrefetchScalarGridSpec(
            num_scalar_prefetch=1,
            grid=(rows // TILE,),
            in_specs=[row_spec(width), row_spec(inner), whole_spec(vectors.shape)] + any_specs(len(down_weight.arrays)),
            out_specs=row_spec(width),
            scratch_shapes=down_weight.scratch(),
        ),
        out_shape=jax.ShapeDtypeStruct((rows, width), F32),
        compiler_params=params(),
        cost_estimate=cost(2 * rows * width * inner, rows * (8 * width + 2 * inner) + 2 * width * inner),
        name="down_forward",
    )(me, middle, active, vectors, *down_weight.arrays)


def first_kernel(
    weight, me_ref, x_ref, gmid_ref, part_a_ref, part_b_ref, vec_ref, cot_ref, mid_ref, up_ref, *refs
):
    count = len(weight.arrays)
    out_ref, rows_ref, sums_ref, joint_sum_ref, scratch, sems = refs[count:]
    load_first([weight], me_ref[0], refs[:count], [(scratch, sems)])

    @pl.when(pl.program_id(0) == 0)
    def _():
        sums_ref[...] = jnp.zeros_like(sums_ref)
        joint_sum_ref[...] = jnp.zeros_like(joint_sum_ref)

    halves = [part_a_ref, part_b_ref]
    pairs = part_a_ref.shape[1] // (3 * PAIR)
    blocks = [
        half[:, (3 * pair + part) * PAIR : (3 * pair + part + 1) * PAIR]
        for part in range(3)
        for half in halves
        for pair in range(pairs)
    ]
    grad = jnp.concatenate(blocks, axis=1)
    joint_sum_ref[...] += fold(grad.astype(F32))
    total = mm(grad, scratch[...], NT)
    unit, scale = normed(x_ref[...].astype(F32))
    sums_ref[0] += fold(total * unit)
    sums_ref[1] += fold(total)
    out_ref[...] = gmid_ref[...] + norm_back(total, unit, scale, vec_ref[0:1, :])

    @pl.when(pl.program_id(0) == pl.num_programs(0) - 1)
    def _():
        width = x_ref.shape[1]
        line = lambda value: jnp.sum(value, axis=0, keepdims=True)
        wide = [line(up_ref[:, at : at + width]) for at in range(0, up_ref.shape[1], width)]
        rows_ref[...] = jnp.concatenate(
            [
                line(sums_ref[0]),
                line(sums_ref[1]),
                line(joint_sum_ref[:, :width]),
                line(joint_sum_ref[:, 2 * width :]),
                line(mid_ref[2]),
                line(mid_ref[0]),
                line(mid_ref[1]),
                line(cot_ref[...]),
            ]
            + wide
            + [jnp.zeros((8 - len(wide), width), F32)],
            axis=0,
        )


def first_back(me, tokens, gmid, part_a, part_b, vectors, cot_sums, mid_sums, up_sums, weight):
    rows, width = tokens.shape
    columns = weight.shape[1]
    return pl.pallas_call(
        functools.partial(first_kernel, weight),
        grid_spec=pltpu.PrefetchScalarGridSpec(
            num_scalar_prefetch=1,
            grid=(rows // TILE,),
            in_specs=[row_spec(width), row_spec(width), row_spec(columns // 2), row_spec(columns // 2)]
            + [whole_spec(array.shape) for array in (vectors, cot_sums, mid_sums, up_sums)]
            + any_specs(len(weight.arrays)),
            out_specs=[row_spec(width), whole_spec((16, width))],
            scratch_shapes=[pltpu.VMEM((2, 8, width), F32), pltpu.VMEM((8, columns), F32)] + weight.scratch(),
        ),
        out_shape=[jax.ShapeDtypeStruct((rows, width), F32), jax.ShapeDtypeStruct((16, width), F32)],
        compiler_params=params(),
        cost_estimate=cost(2 * rows * width * columns, rows * (10 * width + 2 * columns) + 2 * width * columns),
        name="first_back",
    )(me, tokens, gmid, part_a, part_b, vectors, cot_sums, mid_sums, up_sums, *weight.arrays)


def own_rows_kernel(me_ref, left_ref, right_ref, gain_a, shift_a, joint_b, out_b, gain_b, shift_b, down_b, up_b):
    me = me_ref[0]
    own = gain_a.shape[0]
    total = left_ref[0:8, :] + right_ref[0:8, :]
    mine = pltpu.roll(total, lax.rem(8 - me, 8) * own, axis=1)[:, :own]
    for at, ref in enumerate((gain_a, shift_a, None, None, out_b, gain_b, shift_b, down_b)):
        if ref is not None:
            ref[...] = mine[at]
    joint_b[...] = mine[2:4]
    line = 8 + (me >> 1)
    row = left_ref[pl.ds(line, 1), :] + right_ref[pl.ds(line, 1), :]
    half = up_b.shape[0]
    up_b[...] = jnp.where((me & 1) == 1, row[:, half:], row[:, :half])[0]


def own_rows(me, left, right):
    own = left.shape[1] // 8
    vector = jax.ShapeDtypeStruct((own,), F32)
    out_shape = [vector, vector, jax.ShapeDtypeStruct((2, own), F32), vector, vector, vector, vector]
    out_shape.append(jax.ShapeDtypeStruct((4 * own,), F32))
    return pl.pallas_call(
        own_rows_kernel,
        grid_spec=pltpu.PrefetchScalarGridSpec(
            num_scalar_prefetch=1,
            grid=(1,),
            in_specs=[whole_spec(left.shape), whole_spec(right.shape)],
            out_specs=[whole_spec(shape.shape) for shape in out_shape],
        ),
        out_shape=out_shape,
        compiler_params=params(),
        name="own_rows",
    )(me, left, right)


def weight_grad(left, right):
    return lax.dot_general(left, right, (((0,), (0,)), ((), ())), preferred_element_type=F32).astype(BF16)


def on_device(
    fsdp,
    dp,
    tokens,
    crop_ids,
    gain_first,
    shift_first,
    joint_weight,
    joint_bias,
    output_weight,
    output_bias,
    gain_second,
    shift_second,
    up_weight,
    up_bias,
    down_weight,
    down_bias,
    cotangent,
):
    rows, width = tokens.shape
    inner = up_bias.shape[0] * fsdp
    joint_width = joint_weight.shape[1]
    rank = lax.axis_index("fsdp")
    me = rank.astype(jnp.int32).reshape(1)
    own = width // fsdp
    own_up = inner // fsdp

    eight = fsdp == 8
    if eight:
        lines = [gain_first, shift_first, joint_bias[0], joint_bias[1], output_bias, gain_second, shift_second, down_bias]
        first_in = jnp.pad(joint_weight, ((0, 8), (0, 0)))
        for at, line in enumerate(lines):
            first_in += jnp.pad(line[None], ((own + at, 7 - at), (0, joint_width - own)))
        first_in += jnp.pad(up_bias[None], ((own, 7), (128, joint_width - 128 - own_up)))
        vectors = None
    else:
        first_in = joint_weight
        pack = [gain_first, shift_first, joint_bias[0], joint_bias[1], output_bias, gain_second, shift_second, down_bias]
        pack = [lax.all_gather(line.astype(BF16), "fsdp", axis=0, tiled=True) for line in pack + [up_bias]]
        vectors = jnp.concatenate([jnp.stack(pack[:8]), pack[8].reshape(-1, width)], axis=0).astype(F32)
        vectors = jnp.pad(vectors, ((0, 16 - vectors.shape[0]), (0, 0)))
    outer = jnp.concatenate([output_weight, up_weight], axis=1)

    starts = jnp.sum((crop_ids[None, :] < crop_ids[:, None]).astype(jnp.int32), axis=1)
    crops = jnp.broadcast_to(crop_ids.astype(F32)[:, None], (rows, 128))

    pairs = joint_width // (3 * PAIR)
    near = pairs // 2
    group = Gather(first_in, fsdp)
    source = tokens
    if eight:
        group.first()
        group.second()
        group.third()
        source = after(source, starts, crops)
    else:
        group.whole()
    outer_group = Gather(outer, fsdp).whole()
    lower_group = Gather(after(down_weight, outer), fsdp).whole()
    joint_full = Weight(group, 0, joint_width, spare=8 if eight else 0)
    joint, hidden_first, vectors = joint_forward(me, source, vectors, joint_full)
    mixed, logs = attend(starts, crops, joint, near)
    out_full = Weight(outer_group, 0, width)
    up_full = Weight(outer_group, width, inner)
    middle, hidden_second, active, slope = up_forward(me, tokens, mixed, vectors, out_full, up_full)
    grad = cotangent
    down_full = Weight(lower_group, 0, width)

    start = lambda slabs, short=False, scattered=False: Grad(slabs, fsdp, dp, short, scattered)
    behind = lambda value, *grads: after(value, *[g for g in grads if g is not None])

    scattered = lambda value: lax.psum_scatter(value, "fsdp", scatter_dimension=0, tiled=True)
    down_grad = weight_grad(active, grad)
    grad_up, cotangent_sums, up_sums = slope_back(me, behind(cotangent, down_grad), slope, down_full)
    down_grad = scattered(down_grad)
    up_grad = weight_grad(hidden_second, grad_up)
    grad_middle, grad_low, grad_mixed, sums = middle_back(
        me, middle, cotangent, behind(grad_up, up_grad), vectors, out_full, up_full
    )
    up_grad = scattered(up_grad)
    down_grad = start(down_grad, scattered=True)
    grad_a = attend_back(starts, crops, joint, mixed, grad_mixed, logs, 0, near)
    low = behind(grad_low, grad_a)
    out_slabs = weight_grad(mixed, low).reshape(fsdp, own, width)
    slabs_a = weight_grad(hidden_first, grad_a).reshape(fsdp, own, -1)
    mixed_grad = start(jnp.concatenate([out_slabs, slabs_a], axis=2))
    if eight:
        mixed_grad.more = up_grad
    sent = [mixed_grad.step(), down_grad.step(grad_a)]
    grad_b = attend_back(starts, crops, joint, mixed, behind(grad_mixed, *sent), logs, near, pairs - near)
    last_slabs = weight_grad(behind(hidden_first, mixed_grad.step(grad_b)), grad_b)
    last_grad = start(last_slabs.reshape(fsdp, own, -1), True)
    sent = [last_grad.step(), down_grad.step(last_slabs)]
    input_grad, total = first_back(
        me,
        behind(tokens, *sent),
        grad_middle,
        grad_a,
        grad_b,
        vectors,
        cotangent_sums,
        sums,
        up_sums,
        joint_full,
    )
    sent = [mixed_grad.step(total), last_grad.step(total), down_grad.step(total)]
    if eight and dp == 4:
        total = behind(total, *sent)
        other = send(total, CORE)
        acts = down_forward(me, behind(middle, *sent), active, vectors, down_full)
        sent = [mixed_grad.step(acts)]
        total = behind(total + other, *sent)
        sent = [last_grad.step(total), down_grad.step(total)]
        total = behind(total, *sent)
        total = total + send(total, FIRST)
        total = total + send(total, SECOND)
        sent = [mixed_grad.step(total)]
        total = behind(total, *sent)
        sent = [last_grad.step(total)]
        total = behind(total, *sent)
        total = total + send_dp(total, 1)
        sent = [mixed_grad.step(total)]
        total = behind(total, *sent)
        vecs = own_rows(me, total, send_dp(total, 3))
    else:
        acts = down_forward(me, behind(middle, *sent), active, vectors, down_full)
        total = lax.psum(total, ("fsdp", "dp"))
        vecs = [lax.dynamic_slice_in_dim(total[at], rank * own, own) for at in range(8)]
        vecs.append(lax.dynamic_slice_in_dim(total[8:].reshape(-1), rank * own_up, own_up))
        vecs = vecs[:2] + [jnp.stack(vecs[2:4])] + vecs[4:]
    last = last_grad.result()
    mixed_out = mixed_grad.result()
    down_grad = down_grad.result()
    if eight:
        mixed_out, up_grad = mixed_out[:, : -up_grad.shape[1]], mixed_out[:, -up_grad.shape[1] :]
    else:
        up_grad = lax.psum(up_grad, "dp").astype(F32)
    wide_grads = [mixed_out[:, width:], last]
    grad_joint = jnp.concatenate(
        [
            half[:, (3 * pair + part) * PAIR : (3 * pair + part + 1) * PAIR]
            for part in range(3)
            for half in wide_grads
            for pair in range(half.shape[1] // (3 * PAIR))
        ],
        axis=1,
    )
    gain_a, shift_a, joint_b, out_b, gain_b, shift_b, down_b, up_b = vecs
    return (
        acts,
        input_grad,
        gain_a,
        shift_a,
        grad_joint,
        joint_b,
        mixed_out[:, :width],
        out_b,
        gain_b,
        shift_b,
        up_grad,
        up_b,
        down_grad,
        down_b,
    )


def solution(mesh):
    rows, line, flat = P(("fsdp", "dp"), None), P("fsdp"), P("fsdp", None)
    both = P(None, "fsdp")
    return jax.shard_map(
        functools.partial(on_device, mesh.shape["fsdp"], mesh.shape["dp"]),
        mesh=mesh,
        in_specs=(rows, P(("fsdp", "dp")), line, line, flat, both, flat, line, line, line, flat, line, flat, line, rows),
        out_specs=(rows, rows, line, line, flat, both, flat, line, line, line, flat, line, flat, line),
        check_vma=False,
    )
```

```python
import functools

import jax
import jax.numpy as jnp
from jax import lax
from jax.experimental import pallas as pl
from jax.experimental.pallas import tpu as pltpu
from jax.sharding import PartitionSpec as P

HD = 64
PAIR = 2 * HD
EPS = 1e-06
WIN = 256
SNAP = 16
TILE = 256
CHUNK = 512
LIMIT = 58 << 20
F32 = jnp.float32
BF16 = jnp.bfloat16
NT = (((1,), (1,)), ((), ()))
NN = (((1,), (0,)), ((), ()))


def mm(left, right, dims=NN):
    return lax.dot_general(left, right, dims, preferred_element_type=F32)


def fold(values):
    return jnp.sum(values.reshape(values.shape[0] // 8, 8, values.shape[1]), axis=0)


CORE = [(i, i ^ 1) for i in range(8)]
FIRST = [(i, i ^ (4 if i & 1 else 2)) for i in range(8)]
SECOND = [(i, i ^ (2 if i & 1 else 4)) for i in range(8)]


def send(value, pairs):
    return lax.ppermute(value, "fsdp", pairs)


def send_dp(value, bit):
    return lax.ppermute(value, "dp", [(i, i ^ bit) for i in range(4)])


def after(value, *others):
    return lax.optimization_barrier((value,) + others)[0]


def pick(value, at, axis=0):
    return lax.dynamic_index_in_dim(value, at, axis, keepdims=False)


def wide(value):
    return value.astype(F32)


class Scatter:
    def __init__(self, slabs):
        me = lax.axis_index("fsdp")
        self.core = me & 1
        at_x, at_y = (me >> 1) & 1, me >> 2
        rows, columns = slabs.shape[1:]
        self.slabs = slabs.reshape(4, 2, rows, columns)
        even = self.core == 0
        keep, leave = 1 - at_y, 1 - at_x
        self.away = (jnp.where(even, 2 * keep, leave), jnp.where(even, 2 * keep + 1, 2 + leave))
        self.near = jnp.where(even, at_x, at_y)
        self.chip = 2 * at_y + at_x
        self.next_chip = jnp.where(even, 2 * at_y + 1 - at_x, 2 * (1 - at_y) + at_x)
        self.mine = pick(self.slabs, self.core, 1)
        self.got = []

    def give(self):
        if not self.got:
            return pick(self.slabs, 1 - self.core, 1)
        if len(self.got) == 1:
            return jnp.stack([wide(pick(self.mine, at)) + wide(pick(self.got[0], at)) for at in self.away]).astype(BF16)
        total = wide(pick(self.mine, self.next_chip)) + wide(pick(self.got[0], self.next_chip))
        return (total + wide(pick(self.got[1], 1 - self.near))).astype(BF16)

    def take(self, value):
        self.got.append(value)

    def pairs(self):
        return (CORE, SECOND, FIRST)[len(self.got)]

    def result(self):
        total = wide(pick(self.mine, self.chip)) + wide(pick(self.got[0], self.chip))
        return (total + wide(pick(self.got[1], self.near)) + wide(self.got[2])).astype(BF16)


class Sum:
    def __init__(self, value, short=False):
        me = lax.axis_index("dp")
        self.low, self.high = (me ^ (me >> 1)) & 1, me >> 1
        self.value = value
        self.short = short
        self.got = []
        self.split()

    def split(self):
        rows, columns = self.value.shape
        self.halves = self.value.reshape(2, rows // 2, columns)

    def half(self):
        return wide(pick(self.halves, self.low)) + wide(self.got[0])

    def quarters(self):
        half = self.half()
        return half.reshape(2, half.shape[0] // 2, half.shape[1])

    def own(self):
        return (pick(self.quarters(), self.high) + wide(self.got[1])).astype(BF16)

    def join(self, mine, other, bit):
        return jnp.concatenate([jnp.where(bit == 0, mine, other), jnp.where(bit == 0, other, mine)], axis=0)

    def give(self):
        step = len(self.got)
        if self.short:
            return self.value.astype(BF16) if step == 0 else (wide(self.value) + wide(self.got[0])).astype(BF16)
        if step == 0:
            return pick(self.halves, 1 - self.low).astype(BF16)
        if step == 1:
            return pick(self.quarters(), 1 - self.high).astype(BF16)
        if step == 2:
            return self.own()
        return self.join(self.own(), self.got[2], self.high)

    def bit(self):
        return ((1, 3) if self.short else (1, 3, 3, 1))[len(self.got)]

    def take(self, value):
        self.got.append(value)

    def result(self):
        if self.short:
            return wide(self.value) + wide(self.got[0]) + wide(self.got[1])
        half = self.join(self.own(), self.got[2], self.high)
        return wide(self.join(half, self.got[3], self.low))


class Grad:
    def __init__(self, slabs, fsdp, dp, short=False, scattered=False):
        self.dp, self.short = dp, short
        self.sum = self.scatter = self.more = None
        if scattered:
            self.enter(slabs)
        elif fsdp == 8:
            self.scatter = Scatter(slabs)
        else:
            self.enter(lax.psum_scatter(slabs, "fsdp", scatter_dimension=0, tiled=True)[0])

    def enter(self, value):
        if self.dp == 4:
            self.sum = Sum(value, self.short)
        else:
            self.out = lax.psum(value, "dp").astype(F32)

    def step(self, *behind):
        stage = self.scatter if self.scatter is not None else self.sum
        if stage is None or (stage is self.sum and len(stage.got) == (2 if self.short else 4)):
            return None
        if behind and stage.got:
            stage.got[-1] = after(stage.got[-1], *behind)
        elif behind and stage is self.sum:
            stage.value = after(stage.value, *behind)
            stage.split()
        given = stage.give()
        if stage is self.sum:
            stage.take(send_dp(given, stage.bit()))
            return given
        stage.take(send(given, stage.pairs()))
        if len(stage.got) == 3:
            self.scatter = None
            value = stage.result()
            self.enter(value if self.more is None else jnp.concatenate([value, self.more], axis=1))
        return given

    def hold(self, *behind):
        stage = self.scatter if self.scatter is not None else self.sum
        if stage.got:
            stage.got[-1] = after(stage.got[-1], *behind)
        else:
            stage.value = after(stage.value, *behind)
            stage.split()

    def result(self):
        while self.step() is not None:
            pass
        return self.sum.result() if self.sum is not None else self.out


class Gather:
    def __init__(self, shard, fsdp):
        self.fsdp = fsdp
        self.shard = shard

    def whole(self):
        self.fsdp = 1
        self.arrays = [lax.all_gather(self.shard, "fsdp", axis=0, tiled=True)]
        return self

    def first(self):
        self.two = jnp.stack([self.shard, send(self.shard, FIRST)])
        return self.two

    def second(self):
        self.more = send(self.two, SECOND)
        self.swapped = send(self.two, CORE)
        return self.more

    def third(self):
        self.arrays = [self.two, self.more, self.swapped, send(self.more, CORE)]
        return self.arrays[-1]

    def blocks(self):
        def owner(theirs, far, at):
            def of(me):
                base = me ^ 1 if theirs else me
                one, two = 2 + 2 * (base & 1), 4 - 2 * (base & 1)
                return base ^ ((two if far else 0) + (one if at else 0))

            return of

        return [(a, at, owner(a >= 2, a % 2 == 1, at)) for a in range(4) for at in range(2)]


class Weight:
    def __init__(self, gathered, first, columns, deep=1, spare=0):
        self.gathered, self.first, self.columns, self.deep = gathered, first, columns, deep
        self.arrays = gathered.arrays
        self.rows = gathered.shard.shape[0] - spare
        self.shape = (self.rows * deep * 8 if gathered.fsdp == 8 else self.arrays[0].shape[0], columns)
        self.count = deep * 8 if gathered.fsdp == 8 else 1

    def copies(self, me, refs, scratch, sems):
        if self.gathered.fsdp != 8:
            source = refs[0].at[:, pl.ds(self.first, self.columns)]
            return [pltpu.make_async_copy(source, scratch, sems.at[0])]
        made = []
        for array, at, owner in self.gathered.blocks():
            for part in range(self.deep):
                start = pl.multiple_of((owner(me) * self.deep + part) * self.rows, 16)
                source = refs[array].at[at, pl.ds(0, self.rows), pl.ds(self.first + part * self.columns, self.columns)]
                made.append(pltpu.make_async_copy(source, scratch.at[pl.ds(start, self.rows), :], sems.at[len(made)]))
        return made

    def vectors(self, me, refs, held, sems):
        made = []
        for array, at, owner in self.gathered.blocks():
            source = refs[array].at[at, pl.ds(self.rows, 8), pl.ds(0, 512)]
            made.append(pltpu.make_async_copy(source, held.at[owner(me)], sems.at[len(made)]))
        return made

    def scratch(self):
        return [pltpu.VMEM(self.shape, BF16), pltpu.SemaphoreType.DMA((self.count,))]


def any_specs(count):
    return [pl.BlockSpec(memory_space=pl.ANY)] * count


def params():
    return pltpu.CompilerParams(dimension_semantics=("arbitrary",), vmem_limit_bytes=LIMIT)


def cost(flops, reads, exps=0):
    return pl.CostEstimate(flops=int(flops), transcendentals=int(exps), bytes_accessed=int(reads))


def row_spec(columns):
    return pl.BlockSpec((TILE, columns), lambda i, *_: (i, 0))


def whole_spec(shape):
    return pl.BlockSpec(shape, lambda i, *_: (0,) * len(shape))


def normed(values):
    center = values - jnp.mean(values, axis=-1, keepdims=True)
    scale = lax.rsqrt(jnp.mean(center * center, axis=-1, keepdims=True) + EPS)
    return center * scale, scale


def norm_back(grad, unit, scale, gain):
    scaled = grad * gain
    first = jnp.mean(scaled, axis=-1, keepdims=True)
    second = jnp.mean(scaled * unit, axis=-1, keepdims=True)
    return (scaled - first - unit * second) * scale


def load_first(weights, me, refs, scratches):
    @pl.when(pl.program_id(0) == 0)
    def _():
        started = []
        for weight, (scratch, sems) in zip(weights, scratches):
            started += weight.copies(me, refs, scratch, sems)
        for copy in started:
            copy.start()
        for copy in started:
            copy.wait()


def unpack(held_ref):
    total = None
    for at in range(8):
        row = held_ref[at][:, 0:128].astype(F32)
        row = jnp.concatenate([row, jnp.zeros((8, 640), F32)], axis=1)
        row = pltpu.roll(row, 96 * at, axis=1) if at else row
        total = row if total is None else total + row
    flat = [held_ref[at][0:1, 128:512].astype(F32) for at in range(8)]
    rows = [jnp.concatenate([flat[2 * at], flat[2 * at + 1]], axis=1) for at in range(4)]
    return jnp.concatenate([total] + rows + [jnp.zeros((4, 768), F32)], axis=0)


def joint_kernel(weight, packed, me_ref, x_ref, *refs):
    count = len(weight.arrays)
    if packed:
        arrays, (out_ref, hidden_ref, vec_ref, scratch, sems, held_ref, held_sems) = refs[:count], refs[count:]

        @pl.when(pl.program_id(0) == 0)
        def _():
            started = weight.vectors(me_ref[0], arrays, held_ref, held_sems)
            for copy in started:
                copy.start()
            load = weight.copies(me_ref[0], arrays, scratch, sems)
            for copy in load:
                copy.start()
            for copy in started:
                copy.wait()
            vec_ref[...] = unpack(held_ref)
            for copy in load:
                copy.wait()
    else:
        vec_ref, arrays, (out_ref, hidden_ref, scratch, sems) = refs[0], refs[1 : 1 + count], refs[1 + count :]
        load_first([weight], me_ref[0], arrays, [(scratch, sems)])
    unit, _ = normed(x_ref[...].astype(F32))
    hidden = (unit * vec_ref[0:1, :] + vec_ref[1:2, :]).astype(BF16)
    hidden_ref[...] = hidden
    bias = jnp.concatenate([vec_ref[2:3, :], jnp.zeros_like(vec_ref[2:3, :]), vec_ref[3:4, :]], axis=1)
    out_ref[...] = (mm(hidden, scratch[...]) + bias).astype(BF16)


def joint_forward(me, tokens, vectors, weight):
    rows, width = tokens.shape
    columns = weight.shape[1]
    packed = vectors is None
    out_specs = [row_spec(columns), row_spec(width)]
    out_shape = [jax.ShapeDtypeStruct((rows, columns), BF16), jax.ShapeDtypeStruct((rows, width), BF16)]
    scratch = weight.scratch()
    if packed:
        out_specs.append(whole_spec((16, width)))
        out_shape.append(jax.ShapeDtypeStruct((16, width), F32))
        scratch += [pltpu.VMEM((8, 8, 512), BF16), pltpu.SemaphoreType.DMA((8,))]
    outs = pl.pallas_call(
        functools.partial(joint_kernel, weight, packed),
        grid_spec=pltpu.PrefetchScalarGridSpec(
            num_scalar_prefetch=1,
            grid=(rows // TILE,),
            in_specs=[row_spec(width)] + ([] if packed else [whole_spec((16, width))]) + any_specs(len(weight.arrays)),
            out_specs=out_specs,
            scratch_shapes=scratch,
        ),
        out_shape=out_shape,
        compiler_params=params(),
        cost_estimate=cost(2 * rows * width * columns, 2 * (rows * (2 * width + columns) + width * columns)),
        name="joint_forward",
    )(me, tokens, *([] if packed else [vectors]), *weight.arrays)
    return outs if packed else (*outs, vectors)


def plan_groups(starts_ref, crops_ref, table_ref, bias_ref, rows):
    def one(state):
        at, start = state
        base = jnp.minimum((start // SNAP) * SNAP, rows - WIN)
        base = pl.multiple_of(base, SNAP)
        edge = base + WIN
        stop = jnp.where(edge >= rows, rows, starts_ref[jnp.minimum(edge, rows - 1)])
        table_ref[0, at] = base
        table_ref[1, at] = start
        down = crops_ref[pl.ds(base, WIN), :]
        across = down.T
        down = jnp.concatenate([down] * (WIN // 128), axis=1)
        across = jnp.concatenate([across] * (WIN // 128), axis=0)
        bias_ref[at] = jnp.where(down == across, 0.0, -1e30)
        return at + 1, stop

    more = lambda state: jnp.logical_and(state[1] < rows, state[0] < group_bound(rows))
    table_ref[2, 0] = lax.while_loop(more, one, (jnp.int32(0), jnp.int32(0)))[0]


def group_bound(rows):
    return 2 * (rows // (WIN - SNAP + 2)) + 2


def keep_from(ref, base, start, columns, value):
    window = (pl.ds(base, WIN), pl.ds(columns, PAIR))
    row = base + lax.broadcasted_iota(jnp.int32, (WIN, PAIR), 0)
    ref[window] = jnp.where(row >= start, value, ref[window].astype(F32)).astype(ref.dtype)


def attend_kernel(rows, starts_ref, crops_ref, query_ref, key_ref, value_ref, mixed_ref, log_ref, table_ref, bias_ref):
    @pl.when(pl.program_id(0) == 0)
    def _():
        plan_groups(starts_ref, crops_ref, table_ref, bias_ref, rows)

    lane = lax.broadcasted_iota(jnp.int32, (WIN, PAIR), 1)

    def one(at, carry):
        base = pl.multiple_of(table_ref[0, at], SNAP)
        start = table_ref[1, at]
        for pair in range(query_ref.shape[1] // PAIR):
            window = (pl.ds(base, WIN), pl.ds(pair * PAIR, PAIR))
            query = query_ref[window] * jnp.asarray(HD**-0.5, BF16)
            key = key_ref[window]
            value_t = value_ref[window].T
            outs = []
            for head in range(2):
                mine = (lane >= HD) if head else (lane < HD)
                scores = mm(jnp.where(mine, key, jnp.zeros_like(key)), query, NT) + bias_ref[at]
                top = jnp.max(scores, axis=0, keepdims=True)
                expo = jnp.exp(scores - top)
                total = jnp.sum(expo, axis=0, keepdims=True)
                mixed = mm(value_t[head * HD : (head + 1) * HD, :], expo.astype(BF16))
                outs.append(mixed * (1.0 / total))
                log_ref[pair, at, pl.ds(head, 1), :] = top + jnp.log(total)
            keep_from(mixed_ref, base, start, pair * PAIR, jnp.concatenate(outs, axis=0).T)
        return carry

    lax.fori_loop(0, table_ref[2, 0], one, 0)


def attend_scratch(rows):
    return [pltpu.SMEM((3, 16), jnp.int32), pltpu.VMEM((group_bound(rows), WIN, WIN), F32)]


def attend(starts, crops, joint, count):
    rows = joint.shape[0]
    pairs = joint.shape[1] // (3 * PAIR)
    groups = group_bound(rows)
    part = lambda at: pl.BlockSpec((rows, count * PAIR), lambda i, *_: (0, at * (pairs // count) + i))
    return pl.pallas_call(
        functools.partial(attend_kernel, rows),
        grid_spec=pltpu.PrefetchScalarGridSpec(
            num_scalar_prefetch=1,
            grid=(pairs // count,),
            in_specs=[whole_spec((rows, 128)), part(0), part(1), part(2)],
            out_specs=[part(0), pl.BlockSpec((count, groups, 8, WIN), lambda i, *_: (i, 0, 0, 0))],
            scratch_shapes=attend_scratch(rows),
        ),
        out_shape=[
            jax.ShapeDtypeStruct((rows, pairs * PAIR), BF16),
            jax.ShapeDtypeStruct((pairs, groups, 8, WIN), F32),
        ],
        compiler_params=params(),
        cost_estimate=cost(pairs * 6 * 8 * WIN**3, 2 * rows * pairs * 4 * PAIR, pairs * 12 * WIN * WIN),
        name="attend",
    )(starts, crops, joint, joint, joint)


def attend_back_kernel(
    rows,
    starts_ref,
    crops_ref,
    query_ref,
    key_ref,
    value_ref,
    mixed_ref,
    grad_ref,
    log_ref,
    out_ref,
    table_ref,
    bias_ref,
):
    plan_groups(starts_ref, crops_ref, table_ref, bias_ref, rows)
    lane = lax.broadcasted_iota(jnp.int32, (WIN, PAIR), 1)
    low = lane < HD

    def one(at, carry):
        base = pl.multiple_of(table_ref[0, at], SNAP)
        start = table_ref[1, at]
        for pair in range(query_ref.shape[1] // PAIR):
            window = (pl.ds(base, WIN), pl.ds(pair * PAIR, PAIR))
            query = query_ref[window] * jnp.asarray(HD**-0.5, BF16)
            key = key_ref[window]
            value = value_ref[window]
            key_t = key.T
            grad = grad_ref[window]
            inner_t = (grad.astype(F32) * mixed_ref[window].astype(F32)).T
            d_query, d_key, d_value = [], [], []
            for head in range(2):
                mine = (lane >= HD) if head else low
                zero = jnp.zeros_like(key)
                scores = mm(jnp.where(mine, key, zero), query, NT) + bias_ref[at]
                weights = jnp.exp(scores - log_ref[pair, at, pl.ds(head, 1), :])
                inner = jnp.sum(inner_t[head * HD : (head + 1) * HD, :], axis=0, keepdims=True)
                d_weights = mm(jnp.where(mine, value, zero), grad, NT)
                d_scores = (weights * (d_weights - inner)).astype(BF16)
                d_value.append(mm(weights.astype(BF16), grad))
                d_key.append(mm(d_scores, query))
                d_query.append(mm(key_t[head * HD : (head + 1) * HD, :], d_scores) * HD**-0.5)
            column = 3 * PAIR * pair
            keep_from(out_ref, base, start, column, jnp.concatenate(d_query, axis=0).T)
            keep_from(out_ref, base, start, column + PAIR, jnp.where(low, d_key[0], d_key[1]))
            keep_from(out_ref, base, start, column + 2 * PAIR, jnp.where(low, d_value[0], d_value[1]))
        return carry

    lax.fori_loop(0, table_ref[2, 0], one, 0)


def attend_back(starts, crops, joint, mixed, grad, logs, first, count):
    rows = joint.shape[0]
    groups = group_bound(rows)
    at, halves = first // count, joint.shape[1] // (3 * PAIR * count)
    part = lambda at: pl.BlockSpec((rows, count * PAIR), lambda i, *_: (0, at))
    return pl.pallas_call(
        functools.partial(attend_back_kernel, rows),
        grid_spec=pltpu.PrefetchScalarGridSpec(
            num_scalar_prefetch=1,
            grid=(1,),
            in_specs=[whole_spec((rows, 128)), part(at), part(halves + at), part(2 * halves + at), part(at), part(at)]
            + [pl.BlockSpec((count, groups, 8, WIN), lambda i, *_: (at, 0, 0, 0))],
            out_specs=whole_spec((rows, count * 3 * PAIR)),
            scratch_shapes=attend_scratch(rows),
        ),
        out_shape=jax.ShapeDtypeStruct((rows, count * 3 * PAIR), BF16),
        compiler_params=params(),
        cost_estimate=cost(count * 6 * 20 * WIN**3, 2 * rows * count * 8 * PAIR, count * 12 * WIN * WIN),
        name="attend_back",
    )(starts, crops, joint, joint, joint, mixed, grad, logs)


def up_kernel(out_weight, up_weight, me_ref, x_ref, mixed_ref, vec_ref, *refs):
    count = len(out_weight.arrays)
    middle_ref, hidden_ref, active_ref, slope_ref, out_s, out_sem, up_s, up_sem = refs[count:]
    load_first([out_weight, up_weight], me_ref[0], refs[:count], [(out_s, out_sem), (up_s, up_sem)])
    middle = x_ref[...].astype(F32) + mm(mixed_ref[...], out_s[...]) + vec_ref[4:5, :]
    middle_ref[...] = middle
    unit, _ = normed(middle)
    hidden = (unit * vec_ref[5:6, :] + vec_ref[6:7, :]).astype(BF16)
    hidden_ref[...] = hidden
    chunk = vec_ref.shape[1]
    for at in range(up_weight.shape[1] // chunk):
        part = pl.ds(at * chunk, chunk)
        value = mm(hidden, up_s[:, part]) + vec_ref[8 + at : 9 + at, :]
        below = 0.5 + 0.5 * lax.erf(value * (0.5**0.5))
        active_ref[:, part] = (value * below).astype(BF16)
        bell = jnp.exp(value * value * -0.5) * 0.3989422804014327
        slope_ref[:, part] = (below + value * bell).astype(BF16)


def up_forward(me, tokens, mixed, vectors, out_weight, up_weight):
    rows, width = tokens.shape
    inner = up_weight.shape[1]
    arrays = out_weight.arrays
    return pl.pallas_call(
        functools.partial(up_kernel, out_weight, up_weight),
        grid_spec=pltpu.PrefetchScalarGridSpec(
            num_scalar_prefetch=1,
            grid=(rows // TILE,),
            in_specs=[row_spec(width), row_spec(width), whole_spec(vectors.shape)]
            + any_specs(len(arrays)),
            out_specs=[row_spec(width), row_spec(width), row_spec(inner), row_spec(inner)],
            scratch_shapes=out_weight.scratch() + up_weight.scratch(),
        ),
        out_shape=[
            jax.ShapeDtypeStruct((rows, width), F32),
            jax.ShapeDtypeStruct((rows, width), BF16),
            jax.ShapeDtypeStruct((rows, inner), BF16),
            jax.ShapeDtypeStruct((rows, inner), BF16),
        ],
        compiler_params=params(),
        cost_estimate=cost(2 * rows * width * (width + inner), rows * (10 * width + 4 * inner) + 2 * width * inner, rows * inner * 2),
        name="up_forward",
    )(me, tokens, mixed, vectors, *arrays)


def slope_kernel(down_weight, me_ref, grad_ref, slope_ref, *refs):
    count = len(down_weight.arrays)
    ga_ref, sums_ref, upsum_ref, down_s, down_sem = refs[count:]
    load_first([down_weight], me_ref[0], refs[:count], [(down_s, down_sem)])

    @pl.when(pl.program_id(0) == 0)
    def _():
        sums_ref[...] = jnp.zeros_like(sums_ref)
        upsum_ref[...] = jnp.zeros_like(upsum_ref)

    grad = grad_ref[...]
    sums_ref[...] += fold(grad.astype(F32))
    for at in range(0, down_weight.shape[0], CHUNK):
        part = pl.ds(at, CHUNK)
        inner = (mm(grad, down_s[part, :], NT) * slope_ref[:, part].astype(F32)).astype(BF16)
        ga_ref[:, part] = inner
        upsum_ref[:, part] += fold(inner.astype(F32))


def slope_back(me, grad, slope, down_weight):
    rows, width = grad.shape
    inner = slope.shape[1]
    return pl.pallas_call(
        functools.partial(slope_kernel, down_weight),
        grid_spec=pltpu.PrefetchScalarGridSpec(
            num_scalar_prefetch=1,
            grid=(rows // TILE,),
            in_specs=[row_spec(width), row_spec(inner)] + any_specs(len(down_weight.arrays)),
            out_specs=[row_spec(inner), whole_spec((8, width)), whole_spec((8, inner))],
            scratch_shapes=down_weight.scratch(),
        ),
        out_shape=[
            jax.ShapeDtypeStruct((rows, inner), BF16),
            jax.ShapeDtypeStruct((8, width), F32),
            jax.ShapeDtypeStruct((8, inner), F32),
        ],
        compiler_params=params(),
        cost_estimate=cost(2 * rows * width * inner, rows * (2 * width + 4 * inner) + 2 * width * inner),
        name="slope_back",
    )(me, grad, slope, *down_weight.arrays)


def middle_kernel(out_weight, up_weight, me_ref, middle_ref, grad_ref, ga_ref, vec_ref, *refs):
    count = len(up_weight.arrays)
    gmid_ref, glow_ref, gmix_ref, sums_ref, out_s, out_sem, up_s, up_sem = refs[count:]
    load_first([out_weight, up_weight], me_ref[0], refs[:count], [(out_s, out_sem), (up_s, up_sem)])

    @pl.when(pl.program_id(0) == 0)
    def _():
        sums_ref[...] = jnp.zeros_like(sums_ref)

    total = mm(ga_ref[...], up_s[...], NT)
    unit, scale = normed(middle_ref[...])
    sums_ref[0] += fold(total * unit)
    sums_ref[1] += fold(total)
    gmid = grad_ref[...].astype(F32) + norm_back(total, unit, scale, vec_ref[5:6, :])
    gmid_ref[...] = gmid
    low = gmid.astype(BF16)
    glow_ref[...] = low
    sums_ref[2] += fold(low.astype(F32))
    gmix_ref[...] = mm(low, out_s[...], NT).astype(BF16)


def middle_back(me, middle, grad, ga, vectors, out_weight, up_weight):
    rows, width = middle.shape
    inner = ga.shape[1]
    return pl.pallas_call(
        functools.partial(middle_kernel, out_weight, up_weight),
        grid_spec=pltpu.PrefetchScalarGridSpec(
            num_scalar_prefetch=1,
            grid=(rows // TILE,),
            in_specs=[row_spec(width), row_spec(width), row_spec(inner), whole_spec(vectors.shape)]
            + any_specs(len(up_weight.arrays)),
            out_specs=[row_spec(width), row_spec(width), row_spec(width), whole_spec((3, 8, width))],
            scratch_shapes=out_weight.scratch() + up_weight.scratch(),
        ),
        out_shape=[
            jax.ShapeDtypeStruct((rows, width), F32),
            jax.ShapeDtypeStruct((rows, width), BF16),
            jax.ShapeDtypeStruct((rows, width), BF16),
            jax.ShapeDtypeStruct((3, 8, width), F32),
        ],
        compiler_params=params(),
        cost_estimate=cost(2 * rows * width * (width + inner), rows * (14 * width + 2 * inner) + 2 * width * inner),
        name="middle_back",
    )(me, middle, grad, ga, vectors, *up_weight.arrays)


def down_kernel(down_weight, me_ref, middle_ref, active_ref, vec_ref, *refs):
    count = len(down_weight.arrays)
    acts_ref, down_s, down_sem = refs[count:]
    load_first([down_weight], me_ref[0], refs[:count], [(down_s, down_sem)])
    acts_ref[...] = middle_ref[...] + mm(active_ref[...], down_s[...]) + vec_ref[7:8, :]


def down_forward(me, middle, active, vectors, down_weight):
    rows, width = middle.shape
    inner = active.shape[1]
    return pl.pallas_call(
        functools.partial(down_kernel, down_weight),
        grid_spec=pltpu.PrefetchScalarGridSpec(
            num_scalar_prefetch=1,
            grid=(rows // TILE,),
            in_specs=[row_spec(width), row_spec(inner), whole_spec(vectors.shape)] + any_specs(len(down_weight.arrays)),
            out_specs=row_spec(width),
            scratch_shapes=down_weight.scratch(),
        ),
        out_shape=jax.ShapeDtypeStruct((rows, width), F32),
        compiler_params=params(),
        cost_estimate=cost(2 * rows * width * inner, rows * (8 * width + 2 * inner) + 2 * width * inner),
        name="down_forward",
    )(me, middle, active, vectors, *down_weight.arrays)


def first_kernel(
    weight, me_ref, x_ref, gmid_ref, part_a_ref, part_b_ref, vec_ref, cot_ref, mid_ref, up_ref, *refs
):
    count = len(weight.arrays)
    out_ref, rows_ref, sums_ref, joint_sum_ref, scratch, sems = refs[count:]
    load_first([weight], me_ref[0], refs[:count], [(scratch, sems)])

    @pl.when(pl.program_id(0) == 0)
    def _():
        sums_ref[...] = jnp.zeros_like(sums_ref)
        joint_sum_ref[...] = jnp.zeros_like(joint_sum_ref)

    halves = [part_a_ref, part_b_ref]
    pairs = part_a_ref.shape[1] // (3 * PAIR)
    blocks = [
        half[:, (3 * pair + part) * PAIR : (3 * pair + part + 1) * PAIR]
        for part in range(3)
        for half in halves
        for pair in range(pairs)
    ]
    grad = jnp.concatenate(blocks, axis=1)
    joint_sum_ref[...] += fold(grad.astype(F32))
    total = mm(grad, scratch[...], NT)
    unit, scale = normed(x_ref[...].astype(F32))
    sums_ref[0] += fold(total * unit)
    sums_ref[1] += fold(total)
    out_ref[...] = gmid_ref[...] + norm_back(total, unit, scale, vec_ref[0:1, :])

    @pl.when(pl.program_id(0) == pl.num_programs(0) - 1)
    def _():
        width = x_ref.shape[1]
        line = lambda value: jnp.sum(value, axis=0, keepdims=True)
        wide = [line(up_ref[:, at : at + width]) for at in range(0, up_ref.shape[1], width)]
        rows_ref[...] = jnp.concatenate(
            [
                line(sums_ref[0]),
                line(sums_ref[1]),
                line(joint_sum_ref[:, :width]),
                line(joint_sum_ref[:, 2 * width :]),
                line(mid_ref[2]),
                line(mid_ref[0]),
                line(mid_ref[1]),
                line(cot_ref[...]),
            ]
            + wide
            + [jnp.zeros((8 - len(wide), width), F32)],
            axis=0,
        )


def first_back(me, tokens, gmid, part_a, part_b, vectors, cot_sums, mid_sums, up_sums, weight):
    rows, width = tokens.shape
    columns = weight.shape[1]
    return pl.pallas_call(
        functools.partial(first_kernel, weight),
        grid_spec=pltpu.PrefetchScalarGridSpec(
            num_scalar_prefetch=1,
            grid=(rows // TILE,),
            in_specs=[row_spec(width), row_spec(width), row_spec(columns // 2), row_spec(columns // 2)]
            + [whole_spec(array.shape) for array in (vectors, cot_sums, mid_sums, up_sums)]
            + any_specs(len(weight.arrays)),
            out_specs=[row_spec(width), whole_spec((16, width))],
            scratch_shapes=[pltpu.VMEM((2, 8, width), F32), pltpu.VMEM((8, columns), F32)] + weight.scratch(),
        ),
        out_shape=[jax.ShapeDtypeStruct((rows, width), F32), jax.ShapeDtypeStruct((16, width), F32)],
        compiler_params=params(),
        cost_estimate=cost(2 * rows * width * columns, rows * (10 * width + 2 * columns) + 2 * width * columns),
        name="first_back",
    )(me, tokens, gmid, part_a, part_b, vectors, cot_sums, mid_sums, up_sums, *weight.arrays)


def own_rows_kernel(me_ref, left_ref, right_ref, gain_a, shift_a, joint_b, out_b, gain_b, shift_b, down_b, up_b):
    me = me_ref[0]
    own = gain_a.shape[0]
    total = left_ref[0:8, :] + right_ref[0:8, :]
    mine = pltpu.roll(total, lax.rem(8 - me, 8) * own, axis=1)[:, :own]
    for at, ref in enumerate((gain_a, shift_a, None, None, out_b, gain_b, shift_b, down_b)):
        if ref is not None:
            ref[...] = mine[at]
    joint_b[...] = mine[2:4]
    line = 8 + (me >> 1)
    row = left_ref[pl.ds(line, 1), :] + right_ref[pl.ds(line, 1), :]
    half = up_b.shape[0]
    up_b[...] = jnp.where((me & 1) == 1, row[:, half:], row[:, :half])[0]


def own_rows(me, left, right):
    own = left.shape[1] // 8
    vector = jax.ShapeDtypeStruct((own,), F32)
    out_shape = [vector, vector, jax.ShapeDtypeStruct((2, own), F32), vector, vector, vector, vector]
    out_shape.append(jax.ShapeDtypeStruct((4 * own,), F32))
    return pl.pallas_call(
        own_rows_kernel,
        grid_spec=pltpu.PrefetchScalarGridSpec(
            num_scalar_prefetch=1,
            grid=(1,),
            in_specs=[whole_spec(left.shape), whole_spec(right.shape)],
            out_specs=[whole_spec(shape.shape) for shape in out_shape],
        ),
        out_shape=out_shape,
        compiler_params=params(),
        name="own_rows",
    )(me, left, right)


def weight_grad(left, right):
    return lax.dot_general(left, right, (((0,), (0,)), ((), ())), preferred_element_type=F32).astype(BF16)


def on_device(
    fsdp,
    dp,
    tokens,
    crop_ids,
    gain_first,
    shift_first,
    joint_weight,
    joint_bias,
    output_weight,
    output_bias,
    gain_second,
    shift_second,
    up_weight,
    up_bias,
    down_weight,
    down_bias,
    cotangent,
):
    rows, width = tokens.shape
    inner = up_bias.shape[0] * fsdp
    joint_width = joint_weight.shape[1]
    rank = lax.axis_index("fsdp")
    me = rank.astype(jnp.int32).reshape(1)
    own = width // fsdp
    own_up = inner // fsdp

    eight = fsdp == 8
    if eight:
        lines = [gain_first, shift_first, joint_bias[0], joint_bias[1], output_bias, gain_second, shift_second, down_bias]
        first_in = jnp.pad(joint_weight, ((0, 8), (0, 0)))
        for at, line in enumerate(lines):
            first_in += jnp.pad(line[None], ((own + at, 7 - at), (0, joint_width - own)))
        first_in += jnp.pad(up_bias[None], ((own, 7), (128, joint_width - 128 - own_up)))
        vectors = None
    else:
        first_in = joint_weight
        pack = [gain_first, shift_first, joint_bias[0], joint_bias[1], output_bias, gain_second, shift_second, down_bias]
        pack = [lax.all_gather(line.astype(BF16), "fsdp", axis=0, tiled=True) for line in pack + [up_bias]]
        vectors = jnp.concatenate([jnp.stack(pack[:8]), pack[8].reshape(-1, width)], axis=0).astype(F32)
        vectors = jnp.pad(vectors, ((0, 16 - vectors.shape[0]), (0, 0)))
    outer = jnp.concatenate([output_weight, up_weight], axis=1)

    starts = jnp.sum((crop_ids[None, :] < crop_ids[:, None]).astype(jnp.int32), axis=1)
    crops = jnp.broadcast_to(crop_ids.astype(F32)[:, None], (rows, 128))

    pairs = joint_width // (3 * PAIR)
    near = pairs // 2
    group = Gather(first_in, fsdp)
    source = tokens
    if eight:
        group.first()
        group.second()
        group.third()
        source = after(source, starts, crops)
    else:
        group.whole()
    outer_group = Gather(outer, fsdp).whole()
    lower_group = Gather(after(down_weight, outer), fsdp).whole()
    joint_full = Weight(group, 0, joint_width, spare=8 if eight else 0)
    joint, hidden_first, vectors = joint_forward(me, source, vectors, joint_full)
    mixed, logs = attend(starts, crops, joint, near)
    out_full = Weight(outer_group, 0, width)
    up_full = Weight(outer_group, width, inner)
    middle, hidden_second, active, slope = up_forward(me, tokens, mixed, vectors, out_full, up_full)
    grad = cotangent
    down_full = Weight(lower_group, 0, width)

    start = lambda slabs, short=False, scattered=False: Grad(slabs, fsdp, dp, short, scattered)
    behind = lambda value, *grads: after(value, *[g for g in grads if g is not None])

    scattered = lambda value: lax.psum_scatter(value, "fsdp", scatter_dimension=0, tiled=True)
    down_grad = weight_grad(active, grad)
    grad_up, cotangent_sums, up_sums = slope_back(me, behind(cotangent, down_grad), slope, down_full)
    down_grad = scattered(down_grad)
    up_grad = weight_grad(hidden_second, grad_up)
    grad_middle, grad_low, grad_mixed, sums = middle_back(
        me, middle, cotangent, behind(grad_up, up_grad), vectors, out_full, up_full
    )
    up_grad = scattered(up_grad)
    down_grad = start(down_grad, scattered=True)
    grad_a = attend_back(starts, crops, joint, mixed, grad_mixed, logs, 0, near)
    low = behind(grad_low, grad_a)
    out_slabs = weight_grad(mixed, low).reshape(fsdp, own, width)
    slabs_a = weight_grad(hidden_first, grad_a).reshape(fsdp, own, -1)
    mixed_grad = start(jnp.concatenate([out_slabs, slabs_a], axis=2))
    if eight:
        mixed_grad.more = up_grad
    sent = [mixed_grad.step(), down_grad.step(grad_a)]
    grad_b = attend_back(starts, crops, joint, mixed, behind(grad_mixed, *sent), logs, near, pairs - near)
    last_slabs = weight_grad(behind(hidden_first, mixed_grad.step(grad_b)), grad_b)
    last_grad = start(last_slabs.reshape(fsdp, own, -1), True)
    sent = [last_grad.step(), down_grad.step(last_slabs)]
    input_grad, total = first_back(
        me,
        behind(tokens, *sent),
        grad_middle,
        grad_a,
        grad_b,
        vectors,
        cotangent_sums,
        sums,
        up_sums,
        joint_full,
    )
    sent = [mixed_grad.step(total), last_grad.step(total), down_grad.step(total)]
    if eight and dp == 4:
        total = behind(total, *sent)
        other = send(total, CORE)
        acts = down_forward(me, behind(middle, *sent), active, vectors, down_full)
        sent = [mixed_grad.step(acts)]
        total = behind(total + other, *sent)
        sent = [last_grad.step(total), down_grad.step(total)]
        total = behind(total, *sent)
        total = total + send(total, FIRST)
        total = total + send(total, SECOND)
        sent = [mixed_grad.step(total)]
        total = behind(total, *sent)
        sent = [last_grad.step(total)]
        total = behind(total, *sent)
        total = total + send_dp(total, 1)
        sent = [mixed_grad.step(total, last_grad.sum.got[-1], down_grad.sum.got[-1])]
        sent = [mixed_grad.step(*sent)]
        last_grad.hold(*sent)
        last_grad.step()
        total = behind(total, *sent)
        vecs = own_rows(me, total, send_dp(total, 3))
    else:
        acts = down_forward(me, behind(middle, *sent), active, vectors, down_full)
        total = lax.psum(total, ("fsdp", "dp"))
        vecs = [lax.dynamic_slice_in_dim(total[at], rank * own, own) for at in range(8)]
        vecs.append(lax.dynamic_slice_in_dim(total[8:].reshape(-1), rank * own_up, own_up))
        vecs = vecs[:2] + [jnp.stack(vecs[2:4])] + vecs[4:]
    last = last_grad.result()
    mixed_out = mixed_grad.result()
    down_grad = down_grad.result()
    if eight:
        mixed_out, up_grad = mixed_out[:, : -up_grad.shape[1]], mixed_out[:, -up_grad.shape[1] :]
    else:
        up_grad = lax.psum(up_grad, "dp").astype(F32)
    wide_grads = [mixed_out[:, width:], last]
    grad_joint = jnp.concatenate(
        [
            half[:, (3 * pair + part) * PAIR : (3 * pair + part + 1) * PAIR]
            for part in range(3)
            for half in wide_grads
            for pair in range(half.shape[1] // (3 * PAIR))
        ],
        axis=1,
    )
    gain_a, shift_a, joint_b, out_b, gain_b, shift_b, down_b, up_b = vecs
    return (
        acts,
        input_grad,
        gain_a,
        shift_a,
        grad_joint,
        joint_b,
        mixed_out[:, :width],
        out_b,
        gain_b,
        shift_b,
        up_grad,
        up_b,
        down_grad,
        down_b,
    )


def solution(mesh):
    rows, line, flat = P(("fsdp", "dp"), None), P("fsdp"), P("fsdp", None)
    both = P(None, "fsdp")
    return jax.shard_map(
        functools.partial(on_device, mesh.shape["fsdp"], mesh.shape["dp"]),
        mesh=mesh,
        in_specs=(rows, P(("fsdp", "dp")), line, line, flat, both, flat, line, line, line, flat, line, flat, line, rows),
        out_specs=(rows, rows, line, line, flat, both, flat, line, line, line, flat, line, flat, line),
        check_vma=False,
    )
```
